256 devices in a mesh: stack: 4 (over y), plane: 32 (over z, x), phys: 2 (over core).
Axes of the slice: x: 4, y: 4, z: 8, core: 2. Of those that a mesh axis runs over, the one named last changes fastest.
Arguments:
- thermal_offset: float32 [256, 512, 512], P('stack', 'plane', 'phys'), may hold values from -6 to 6
- volume_power_source: float32 [256, 512, 512], P('stack', 'plane', 'phys'), may hold values from -0.024 to 0.024
- substance_code: int32 [256, 512, 512], P('stack', 'plane', 'phys'), may hold values from 0 to 4
- creeping_joint_flag: int32 [256, 512, 512], P('stack', 'plane', 'phys'), may hold values 0 or 1
- imposed_overall_distortion: float32 [256, 512, 512], P('stack', 'plane', 'phys'), may hold values from -1 to 1
- plastic_distortion: float32 [256, 512, 512], P('stack', 'plane', 'phys'), may hold values from -3 to 3
- anand_hardness: float32 [256, 512, 512], P('stack', 'plane', 'phys'), may hold values from 0.8 to 2.4
Outputs:
- new_temperature: float32 [256, 512, 512], P('stack', 'plane', 'phys')
- new_creep_strain: float32 [256, 512, 512], P('stack', 'plane', 'phys')
- new_resistance: float32 [256, 512, 512], P('stack', 'plane', 'phys')
- stress_residual: float32 [256, 512, 512], P('stack', 'plane', 'phys')
The draws below stay inside these ranges and needn't reach their ends.
Inputs may be any that keep to these rules, and one draw needn't show every extreme that they name: `substance_code`: material of each cell: 0 die, 1 underfill, 2 solder ball, 3 substrate, 4 board.
All inputs are finite; a program needn't handle non-finite values. No bound on the sum of `creeping_joint_flag` on one device may be relied on, other than what follows from the above.
Results may differ from the reference program's by a relative error of at most 0.0003.
Values sent between devices are 32-bit elements; how exact they have to be, the bound alone decides.
A program may use at most 128 MiB of HBM per device.

```python
import math
import jax
import jax.numpy as jnp
from jax import lax

TSTEPS = 3
STACK_LEVELS = 256
COUNT_ALONG_X = 512
COUNT_ALONG_Y = 512


def draw_volume_power_source(key, part):
    shape_all = (STACK_LEVELS, COUNT_ALONG_X, COUNT_ALONG_Y)
    return jnp.clip(0.004 * jax.random.normal(key, shape_all, jnp.float32), -0.024, 0.024)


def with_ends(drawn, rng, low, high):
    longest = drawn.shape.index(max(drawn.shape))
    spots = []
    for shift in (0, 1):
        where = [jax.random.randint(jax.random.fold_in(rng, axis), (), 0, length) for axis, length in enumerate(drawn.shape)]
        where[longest] = (where[longest] + shift) % drawn.shape[longest]
        spots.append(tuple(where))
    return drawn.at[spots[0]].set(low).at[spots[1]].set(high)


def block_levels(own_key, dims, shards, least, high):
    loudness, own = 1.0, jax.random.fold_in(own_key, 6)
    for position, blocks in shards:
        draws = jnp.exp(jax.random.uniform(jax.random.fold_in(own, position), (blocks,), jnp.float32, least / len(shards), high / len(shards)))
        loudness = loudness * jnp.repeat(draws, dims[position] // blocks).reshape([-1 if axis == position else 1 for axis in range(len(dims))])
    return loudness


def bell_draw(rng, extent, deviation, bound, shards=(), held_as=jnp.bfloat16):
    gain = block_levels(rng, extent, shards, -0.22, 0.18) if shards else 1.0
    array = jax.random.normal(rng, extent, jnp.float32) * deviation * gain
    return jnp.minimum(jnp.maximum(array, -bound), bound).astype(held_as)


def setup_inputs(seed: int = 0) -> dict:
    streams_of = jax.random.split(jax.random.key(seed), 8)
    thermal_offset = bell_draw(streams_of[0], (STACK_LEVELS, COUNT_ALONG_X, COUNT_ALONG_Y), 1.0, 6.0, ((0, 4), (1, 32), (2, 2)), jnp.float32)
    volume_power_source = draw_volume_power_source(jax.random.fold_in(streams_of[7], 71), 0)
    substance_code = with_ends(jax.random.randint(streams_of[2], (STACK_LEVELS, COUNT_ALONG_X, COUNT_ALONG_Y), 0, 5), jax.random.fold_in(streams_of[2], 1), 0, 4).astype(jnp.int32)
    creeping_joint_flag = with_ends((jax.random.randint(streams_of[3], (STACK_LEVELS, COUNT_ALONG_X, COUNT_ALONG_Y), 0, 2) < 1).astype(jnp.int32), jax.random.fold_in(streams_of[3], 1), 0, 1)
    imposed_overall_distortion = jnp.clip(jax.random.uniform(streams_of[4], (STACK_LEVELS, COUNT_ALONG_X, COUNT_ALONG_Y), jnp.float32, -1.0, 1.0) * block_levels(streams_of[4], (STACK_LEVELS, COUNT_ALONG_X, COUNT_ALONG_Y), ((0, 4), (1, 32), (2, 2)), -0.4, 0.0), -1.0, 1.0)
    plastic_distortion = bell_draw(streams_of[5], (STACK_LEVELS, COUNT_ALONG_X, COUNT_ALONG_Y), 0.3, 3.0, ((0, 4), (1, 32), (2, 2)), jnp.float32)
    anand_hardness = jnp.clip(jnp.exp(math.log(2.4) - 1.0986123 * jax.random.uniform(streams_of[6], (STACK_LEVELS, COUNT_ALONG_X, COUNT_ALONG_Y), jnp.float32) ** block_levels(streams_of[6], (STACK_LEVELS, COUNT_ALONG_X, COUNT_ALONG_Y), ((0, 4), (1, 32), (2, 2)), -0.2, 0.2)), 0.8, 2.4)
    return dict(thermal_offset=thermal_offset, volume_power_source=volume_power_source, substance_code=substance_code, creeping_joint_flag=creeping_joint_flag, imposed_overall_distortion=imposed_overall_distortion, plastic_distortion=plastic_distortion, anand_hardness=anand_hardness)


k_table = (4.0, 0.6, 2.5, 1.2, 0.8)
cap_table = (1.6, 1.8, 1.7, 2.0, 1.9)
mod_table = (1.5, 0.6, 0.9, 1.2, 0.8)
expand_table = (0.1, 0.3, 0.25, 0.15, 0.2)
cap_unit = 0.0003
lat_unit = 1.2e-05
h_conv = 0.05
creep_rate = 0.05
stress_mult = 0.5
act_energy = 2.0
sat_value = 2.0
sat_power = 0.1

def lookup(substance_code, values_table):
    result = jnp.zeros(substance_code.shape, jnp.float32)
    for entry_index, entry_value in enumerate(values_table):
        result = result + jnp.where(substance_code == entry_index, jnp.float32(entry_value), jnp.float32(0.0))
    return result

def conductance(first_k, second_k):
    return 2.0 * first_k * second_k / (first_k + second_k)

def lateral_flow(field_pad, conduct_pad):
    center = field_pad[:, 1:-1, 1:-1]
    center_k = conduct_pad[:, 1:-1, 1:-1]
    width_x = center.shape[1]
    width_y = center.shape[2]
    total_flow = jnp.zeros(center.shape, jnp.float32)
    for shift_x, shift_y in ((2, 1), (0, 1), (1, 2), (1, 0)):
        near_field = field_pad[:, shift_x:shift_x + width_x, shift_y:shift_y + width_y]
        near_k = conduct_pad[:, shift_x:shift_x + width_x, shift_y:shift_y + width_y]
        total_flow = total_flow + lat_unit * conductance(center_k, near_k) * (near_field - center)
    return total_flow

def vertical_terms(conduct_pad, capacity, global_rows, total_rows):
    inner_k = conduct_pad[:, 1:-1, 1:-1]
    center = inner_k[1:-1]
    lower_band = -conductance(inner_k[:-2], center)
    upper_band = -conductance(inner_k[2:], center)
    edge_loss = jnp.where((global_rows == 0) | (global_rows == total_rows - 1), jnp.float32(h_conv), jnp.float32(0.0))
    main_band = capacity - lower_band - upper_band + edge_loss
    return (lower_band, main_band, upper_band)

def thomas(lower_band, main_band, upper_band, right_side):
    zero_rows = jnp.zeros(main_band.shape[1:], jnp.float32)

    def forward(state_carry, row_data):
        c_prev, d_prev = state_carry
        a_row, b_row, c_row, d_row = row_data
        pivot_value = b_row - a_row * c_prev
        c_new = c_row / pivot_value
        d_new = (d_row - a_row * d_prev) / pivot_value
        return ((c_new, d_new), (c_new, d_new))
    _, (c_mod, d_mod) = lax.scan(forward, (zero_rows, zero_rows), (lower_band, main_band, upper_band, right_side))

    def backward(next_value, row_data):
        c_row, d_row = row_data
        x_row = d_row - c_row * next_value
        return (x_row, x_row)
    _, solution = lax.scan(backward, zero_rows, (c_mod, d_mod), reverse=True)
    return solution

def creep_update(current_reading, substance_code, creeping_joint_flag, imposed_overall_distortion, plastic_distortion, anand_hardness):
    modulus = lookup(substance_code, mod_table)
    expansion = lookup(substance_code, expand_table)
    tangential_traction = modulus * (imposed_overall_distortion - plastic_distortion - expansion * current_reading)
    absolute = 1.5 + 0.5 * jnp.tanh(0.25 * current_reading)
    arrhenius = jnp.exp(-act_energy / absolute)
    drive_term = jnp.sinh(stress_mult * jnp.abs(tangential_traction) / anand_hardness)
    rate_term = creep_rate * arrhenius * drive_term
    saturation = sat_value * (0.5 + drive_term) ** sat_power
    gap_term = 1.0 - anand_hardness / saturation
    active = creeping_joint_flag == 1
    creep_new = jnp.where(active, plastic_distortion + jnp.sign(tangential_traction) * rate_term, plastic_distortion)
    resist_new = jnp.where(active, anand_hardness + gap_term * jnp.sqrt(jnp.abs(gap_term)) * rate_term, anand_hardness)
    stress_new = modulus * (imposed_overall_distortion - creep_new - expansion * current_reading)
    return (creep_new, resist_new, stress_new)

def stress_balance(padded):
    center = padded[1:-1, 1:-1, 1:-1]
    total_sum = padded[2:, 1:-1, 1:-1] + padded[:-2, 1:-1, 1:-1]
    total_sum = total_sum + padded[1:-1, 2:, 1:-1] + padded[1:-1, :-2, 1:-1]
    total_sum = total_sum + padded[1:-1, 1:-1, 2:] + padded[1:-1, 1:-1, :-2]
    return total_sum - 6.0 * center

def reference(thermal_offset, volume_power_source, substance_code, creeping_joint_flag, imposed_overall_distortion, plastic_distortion, anand_hardness):
    conduct = lookup(substance_code, k_table)
    capacity = cap_unit * lookup(substance_code, cap_table)
    conduct_pad = jnp.pad(conduct, 1)
    global_rows = lax.broadcasted_iota(jnp.int32, (STACK_LEVELS, 1, 1), 0)
    lower_band, main_band, upper_band = vertical_terms(conduct_pad, capacity, global_rows, STACK_LEVELS)
    lateral_k = conduct_pad[1:-1]
    current_reading = thermal_offset
    tangential_traction = jnp.zeros_like(thermal_offset)
    for time_step in range(TSTEPS):
        field_pad = jnp.pad(current_reading, ((0, 0), (1, 1), (1, 1)))
        right_side = capacity * current_reading + lateral_flow(field_pad, lateral_k) + volume_power_source
        current_reading = thomas(lower_band, main_band, upper_band, right_side)
        plastic_distortion, anand_hardness, tangential_traction = creep_update(current_reading, substance_code, creeping_joint_flag, imposed_overall_distortion, plastic_distortion, anand_hardness)
    residual = stress_balance(jnp.pad(tangential_traction, 1))
    return (current_reading, plastic_distortion, anand_hardness, residual)
```

```python
import functools

import jax
import jax.numpy as jnp
from jax import lax
from jax.experimental import pallas as pl
from jax.experimental.pallas import tpu as pltpu
from jax.sharding import PartitionSpec as P

MESH = pl.DeviceIdType.MESH
TSTEPS = 3
L, X, W = 64, 16, 128
HALF = L // 2

k_table = (4.0, 0.6, 2.5, 1.2, 0.8)
cap_table = (1.6, 1.8, 1.7, 2.0, 1.9)
mod_table = (1.5, 0.6, 0.9, 1.2, 0.8)
expand_table = (0.1, 0.3, 0.25, 0.15, 0.2)
half_resistance = tuple(0.5 / k for k in k_table)
capacities = tuple(0.0003 * c for c in cap_table)
LAT = 1.2e-05
H_CONV = 0.05
LOG2E = 1.4426950408889634
HALF_LN2 = 0.34657359027997264
RATE = 0.05 * 0.22313016014842982

M_START, M_RZ, M_S, M_UV, M_A, M_B, M_C, M_F = 0, 3, 4, 7, 10, 19, 25, 31
N_MSG = 36


def rcp(x):
    return pl.reciprocal(x)


def lookup(c, t):
    low = jnp.where(c < 1, jnp.float32(t[0]), jnp.float32(t[1]))
    top = jnp.where(c < 4, jnp.float32(t[3]), jnp.float32(t[4]))
    return jnp.where(c < 2, low, jnp.where(c < 3, jnp.float32(t[2]), top))


def flat(ref):
    return ref.reshape(2, (L + 2) * X, W)


def shifted(ref, h, l, off):
    return flat(ref)[h, pl.ds(l * X + X + off, X), :]


def loop(n, body, carry, unroll):
    return lax.fori_loop(0, n, body, carry, unroll=unroll)


def kernel(
    t_in, src_in, code_in, flag_in, imp_in, cre_in, har_in,
    t_out, c_out, h_out, s_out,
    code, flag, temp, src, imp, cre, har,
    rk, cap, ip, el, us, vs, gxm, gxp, gym, gyp, c0, rhs, base, md, ex, fl, stress,
    mid, red, planes, abuf, qbuf,
    sx, sy, xs, ys, rz, uvx, uvy, uvxr, uvyr, bx, by, bxr, byr, qx, qy,
    ghost, ghosty, fx, fy, fxr, fyr, zm, zp,
    in_sem, out_sem, ss, rs,
):
    k = lax.axis_index("stack")
    p = lax.axis_index("plane")
    f = lax.axis_index("phys")
    ns, np_ = 4, 32
    up = {"plane": lax.rem(p + 1, np_)}
    down = {"plane": lax.rem(p + np_ - 1, np_)}
    mate = {"phys": 1 - f}
    others = [{"stack": lax.rem(k + o, ns)} for o in (1, 2, 3)]
    first_col, last_col = f == 0, f == 1

    def dev(where):
        return (where.get("stack", k), where.get("plane", p), where.get("phys", f))

    barrier = pltpu.get_barrier_semaphore()
    peers = [up, down, mate] + others
    for w in peers:
        pl.semaphore_signal(barrier, inc=1, device_id=dev(w), device_id_type=MESH)

    loads = {}
    for i, (name, hbm, vm, off) in enumerate((
        ("code", code_in, code, 0), ("temp", t_in, temp, 1), ("src", src_in, src, 0),
        ("flag", flag_in, flag, 0), ("imp", imp_in, imp, 0), ("cre", cre_in, cre, 0),
        ("har", har_in, har, 0),
    )):
        loads[name] = []
        for h in (0, 1):
            cp = pltpu.make_async_copy(
                hbm.at[:, :, pl.ds(W * h, W)], vm.at[h, pl.ds(off, L)], in_sem.at[i, h]
            )
            cp.start()
            loads[name].append(cp)

    def loaded(name):
        for cp in loads[name]:
            cp.wait()

    def message(i, s, d, where):
        return pltpu.make_async_remote_copy(
            src_ref=s, dst_ref=d, send_sem=ss.at[i], recv_sem=rs.at[i],
            device_id=dev(where), device_id_type=MESH,
        )

    sent = []

    def send(i, s, d, where):
        m = message(i, s, d, where)
        m.start()
        sent.append(m)
        return m

    row = lax.broadcasted_iota(jnp.int32, (X, W), 0)
    lane = lax.broadcasted_iota(jnp.int32, (X, W), 1)
    zero = jnp.float32(0.0)

    loaded("code")

    def tables(i, _):
        for h in (0, 1):
            c = code[h, pl.ds(i * 2, 2)]
            rk[h, pl.ds(i * 2 + 1, 2)] = lookup(c, half_resistance)
            cap[h, pl.ds(i * 2, 2)] = lookup(c, capacities)
        return 0

    loop(L // 2, tables, 0, 4)

    def pack_rows(ref, dst, side, off):
        r = 0 if side == 0 else X - 1
        n = ref.shape[1]
        view = ref.reshape(2, n * X, W)
        for h in (0, 1):
            dst[h] = view[h, pl.ds(off * X + r, L, stride=X), :]

    def pack_column(ref, off, dst):
        def body(l, acc):
            v = pltpu.roll(ref[1 - f, l + off], lax.rem(l + 1 - f, W), axis=1)
            return jnp.where(lane == l, v, acc)

        dst[...] = loop(L, body, jnp.zeros((X, W), jnp.float32), 8)

    loaded("temp")
    for side in (0, 1):
        pack_rows(rk, sx.at[side, 0], side, 1)
        pack_rows(temp, sx.at[side, 1], side, 1)
    pack_column(rk, 1, sy.at[0])
    pack_column(temp, 1, sy.at[1])
    pl.semaphore_wait(barrier, len(peers))
    start = [
        send(M_START, sx.at[1], xs.at[0], up),
        send(M_START + 1, sx.at[0], xs.at[1], down),
        send(M_START + 2, sy, ys, mate),
    ]
    to_below = send(M_RZ, rk.at[:, L], rz, others[0])

    one = jnp.ones((2, X, W), jnp.float32)
    top_cap = cap[:, 0] + jnp.where(k == 0, jnp.float32(H_CONV), zero)
    bottom_cap = cap[:, L - 1] + jnp.where(k == ns - 1, jnp.float32(H_CONV), zero)

    def eliminate(i, carry):
        dt, nt, wt, db, nb, wb = carry
        m = L - 1 - i
        g = rcp(rk[:, i + 1] + rk[:, i + 2])
        dn = g * dt + nt
        nn = cap[:, i + 1] * dn + g * nt
        ipv = dt * rcp(dn)
        e = g * ipv
        ip[:, i] = ipv
        el[:, i] = e
        us[:, i] = ipv * wt
        gb = rcp(rk[:, m + 1] + rk[:, m])
        dbn = gb * db + nb
        nbn = cap[:, m - 1] * dbn + gb * nb
        ipb = db * rcp(dbn)
        eb = gb * ipb
        ip[:, m] = ipb
        el[:, m] = eb
        vs[:, m] = ipb * wb
        return dn, nn, e * wt, dbn, nbn, eb * wb

    dt, nt, wt, db, nb, wb = loop(
        HALF - 1, eliminate, (one, top_cap, one, one, bottom_cap, one), 4
    )
    st, sb = nt * rcp(dt), nb * rcp(db)
    gm = rcp(rk[:, HALF] + rk[:, HALF + 1])
    idet = rcp(st * sb + gm * (st + sb))
    m11, m12, m22 = (sb + gm) * idet, gm * idet, (st + gm) * idet
    mid[0], mid[1], mid[2] = m11, m12, m22
    ut, ub, vt, vb = m11 * wt, m12 * wt, m12 * wb, m22 * wb
    us[:, HALF - 1], us[:, HALF], vs[:, HALF - 1], vs[:, HALF] = ut, ub, vt, vb

    def spikes(i, carry):
        ut, ub, vt, vb = carry
        l, m = HALF - 2 - i, HALF + 1 + i
        e, eb = el[:, l], el[:, m]
        ut = us[:, l] + e * ut
        vt = e * vt
        ub = eb * ub
        vb = vs[:, m] + eb * vb
        us[:, l], vs[:, l], us[:, m], vs[:, m] = ut, vt, ub, vb
        return ut, ub, vt, vb

    ut, ub, vt, vb = loop(HALF - 1, spikes, (ut, ub, vt, vb), 4)
    to_below.wait_recv()
    planes[k, 0] = ut + rz[...] + rk[:, 1]
    planes[k, 1] = vb
    planes[k, 2] = ub
    spread = [
        send(M_S + o, planes.at[k], planes.at[k], others[o]) for o in range(3)
    ]

    def halo_rows(xm, xp, h, l):
        return xm[h, pl.ds(l, 1), :], xp[h, pl.ds(l, 1), :]

    def x_shifts(ref, xm, xp, h, l):
        hm, hp = halo_rows(xm, xp, h, l)
        return (
            jnp.where(row == 0, hm, shifted(ref, h, l, -1)),
            jnp.where(row == X - 1, hp, shifted(ref, h, l, 1)),
        )

    def column_of(hy, l):
        v = pltpu.roll(hy[...], lax.rem(W - l, W), axis=1)
        return jnp.broadcast_to(v[:, 0:1], (X, W))

    def y_shifts(v0, v1, e0, e1):
        r0, r1 = pltpu.roll(v0, 1, axis=1), pltpu.roll(v1, 1, axis=1)
        q0, q1 = pltpu.roll(v0, W - 1, axis=1), pltpu.roll(v1, W - 1, axis=1)
        return (
            (jnp.where(lane == 0, e0, r0), jnp.where(lane == W - 1, q1, q0)),
            (jnp.where(lane == 0, r0, r1), jnp.where(lane == W - 1, e1, q1)),
        )

    for m in start:
        m.wait_recv()
    lat = jnp.float32(LAT)
    sxm = jnp.where((row == 0) & (p == 0), zero, lat)
    sxp = jnp.where((row == X - 1) & (p == np_ - 1), zero, lat)
    sym = (jnp.where((lane == 0) & first_col, zero, lat), lat)
    syp = (lat, jnp.where((lane == W - 1) & last_col, zero, lat))

    def lateral(l, _):
        hy = column_of(ys.at[0], l)
        kc = (rk[0, l + 1], rk[1, l + 1])
        ysh = y_shifts(kc[0], kc[1], hy, hy)
        for h in (0, 1):
            km, kp = x_shifts(rk, xs.at[0, 0], xs.at[1, 0], h, l)
            a = sxm * rcp(kc[h] + km)
            b = sxp * rcp(kc[h] + kp)
            c = sym[h] * rcp(kc[h] + ysh[h][0])
            d = syp[h] * rcp(kc[h] + ysh[h][1])
            gxm[h, l], gxp[h, l], gym[h, l], gyp[h, l] = a, b, c, d
            c0[h, l] = cap[h, l] - ((a + b) + (c + d))
        return 0

    loop(L, lateral, 0, 2)

    for side in (0, 1):
        pack_rows(us, uvx.at[side, 0], side, 0)
        pack_rows(vs, uvx.at[side, 1], side, 0)
    pack_column(us, 0, uvy.at[0])
    pack_column(vs, 0, uvy.at[1])
    uv = [
        send(M_UV, uvx.at[1], uvxr.at[0], up),
        send(M_UV + 1, uvx.at[0], uvxr.at[1], down),
        send(M_UV + 2, uvy, uvyr, mate),
    ]

    def right_side(xm, xp, hy_ref):
        def body(l, carry):
            bf, bl = carry
            hy = column_of(hy_ref, l)
            tc = (temp[0, l + 1], temp[1, l + 1])
            ysh = y_shifts(tc[0], tc[1], hy, hy)
            nf, nl = [], []
            for h in (0, 1):
                tm, tp = x_shifts(temp, xm, xp, h, l)
                d = (c0[h, l] * tc[h] + src[h, l]) + (
                    (gxm[h, l] * tm + gxp[h, l] * tp)
                    + (gym[h, l] * ysh[h][0] + gyp[h, l] * ysh[h][1])
                )
                rhs[h, l] = d
                nf.append(bf[h] + us[h, l] * d)
                nl.append(bl[h] + vs[h, l] * d)
            return tuple(nf), tuple(nl)

        z = jnp.zeros((X, W), jnp.float32)
        return loop(L, body, ((z, z), (z, z)), 2)

    def block_solve():
        def forward(i, carry):
            t, b = carry
            m = L - 1 - i
            base[:, i] = ip[:, i] * t
            base[:, m] = ip[:, m] * b
            return rhs[:, i + 1] + el[:, i] * t, rhs[:, m - 1] + el[:, m] * b

        t, b = loop(HALF - 1, forward, (rhs[:, 0], rhs[:, L - 1]), 4)
        t, b = mid[0] * t + mid[1] * b, mid[1] * t + mid[2] * b
        base[:, HALF - 1], base[:, HALF] = t, b

        def backward(i, carry):
            t, b = carry
            l, m = HALF - 2 - i, HALF + 1 + i
            t = base[:, l] + el[:, l] * t
            b = base[:, m] + el[:, m] * b
            base[:, l], base[:, m] = t, b
            return t, b

        loop(HALF - 1, backward, (t, b), 4)

    def correct(qt, qb):
        def body(i, _):
            temp[:, i + 1] = base[:, i] + (us[:, i] * qt + vs[:, i] * qb)
            return 0

        loop(L, body, 0, 4)

    def creep_tables(i, _):
        for h in (0, 1):
            at = pl.ds(i * 2, 2)
            c = code[h, at]
            md[h, at] = lookup(c, mod_table)
            ex[h, at] = lookup(c, expand_table)
            fl[h, at] = jnp.where(flag[h, at] == 1, jnp.float32(RATE), zero)
        return 0

    def creep(last):
        def body(i, _):
            t = temp[:, i + 1]
            c, hd, m = cre[:, i], har[:, i], md[:, i]
            load = imp[:, i] - ex[:, i] * t
            s = m * (load - c)
            z = jnp.abs(s) * (rcp(hd) * jnp.float32(0.5 * LOG2E))
            d = jnp.exp2(z - 1.0) - jnp.exp2(-1.0 - z)
            arr = jnp.exp2(jnp.float32(0.5 * LOG2E) * jnp.tanh(0.25 * t + jnp.float32(HALF_LN2)))
            rate = (fl[:, i] * arr) * d
            q = jnp.exp2(jnp.float32(-0.1 * LOG2E) * jnp.log(0.5 + d))
            gap = 1.0 - (0.5 * hd) * q
            size = jnp.abs(gap)
            root = size * lax.rsqrt(jnp.maximum(size, jnp.float32(1e-30)))
            har[:, i] = hd + (gap * root) * rate
            cn = c + jnp.where(s < 0.0, -rate, rate)
            cre[:, i] = cn
            if last:
                stress[:, i + 1] = m * (load - cn)
            return 0

        loop(L, body, 0, 4)

    xm, xp, hy_ref = xs.at[0, 1], xs.at[1, 1], ys.at[1]
    loaded("src")
    for n in range(TSTEPS):
        bf, bl = right_side(xm, xp, hy_ref)
        for h in (0, 1):
            abuf[n, k, 0, h] = bf[h]
            abuf[n, k, 1, h] = bl[h]
        ends = [
            send(M_A + 3 * n + o, abuf.at[n, k], abuf.at[n, k], others[o]) for o in range(3)
        ]
        block_solve()
        more = n < TSTEPS - 1
        if more:
            for side in (0, 1):
                pack_rows(base, bx.at[n, side], side, 0)
            pack_column(base, 0, by.at[n])
            bases = [
                send(M_B + 3 * n, bx.at[n, 1], bxr.at[n, 0], up),
                send(M_B + 3 * n + 1, bx.at[n, 0], bxr.at[n, 1], down),
                send(M_B + 3 * n + 2, by.at[n], byr.at[n], mate),
            ]
        if n == 0:
            loaded("flag")
            loop(L // 2, creep_tables, 0, 2)
            for m in spread:
                m.wait_recv()
            a1 = planes[0, 1] + planes[1, 0]
            a2 = planes[1, 1] + planes[2, 0]
            a3 = planes[2, 1] + planes[3, 0]
            b1, b2 = planes[1, 2], planes[2, 2]
            d12 = a1 * a2 - b1 * b1
            idet = rcp(d12 * a3 - a1 * (b2 * b2))
            v11, v12, v13 = (a2 * a3 - b2 * b2) * idet, b1 * a3 * idet, b1 * b2 * idet
            v22, v23, v33 = a1 * a3 * idet, a1 * b2 * idet, d12 * idet
            table = ((v11, v12, v13), (v12, v22, v23), (v13, v23, v33))
            for j in range(3):
                for r, shift, sign in ((0, 0, 1.0), (1, 1, -1.0)):
                    at = k + shift
                    v = jnp.where(
                        at == 1, table[0][j],
                        jnp.where(at == 2, table[1][j], jnp.where(at == 3, table[2][j], zero)),
                    )
                    red[r, j] = v * sign
        else:
            if n == 1:
                for name in ("imp", "cre", "har"):
                    loaded(name)
            creep(False)
        for m in ends:
            m.wait_recv()
        r = [abuf[n, j, 1] - abuf[n, j + 1, 0] for j in range(3)]
        qt, qb = [
            red[s, 0] * r[0] + red[s, 1] * r[1] + red[s, 2] * r[2] for s in (0, 1)
        ]
        if more:
            qbuf[n, 0], qbuf[n, 1] = qt, qb
            fluxes = [
                send(M_C + 3 * n, qbuf.at[n, :, :, pl.ds(8, 8)], qx.at[n, 0], up),
                send(M_C + 3 * n + 1, qbuf.at[n, :, :, pl.ds(0, 8)], qx.at[n, 1], down),
                send(M_C + 3 * n + 2, qbuf.at[n, :, 1 - f], qy.at[n], mate),
            ]
        correct(qt, qb)
        if more:
            if n == 0:
                for m in uv:
                    m.wait_recv()
            for m in bases + fluxes:
                m.wait_recv()
            for side, at in ((0, 7), (1, 0)):
                for h in (0, 1):
                    ghost[side, h] = bxr[n, side, h] + (
                        uvxr[side, 0, h] * qx[n, side, 0, h, at : at + 1, :]
                        + uvxr[side, 1, h] * qx[n, side, 1, h, at : at + 1, :]
                    )
            col = [
                jnp.broadcast_to(pltpu.roll(qy[n, s], f, axis=1)[:, 0:1], (X, W)) for s in (0, 1)
            ]
            ghosty[...] = byr[n] + (uvyr[0] * col[0] + uvyr[1] * col[1])
            xm, xp, hy_ref = ghost.at[0], ghost.at[1], ghosty

    stores = []

    def store(i, vm, off, hbm):
        for h in (0, 1):
            cp = pltpu.make_async_copy(
                vm.at[h, pl.ds(off, L)], hbm.at[:, :, pl.ds(W * h, W)], out_sem.at[i, h]
            )
            cp.start()
            stores.append(cp)

    store(0, temp, 1, t_out)
    creep(True)
    store(1, cre, 0, c_out)
    store(2, har, 0, h_out)

    for side in (0, 1):
        pack_rows(stress, fx.at[side], side, 1)
    pack_column(stress, 1, fy)
    edges = [
        send(M_F, fx.at[1], fxr.at[0], up),
        send(M_F + 1, fx.at[0], fxr.at[1], down),
        send(M_F + 2, fy, fyr, mate),
        send(M_F + 3, stress.at[:, L], zm, others[0]),
        send(M_F + 4, stress.at[:, 1], zp, others[2]),
    ]
    for m in edges:
        m.wait_recv()
    stress[:, 0] = jnp.where(k == 0, zero, zm[...])
    stress[:, L + 1] = jnp.where(k == ns - 1, zero, zp[...])
    ghost[0] = jnp.where(p == 0, zero, fxr[0])
    ghost[1] = jnp.where(p == np_ - 1, zero, fxr[1])

    def residual(l, _):
        hy = column_of(fyr, l)
        sc = (stress[0, l + 1], stress[1, l + 1])
        ysh = y_shifts(
            sc[0], sc[1], jnp.where(first_col, zero, hy), jnp.where(last_col, zero, hy)
        )
        for h in (0, 1):
            sm, sp = x_shifts(stress, ghost.at[0], ghost.at[1], h, l)
            rhs[h, l] = (
                ((stress[h, l + 2] + stress[h, l]) + (sm + sp))
                + (ysh[h][0] + ysh[h][1])
            ) - 6.0 * sc[h]
        return 0

    loop(L, residual, 0, 2)
    store(3, rhs, 0, s_out)
    for m in sent:
        m.wait_send()
    for cp in stores:
        cp.wait()


def per_device(*args):
    f32 = jnp.float32
    block = (2, L, X, W)
    tall = (2, L + 2, X, W)

    def vm(*shape):
        return pltpu.VMEM(shape, f32)

    scratch = [
        pltpu.VMEM(block, jnp.int32), pltpu.VMEM(block, jnp.int32), vm(*tall),
        vm(*block), vm(*block), vm(*block), vm(*block),
        vm(*tall),
        *[vm(*block) for _ in range(15)],
        vm(*tall),
        vm(3, 2, X, W), vm(2, 3, 2, X, W),
        vm(4, 3, 2, X, W), vm(TSTEPS, 4, 2, 2, X, W), vm(2, 2, 2, X, W),
        vm(2, 2, 2, L, W), vm(2, X, W), vm(2, 2, 2, L, W), vm(2, X, W),
        vm(2, X, W),
        vm(2, 2, 2, L, W), vm(2, X, W), vm(2, 2, 2, L, W), vm(2, X, W),
        vm(2, 2, 2, L, W), vm(2, X, W), vm(2, 2, 2, L, W), vm(2, X, W),
        vm(2, 2, 2, 2, 8, W), vm(2, 2, X, W),
        vm(2, 2, L, W), vm(X, W),
        vm(2, 2, L, W), vm(X, W), vm(2, 2, L, W), vm(X, W),
        vm(2, X, W), vm(2, X, W),
        pltpu.SemaphoreType.DMA((7, 2)), pltpu.SemaphoreType.DMA((4, 2)),
        pltpu.SemaphoreType.DMA((N_MSG,)), pltpu.SemaphoreType.DMA((N_MSG,)),
    ]
    shape = args[0].shape
    return pl.pallas_call(
        kernel,
        out_shape=[jax.ShapeDtypeStruct(shape, f32)] * 4,
        in_specs=[pl.BlockSpec(memory_space=pl.ANY)] * 7,
        out_specs=[pl.BlockSpec(memory_space=pl.ANY)] * 4,
        scratch_shapes=scratch,
        compiler_params=pltpu.CompilerParams(
            collective_id=0, has_side_effects=True, vmem_limit_bytes=40 << 20
        ),
        name="thermal_creep_step",
    )(*args)


def solution(mesh):
    spec = P("stack", "plane", "phys")
    return jax.shard_map(
        per_device, mesh=mesh, in_specs=(spec,) * 7, out_specs=(spec,) * 4, check_vma=False
    )
```

```python
import functools

import jax
import jax.numpy as jnp
from jax import lax
from jax.experimental import pallas as pl
from jax.experimental.pallas import tpu as pltpu
from jax.sharding import PartitionSpec as P

MESH = pl.DeviceIdType.MESH
TSTEPS = 3
L, X, W = 64, 16, 128
HALF = L // 2

k_table = (4.0, 0.6, 2.5, 1.2, 0.8)
cap_table = (1.6, 1.8, 1.7, 2.0, 1.9)
mod_table = (1.5, 0.6, 0.9, 1.2, 0.8)
expand_table = (0.1, 0.3, 0.25, 0.15, 0.2)
half_resistance = tuple(0.5 / k for k in k_table)
capacities = tuple(0.0003 * c for c in cap_table)
LAT = 1.2e-05
H_CONV = 0.05
LOG2E = 1.4426950408889634
HALF_LN2 = 0.34657359027997264
RATE = 0.05 * 0.22313016014842982

M_START, M_RZ, M_S, M_UV, M_A, M_B, M_C, M_F = 0, 3, 4, 7, 10, 19, 25, 31
N_MSG = 36


def rcp(x):
    return pl.reciprocal(x)


def lookup(c, t):
    low = jnp.where(c < 1, jnp.float32(t[0]), jnp.float32(t[1]))
    top = jnp.where(c < 4, jnp.float32(t[3]), jnp.float32(t[4]))
    return jnp.where(c < 2, low, jnp.where(c < 3, jnp.float32(t[2]), top))


def flat(ref):
    return ref.reshape(2, (L + 2) * X, W)


def shifted(ref, h, l, off):
    return flat(ref)[h, pl.ds(l * X + X + off, X), :]


def loop(n, body, carry, unroll):
    return lax.fori_loop(0, n, body, carry, unroll=unroll)


def kernel(
    t_in, src_in, code_in, flag_in, imp_in, cre_in, har_in,
    t_out, c_out, h_out, s_out,
    code, flag, temp, src, imp, cre, har,
    rk, cap, ip, el, us, vs, gxm, gxp, gym, gyp, c0, rhs, base, md, ex, fl, stress,
    mid, red, planes, abuf, qbuf,
    sx, sy, xs, ys, rz, uvx, uvy, uvxr, uvyr, bx, by, bxr, byr, qx, qy,
    ghost, ghosty, fx, fy, fxr, fyr, zm, zp,
    in_sem, out_sem, ss, rs,
):
    k = lax.axis_index("stack")
    p = lax.axis_index("plane")
    f = lax.axis_index("phys")
    ns, np_ = 4, 32
    up = {"plane": lax.rem(p + 1, np_)}
    down = {"plane": lax.rem(p + np_ - 1, np_)}
    mate = {"phys": 1 - f}
    others = [{"stack": lax.rem(k + o, ns)} for o in (1, 2, 3)]
    first_col, last_col = f == 0, f == 1

    def dev(where):
        return (where.get("stack", k), where.get("plane", p), where.get("phys", f))

    barrier = pltpu.get_barrier_semaphore()
    peers = [up, down, mate] + others
    for w in peers:
        pl.semaphore_signal(barrier, inc=1, device_id=dev(w), device_id_type=MESH)

    loads = {}
    for i, (name, hbm, vm, off) in enumerate((
        ("code", code_in, code, 0), ("temp", t_in, temp, 1), ("src", src_in, src, 0),
        ("flag", flag_in, flag, 0), ("imp", imp_in, imp, 0), ("cre", cre_in, cre, 0),
        ("har", har_in, har, 0),
    )):
        loads[name] = []
        for h in (0, 1):
            cp = pltpu.make_async_copy(
                hbm.at[:, :, pl.ds(W * h, W)], vm.at[h, pl.ds(off, L)], in_sem.at[i, h]
            )
            loads[name].append(cp)

    def load(*names):
        for name in names:
            for cp in loads[name]:
                cp.start()

    load("code", "temp")

    def loaded(name):
        for cp in loads[name]:
            cp.wait()

    def message(i, s, d, where):
        return pltpu.make_async_remote_copy(
            src_ref=s, dst_ref=d, send_sem=ss.at[i], recv_sem=rs.at[i],
            device_id=dev(where), device_id_type=MESH,
        )

    sent = []

    def send(i, s, d, where):
        m = message(i, s, d, where)
        m.start()
        sent.append(m)
        return m

    row = lax.broadcasted_iota(jnp.int32, (X, W), 0)
    lane = lax.broadcasted_iota(jnp.int32, (X, W), 1)
    zero = jnp.float32(0.0)

    loaded("code")
    load("src")

    def tables(i, _):
        for h in (0, 1):
            c = code[h, pl.ds(i * 2, 2)]
            rk[h, pl.ds(i * 2 + 1, 2)] = lookup(c, half_resistance)
            cap[h, pl.ds(i * 2, 2)] = lookup(c, capacities)
        return 0

    loop(L // 2, tables, 0, 4)

    def pack_rows(ref, dst, side, off):
        r = 0 if side == 0 else X - 1
        n = ref.shape[1]
        view = ref.reshape(2, n * X, W)
        for h in (0, 1):
            dst[h] = view[h, pl.ds(off * X + r, L, stride=X), :]

    def pack_column(ref, off, dst):
        def body(l, acc):
            v = pltpu.roll(ref[1 - f, l + off], lax.rem(l + 1 - f, W), axis=1)
            return jnp.where(lane == l, v, acc)

        dst[...] = loop(L, body, jnp.zeros((X, W), jnp.float32), L)

    loaded("temp")
    load("flag", "imp", "cre", "har")
    for side in (0, 1):
        pack_rows(rk, sx.at[side, 0], side, 1)
        pack_rows(temp, sx.at[side, 1], side, 1)
    pack_column(rk, 1, sy.at[0])
    pack_column(temp, 1, sy.at[1])
    pl.semaphore_wait(barrier, len(peers))
    start = [
        send(M_START, sx.at[1], xs.at[0], up),
        send(M_START + 1, sx.at[0], xs.at[1], down),
        send(M_START + 2, sy, ys, mate),
    ]
    to_below = send(M_RZ, rk.at[:, L], rz, others[0])

    one = jnp.ones((2, X, W), jnp.float32)
    top_cap = cap[:, 0] + jnp.where(k == 0, jnp.float32(H_CONV), zero)
    bottom_cap = cap[:, L - 1] + jnp.where(k == ns - 1, jnp.float32(H_CONV), zero)

    def eliminate(i, carry):
        dt, nt, wt, db, nb, wb = carry
        m = L - 1 - i
        g = rcp(rk[:, i + 1] + rk[:, i + 2])
        dn = g * dt + nt
        nn = cap[:, i + 1] * dn + g * nt
        ipv = dt * rcp(dn)
        e = g * ipv
        ip[:, i] = ipv
        el[:, i] = e
        us[:, i] = ipv * wt
        gb = rcp(rk[:, m + 1] + rk[:, m])
        dbn = gb * db + nb
        nbn = cap[:, m - 1] * dbn + gb * nb
        ipb = db * rcp(dbn)
        eb = gb * ipb
        ip[:, m] = ipb
        el[:, m] = eb
        vs[:, m] = ipb * wb
        return dn, nn, e * wt, dbn, nbn, eb * wb

    dt, nt, wt, db, nb, wb = loop(
        HALF - 1, eliminate, (one, top_cap, one, one, bottom_cap, one), 4
    )
    st, sb = nt * rcp(dt), nb * rcp(db)
    gm = rcp(rk[:, HALF] + rk[:, HALF + 1])
    idet = rcp(st * sb + gm * (st + sb))
    m11, m12, m22 = (sb + gm) * idet, gm * idet, (st + gm) * idet
    mid[0], mid[1], mid[2] = m11, m12, m22
    ut, ub, vt, vb = m11 * wt, m12 * wt, m12 * wb, m22 * wb
    us[:, HALF - 1], us[:, HALF], vs[:, HALF - 1], vs[:, HALF] = ut, ub, vt, vb

    def spikes(i, carry):
        ut, ub, vt, vb = carry
        l, m = HALF - 2 - i, HALF + 1 + i
        e, eb = el[:, l], el[:, m]
        ut = us[:, l] + e * ut
        vt = e * vt
        ub = eb * ub
        vb = vs[:, m] + eb * vb
        us[:, l], vs[:, l], us[:, m], vs[:, m] = ut, vt, ub, vb
        return ut, ub, vt, vb

    ut, ub, vt, vb = loop(HALF - 1, spikes, (ut, ub, vt, vb), 4)
    to_below.wait_recv()
    planes[k, 0] = ut + rz[...] + rk[:, 1]
    planes[k, 1] = vb
    planes[k, 2] = ub
    spread = [
        send(M_S + o, planes.at[k], planes.at[k], others[o]) for o in range(3)
    ]

    def halo_rows(xm, xp, h, l):
        return xm[h, pl.ds(l, 1), :], xp[h, pl.ds(l, 1), :]

    def x_shifts(ref, xm, xp, h, l):
        hm, hp = halo_rows(xm, xp, h, l)
        return (
            jnp.where(row == 0, hm, shifted(ref, h, l, -1)),
            jnp.where(row == X - 1, hp, shifted(ref, h, l, 1)),
        )

    def column_of(hy, l):
        v = pltpu.roll(hy[...], lax.rem(W - l, W), axis=1)
        return jnp.broadcast_to(v[:, 0:1], (X, W))

    def y_shifts(v0, v1, e0, e1):
        r0, r1 = pltpu.roll(v0, 1, axis=1), pltpu.roll(v1, 1, axis=1)
        q0, q1 = pltpu.roll(v0, W - 1, axis=1), pltpu.roll(v1, W - 1, axis=1)
        return (
            (jnp.where(lane == 0, e0, r0), jnp.where(lane == W - 1, q1, q0)),
            (jnp.where(lane == 0, r0, r1), jnp.where(lane == W - 1, e1, q1)),
        )

    for m in start:
        m.wait_recv()
    lat = jnp.float32(LAT)
    sxm = jnp.where((row == 0) & (p == 0), zero, lat)
    sxp = jnp.where((row == X - 1) & (p == np_ - 1), zero, lat)
    sym = (jnp.where((lane == 0) & first_col, zero, lat), lat)
    syp = (lat, jnp.where((lane == W - 1) & last_col, zero, lat))

    def lateral(l, _):
        hy = column_of(ys.at[0], l)
        kc = (rk[0, l + 1], rk[1, l + 1])
        ysh = y_shifts(kc[0], kc[1], hy, hy)
        for h in (0, 1):
            km, kp = x_shifts(rk, xs.at[0, 0], xs.at[1, 0], h, l)
            a = sxm * rcp(kc[h] + km)
            b = sxp * rcp(kc[h] + kp)
            c = sym[h] * rcp(kc[h] + ysh[h][0])
            d = syp[h] * rcp(kc[h] + ysh[h][1])
            gxm[h, l], gxp[h, l], gym[h, l], gyp[h, l] = a, b, c, d
            c0[h, l] = cap[h, l] - ((a + b) + (c + d))
        return 0

    loop(L, lateral, 0, 8)

    for side in (0, 1):
        pack_rows(us, uvx.at[side, 0], side, 0)
        pack_rows(vs, uvx.at[side, 1], side, 0)
    pack_column(us, 0, uvy.at[0])
    pack_column(vs, 0, uvy.at[1])
    uv = [
        send(M_UV, uvx.at[1], uvxr.at[0], up),
        send(M_UV + 1, uvx.at[0], uvxr.at[1], down),
        send(M_UV + 2, uvy, uvyr, mate),
    ]

    def right_side(xm, xp, hy_ref):
        def body(l, carry):
            bf, bl = carry
            hy = column_of(hy_ref, l)
            tc = (temp[0, l + 1], temp[1, l + 1])
            ysh = y_shifts(tc[0], tc[1], hy, hy)
            nf, nl = [], []
            for h in (0, 1):
                tm, tp = x_shifts(temp, xm, xp, h, l)
                d = (c0[h, l] * tc[h] + src[h, l]) + (
                    (gxm[h, l] * tm + gxp[h, l] * tp)
                    + (gym[h, l] * ysh[h][0] + gyp[h, l] * ysh[h][1])
                )
                rhs[h, l] = d
                nf.append(bf[h] + us[h, l] * d)
                nl.append(bl[h] + vs[h, l] * d)
            return tuple(nf), tuple(nl)

        z = jnp.zeros((X, W), jnp.float32)
        return loop(L, body, ((z, z), (z, z)), 8)

    def block_solve():
        def forward(i, carry):
            t, b = carry
            m = L - 1 - i
            base[:, i] = ip[:, i] * t
            base[:, m] = ip[:, m] * b
            return rhs[:, i + 1] + el[:, i] * t, rhs[:, m - 1] + el[:, m] * b

        t, b = loop(HALF - 1, forward, (rhs[:, 0], rhs[:, L - 1]), 4)
        t, b = mid[0] * t + mid[1] * b, mid[1] * t + mid[2] * b
        base[:, HALF - 1], base[:, HALF] = t, b

        def backward(i, carry):
            t, b = carry
            l, m = HALF - 2 - i, HALF + 1 + i
            t = base[:, l] + el[:, l] * t
            b = base[:, m] + el[:, m] * b
            base[:, l], base[:, m] = t, b
            return t, b

        loop(HALF - 1, backward, (t, b), 4)

    def correct(qt, qb):
        def body(i, _):
            temp[:, i + 1] = base[:, i] + (us[:, i] * qt + vs[:, i] * qb)
            return 0

        loop(L, body, 0, 4)

    def creep_tables(i, _):
        for h in (0, 1):
            at = pl.ds(i * 2, 2)
            c = code[h, at]
            md[h, at] = lookup(c, mod_table)
            ex[h, at] = lookup(c, expand_table)
            fl[h, at] = jnp.where(flag[h, at] == 1, jnp.float32(RATE), zero)
        return 0

    def creep(last):
        def body(i, _):
            t = temp[:, i + 1]
            c, hd, m = cre[:, i], har[:, i], md[:, i]
            load = imp[:, i] - ex[:, i] * t
            s = m * (load - c)
            z = jnp.abs(s) * (rcp(hd) * jnp.float32(0.5 * LOG2E))
            d = jnp.exp2(z - 1.0) - jnp.exp2(-1.0 - z)
            arr = jnp.exp2(jnp.float32(0.5 * LOG2E) * jnp.tanh(0.25 * t + jnp.float32(HALF_LN2)))
            rate = (fl[:, i] * arr) * d
            q = jnp.exp2(jnp.float32(-0.1 * LOG2E) * jnp.log(0.5 + d))
            gap = 1.0 - (0.5 * hd) * q
            size = jnp.abs(gap)
            root = size * lax.rsqrt(jnp.maximum(size, jnp.float32(1e-30)))
            har[:, i] = hd + (gap * root) * rate
            cn = c + jnp.where(s < 0.0, -rate, rate)
            cre[:, i] = cn
            if last:
                stress[:, i + 1] = m * (load - cn)
            return 0

        loop(L, body, 0, 4)

    xm, xp, hy_ref = xs.at[0, 1], xs.at[1, 1], ys.at[1]
    loaded("src")
    for n in range(TSTEPS):
        bf, bl = right_side(xm, xp, hy_ref)
        for h in (0, 1):
            abuf[n, k, 0, h] = bf[h]
            abuf[n, k, 1, h] = bl[h]
        ends = [
            send(M_A + 3 * n + o, abuf.at[n, k], abuf.at[n, k], others[o]) for o in range(3)
        ]
        block_solve()
        more = n < TSTEPS - 1
        if more:
            for side in (0, 1):
                pack_rows(base, bx.at[n, side], side, 0)
            pack_column(base, 0, by.at[n])
            bases = [
                send(M_B + 3 * n, bx.at[n, 1], bxr.at[n, 0], up),
                send(M_B + 3 * n + 1, bx.at[n, 0], bxr.at[n, 1], down),
                send(M_B + 3 * n + 2, by.at[n], byr.at[n], mate),
            ]
        if n == 0:
            loaded("flag")
            loop(L // 2, creep_tables, 0, 2)
            for m in spread:
                m.wait_recv()
            a1 = planes[0, 1] + planes[1, 0]
            a2 = planes[1, 1] + planes[2, 0]
            a3 = planes[2, 1] + planes[3, 0]
            b1, b2 = planes[1, 2], planes[2, 2]
            d12 = a1 * a2 - b1 * b1
            idet = rcp(d12 * a3 - a1 * (b2 * b2))
            v11, v12, v13 = (a2 * a3 - b2 * b2) * idet, b1 * a3 * idet, b1 * b2 * idet
            v22, v23, v33 = a1 * a3 * idet, a1 * b2 * idet, d12 * idet
            table = ((v11, v12, v13), (v12, v22, v23), (v13, v23, v33))
            for j in range(3):
                for r, shift, sign in ((0, 0, 1.0), (1, 1, -1.0)):
                    at = k + shift
                    v = jnp.where(
                        at == 1, table[0][j],
                        jnp.where(at == 2, table[1][j], jnp.where(at == 3, table[2][j], zero)),
                    )
                    red[r, j] = v * sign
        else:
            if n == 1:
                for name in ("imp", "cre", "har"):
                    loaded(name)
            creep(False)
        for m in ends:
            m.wait_recv()
        r = [abuf[n, j, 1] - abuf[n, j + 1, 0] for j in range(3)]
        qt, qb = [
            red[s, 0] * r[0] + red[s, 1] * r[1] + red[s, 2] * r[2] for s in (0, 1)
        ]
        if more:
            qbuf[n, 0], qbuf[n, 1] = qt, qb
            fluxes = [
                send(M_C + 3 * n, qbuf.at[n, :, :, pl.ds(8, 8)], qx.at[n, 0], up),
                send(M_C + 3 * n + 1, qbuf.at[n, :, :, pl.ds(0, 8)], qx.at[n, 1], down),
                send(M_C + 3 * n + 2, qbuf.at[n, :, 1 - f], qy.at[n], mate),
            ]
        correct(qt, qb)
        if more:
            if n == 0:
                for m in uv:
                    m.wait_recv()
            for m in bases + fluxes:
                m.wait_recv()
            for side, at in ((0, 7), (1, 0)):
                for h in (0, 1):
                    ghost[side, h] = bxr[n, side, h] + (
                        uvxr[side, 0, h] * qx[n, side, 0, h, at : at + 1, :]
                        + uvxr[side, 1, h] * qx[n, side, 1, h, at : at + 1, :]
                    )
            col = [
                jnp.broadcast_to(pltpu.roll(qy[n, s], f, axis=1)[:, 0:1], (X, W)) for s in (0, 1)
            ]
            ghosty[...] = byr[n] + (uvyr[0] * col[0] + uvyr[1] * col[1])
            xm, xp, hy_ref = ghost.at[0], ghost.at[1], ghosty

    stores = []

    def store(i, vm, off, hbm):
        for h in (0, 1):
            cp = pltpu.make_async_copy(
                vm.at[h, pl.ds(off, L)], hbm.at[:, :, pl.ds(W * h, W)], out_sem.at[i, h]
            )
            cp.start()
            stores.append(cp)

    store(0, temp, 1, t_out)
    creep(True)
    store(1, cre, 0, c_out)
    store(2, har, 0, h_out)

    for side in (0, 1):
        pack_rows(stress, fx.at[side], side, 1)
    pack_column(stress, 1, fy)
    edges = [
        send(M_F, fx.at[1], fxr.at[0], up),
        send(M_F + 1, fx.at[0], fxr.at[1], down),
        send(M_F + 2, fy, fyr, mate),
        send(M_F + 3, stress.at[:, L], zm, others[0]),
        send(M_F + 4, stress.at[:, 1], zp, others[2]),
    ]
    for m in edges:
        m.wait_recv()
    stress[:, 0] = jnp.where(k == 0, zero, zm[...])
    stress[:, L + 1] = jnp.where(k == ns - 1, zero, zp[...])
    ghost[0] = jnp.where(p == 0, zero, fxr[0])
    ghost[1] = jnp.where(p == np_ - 1, zero, fxr[1])

    def residual(l, _):
        hy = column_of(fyr, l)
        sc = (stress[0, l + 1], stress[1, l + 1])
        ysh = y_shifts(
            sc[0], sc[1], jnp.where(first_col, zero, hy), jnp.where(last_col, zero, hy)
        )
        for h in (0, 1):
            sm, sp = x_shifts(stress, ghost.at[0], ghost.at[1], h, l)
            rhs[h, l] = (
                ((stress[h, l + 2] + stress[h, l]) + (sm + sp))
                + (ysh[h][0] + ysh[h][1])
            ) - 6.0 * sc[h]
        return 0

    loop(L, residual, 0, 8)
    store(3, rhs, 0, s_out)
    for m in sent:
        m.wait_send()
    for cp in stores:
        cp.wait()


def per_device(*args):
    f32 = jnp.float32
    block = (2, L, X, W)
    tall = (2, L + 2, X, W)

    def vm(*shape):
        return pltpu.VMEM(shape, f32)

    scratch = [
        pltpu.VMEM(block, jnp.int32), pltpu.VMEM(block, jnp.int32), vm(*tall),
        vm(*block), vm(*block), vm(*block), vm(*block),
        vm(*tall),
        *[vm(*block) for _ in range(15)],
        vm(*tall),
        vm(3, 2, X, W), vm(2, 3, 2, X, W),
        vm(4, 3, 2, X, W), vm(TSTEPS, 4, 2, 2, X, W), vm(2, 2, 2, X, W),
        vm(2, 2, 2, L, W), vm(2, X, W), vm(2, 2, 2, L, W), vm(2, X, W),
        vm(2, X, W),
        vm(2, 2, 2, L, W), vm(2, X, W), vm(2, 2, 2, L, W), vm(2, X, W),
        vm(2, 2, 2, L, W), vm(2, X, W), vm(2, 2, 2, L, W), vm(2, X, W),
        vm(2, 2, 2, 2, 8, W), vm(2, 2, X, W),
        vm(2, 2, L, W), vm(X, W),
        vm(2, 2, L, W), vm(X, W), vm(2, 2, L, W), vm(X, W),
        vm(2, X, W), vm(2, X, W),
        pltpu.SemaphoreType.DMA((7, 2)), pltpu.SemaphoreType.DMA((4, 2)),
        pltpu.SemaphoreType.DMA((N_MSG,)), pltpu.SemaphoreType.DMA((N_MSG,)),
    ]
    shape = args[0].shape
    return pl.pallas_call(
        kernel,
        out_shape=[jax.ShapeDtypeStruct(shape, f32)] * 4,
        in_specs=[pl.BlockSpec(memory_space=pl.ANY)] * 7,
        out_specs=[pl.BlockSpec(memory_space=pl.ANY)] * 4,
        scratch_shapes=scratch,
        compiler_params=pltpu.CompilerParams(
            collective_id=0, has_side_effects=True, vmem_limit_bytes=60 << 20
        ),
        name="thermal_creep_step",
    )(*args)


def solution(mesh):
    spec = P("stack", "plane", "phys")
    return jax.shard_map(
        per_device, mesh=mesh, in_specs=(spec,) * 7, out_specs=(spec,) * 4, check_vma=False
    )
```

```python
import functools

import jax
import jax.numpy as jnp
from jax import lax
from jax.experimental import pallas as pl
from jax.experimental.pallas import tpu as pltpu
from jax.sharding import PartitionSpec as P

MESH = pl.DeviceIdType.MESH
TSTEPS = 3
L, X, W = 64, 16, 128
HALF = L // 2

k_table = (4.0, 0.6, 2.5, 1.2, 0.8)
cap_table = (1.6, 1.8, 1.7, 2.0, 1.9)
mod_table = (1.5, 0.6, 0.9, 1.2, 0.8)
expand_table = (0.1, 0.3, 0.25, 0.15, 0.2)
half_resistance = tuple(0.5 / k for k in k_table)
capacities = tuple(0.0003 * c for c in cap_table)
LAT = 1.2e-05
H_CONV = 0.05
LOG2E = 1.4426950408889634
HALF_LN2 = 0.34657359027997264
RATE = 0.05 * 0.22313016014842982

M_START, M_RZ, M_S, M_UV, M_A, M_B, M_C, M_F = 0, 3, 4, 7, 10, 19, 25, 31
N_MSG = 36


def rcp(x):
    return pl.reciprocal(x)


def lookup(c, t):
    low = jnp.where(c < 1, jnp.float32(t[0]), jnp.float32(t[1]))
    top = jnp.where(c < 4, jnp.float32(t[3]), jnp.float32(t[4]))
    return jnp.where(c < 2, low, jnp.where(c < 3, jnp.float32(t[2]), top))


def flat(ref):
    return ref.reshape(2, (L + 2) * X, W)


def shifted(ref, h, l, off):
    return flat(ref)[h, pl.ds(l * X + X + off, X), :]


def loop(n, body, carry, unroll):
    return lax.fori_loop(0, n, body, carry, unroll=unroll)


def kernel(
    t_in, src_in, code_in, flag_in, imp_in, cre_in, har_in,
    t_end, cre, har, rhs,
    code, flag, temp, src, imp,
    rk, cap, ip, el, us, vs, gxm, gxp, gym, gyp, c0, base, md, ex, fl, stress,
    mid, red, planes, abuf, qbuf,
    sx, sy, xs, ys, rz, uvx, uvy, uvxr, uvyr, bx, by, bxr, byr, qx, qy,
    ghost, ghosty, fx, fy, fxr, fyr, zs, zm, zp, gg, dx,
    in_sem, ss, rs,
):
    k = lax.axis_index("stack")
    p = lax.axis_index("plane")
    f = lax.axis_index("phys")
    ns, np_ = 4, 32
    up = {"plane": lax.rem(p + 1, np_)}
    down = {"plane": lax.rem(p + np_ - 1, np_)}
    mate = {"phys": 1 - f}
    others = [{"stack": lax.rem(k + o, ns)} for o in (1, 2, 3)]
    first_col, last_col = f == 0, f == 1

    def dev(where):
        return (where.get("stack", k), where.get("plane", p), where.get("phys", f))

    barrier = pltpu.get_barrier_semaphore()
    peers = [up, down, mate] + others
    for w in peers:
        pl.semaphore_signal(barrier, inc=1, device_id=dev(w), device_id_type=MESH)

    loads = {}
    for i, (name, hbm, vm, off) in enumerate((
        ("code", code_in, code, 0), ("temp", t_in, temp, 1), ("src", src_in, src, 0),
        ("flag", flag_in, flag, 0), ("imp", imp_in, imp, 0), ("cre", cre_in, cre, 0),
        ("har", har_in, har, 0),
    )):
        loads[name] = []
        for h in (0, 1):
            cp = pltpu.make_async_copy(
                hbm.at[:, :, pl.ds(W * h, W)], vm.at[h, pl.ds(off, L)], in_sem.at[i, h]
            )
            loads[name].append(cp)

    def load(*names):
        for name in names:
            for cp in loads[name]:
                cp.start()

    load("code", "temp")

    def loaded(name):
        for cp in loads[name]:
            cp.wait()

    def message(i, s, d, where):
        return pltpu.make_async_remote_copy(
            src_ref=s, dst_ref=d, send_sem=ss.at[i], recv_sem=rs.at[i],
            device_id=dev(where), device_id_type=MESH,
        )

    sent = []

    def send(i, s, d, where):
        m = message(i, s, d, where)
        m.start()
        sent.append(m)
        return m

    row = lax.broadcasted_iota(jnp.int32, (X, W), 0)
    lane = lax.broadcasted_iota(jnp.int32, (X, W), 1)
    zero = jnp.float32(0.0)

    blank = jnp.zeros((2, X, W), jnp.float32)
    for edge in (0, L + 1):
        rk[:, edge], temp[:, edge], stress[:, edge] = blank + 1.0, blank, blank

    loaded("code")
    load("src")

    def tables(i, _):
        for h in (0, 1):
            c = code[h, pl.ds(i * 2, 2)]
            rk[h, pl.ds(i * 2 + 1, 2)] = lookup(c, half_resistance)
            cap[h, pl.ds(i * 2, 2)] = lookup(c, capacities)
        return 0

    loop(L // 2, tables, 0, 4)

    def pack_rows(ref, dst, side, off):
        r = 0 if side == 0 else X - 1
        n = ref.shape[1]
        view = ref.reshape(2, n * X, W)
        for h in (0, 1):
            dst[h] = view[h, pl.ds(off * X + r, L, stride=X), :]

    def pack_column(ref, off, dst):
        def body(l, acc):
            v = pltpu.roll(ref[1 - f, l + off], lax.rem(l + 1 - f, W), axis=1)
            return jnp.where(lane == l, v, acc)

        dst[...] = loop(L, body, jnp.zeros((X, W), jnp.float32), L)

    loaded("temp")
    load("flag", "imp", "cre", "har")
    for side in (0, 1):
        pack_rows(rk, sx.at[side, 0], side, 1)
        pack_rows(temp, sx.at[side, 1], side, 1)
    pack_column(rk, 1, sy.at[0])
    pack_column(temp, 1, sy.at[1])
    pl.semaphore_wait(barrier, len(peers))
    start = [
        send(M_START, sx.at[1], xs.at[0], up),
        send(M_START + 1, sx.at[0], xs.at[1], down),
        send(M_START + 2, sy, ys, mate),
    ]
    to_below = send(M_RZ, rk.at[:, L], rz, others[0])

    one = jnp.ones((2, X, W), jnp.float32)
    top_cap = cap[:, 0] + jnp.where(k == 0, jnp.float32(H_CONV), zero)
    bottom_cap = cap[:, L - 1] + jnp.where(k == ns - 1, jnp.float32(H_CONV), zero)

    def eliminate(i, carry):
        dt, nt, wt, db, nb, wb = carry
        m = L - 1 - i
        g = rcp(rk[:, i + 1] + rk[:, i + 2])
        dn = g * dt + nt
        nn = cap[:, i + 1] * dn + g * nt
        ipv = dt * rcp(dn)
        e = g * ipv
        ip[:, i] = ipv
        el[:, i] = e
        us[:, i] = ipv * wt
        gb = rcp(rk[:, m + 1] + rk[:, m])
        dbn = gb * db + nb
        nbn = cap[:, m - 1] * dbn + gb * nb
        ipb = db * rcp(dbn)
        eb = gb * ipb
        ip[:, m] = ipb
        el[:, m] = eb
        vs[:, m] = ipb * wb
        return dn, nn, e * wt, dbn, nbn, eb * wb

    dt, nt, wt, db, nb, wb = loop(
        HALF - 1, eliminate, (one, top_cap, one, one, bottom_cap, one), 4
    )
    st, sb = nt * rcp(dt), nb * rcp(db)
    gm = rcp(rk[:, HALF] + rk[:, HALF + 1])
    idet = rcp(st * sb + gm * (st + sb))
    m11, m12, m22 = (sb + gm) * idet, gm * idet, (st + gm) * idet
    mid[0], mid[1], mid[2] = m11, m12, m22
    ut, ub, vt, vb = m11 * wt, m12 * wt, m12 * wb, m22 * wb
    us[:, HALF - 1], us[:, HALF], vs[:, HALF - 1], vs[:, HALF] = ut, ub, vt, vb

    def spikes(i, carry):
        ut, ub, vt, vb = carry
        l, m = HALF - 2 - i, HALF + 1 + i
        e, eb = el[:, l], el[:, m]
        ut = us[:, l] + e * ut
        vt = e * vt
        ub = eb * ub
        vb = vs[:, m] + eb * vb
        us[:, l], vs[:, l], us[:, m], vs[:, m] = ut, vt, ub, vb
        return ut, ub, vt, vb

    ut, ub, vt, vb = loop(HALF - 1, spikes, (ut, ub, vt, vb), 4)
    to_below.wait_recv()
    planes[k, 0] = ut + rz[...] + rk[:, 1]
    planes[k, 1] = vb
    planes[k, 2] = ub
    spread = [
        send(M_S + o, planes.at[k], planes.at[k], others[o]) for o in range(3)
    ]

    def x_shifts(ref, h, l):
        return shifted(ref, h, l, -1), shifted(ref, h, l, 1)

    def column_of(hy, l):
        v = pltpu.roll(hy[...], lax.rem(W - l, W), axis=1)
        return jnp.broadcast_to(v[:, 0:1], (X, W))

    def y_shifts(v0, v1, e0, e1):
        r0, r1 = pltpu.roll(v0, 1, axis=1), pltpu.roll(v1, 1, axis=1)
        q0, q1 = pltpu.roll(v0, W - 1, axis=1), pltpu.roll(v1, W - 1, axis=1)
        return (
            (jnp.where(lane == 0, e0, r0), jnp.where(lane == W - 1, q1, q0)),
            (jnp.where(lane == 0, r0, r1), jnp.where(lane == W - 1, e1, q1)),
        )

    start[2].wait_recv()
    lat = jnp.float32(LAT)
    sxm = jnp.where(row == 0, zero, lat)
    sxp = jnp.where(row == X - 1, zero, lat)
    sym = (jnp.where((lane == 0) & first_col, zero, lat), lat)
    syp = (lat, jnp.where((lane == W - 1) & last_col, zero, lat))

    def lateral(l, _):
        hy = column_of(ys.at[0], l)
        kc = (rk[0, l + 1], rk[1, l + 1])
        ysh = y_shifts(kc[0], kc[1], hy, hy)
        for h in (0, 1):
            km, kp = x_shifts(rk, h, l)
            a = sxm * rcp(kc[h] + km)
            b = sxp * rcp(kc[h] + kp)
            c = sym[h] * rcp(kc[h] + ysh[h][0])
            d = syp[h] * rcp(kc[h] + ysh[h][1])
            gxm[h, l], gxp[h, l], gym[h, l], gyp[h, l] = a, b, c, d
            c0[h, l] = cap[h, l] - ((a + b) + (c + d))
        return 0

    loop(L, lateral, 0, 8)

    for side in (0, 1):
        pack_rows(us, uvx.at[side, 0], side, 0)
        pack_rows(vs, uvx.at[side, 1], side, 0)
    pack_column(us, 0, uvy.at[0])
    pack_column(vs, 0, uvy.at[1])
    uv = [
        send(M_UV, uvx.at[1], uvxr.at[0], up),
        send(M_UV + 1, uvx.at[0], uvxr.at[1], down),
        send(M_UV + 2, uvy, uvyr, mate),
    ]

    def right_side(hy_ref):
        def body(l, carry):
            bf, bl = carry
            hy = column_of(hy_ref, l)
            tc = (temp[0, l + 1], temp[1, l + 1])
            ysh = y_shifts(tc[0], tc[1], hy, hy)
            nf, nl = [], []
            for h in (0, 1):
                tm, tp = x_shifts(temp, h, l)
                d = (c0[h, l] * tc[h] + src[h, l]) + (
                    (gxm[h, l] * tm + gxp[h, l] * tp)
                    + (gym[h, l] * ysh[h][0] + gyp[h, l] * ysh[h][1])
                )
                rhs[h, l] = d
                nf.append(bf[h] + us[h, l] * d)
                nl.append(bl[h] + vs[h, l] * d)
            return tuple(nf), tuple(nl)

        z = jnp.zeros((X, W), jnp.float32)
        return loop(L, body, ((z, z), (z, z)), 8)

    def side_row(ref, s, h, off):
        view = ref.reshape(2, ref.shape[1] * X, W)
        return view[h, pl.ds(off * X + (0 if s == 0 else X - 1), L, stride=X), :]

    def ghost_terms(ghost_rows, bf, bl):
        nf, nl = [], []
        for h in (0, 1):
            f_sum, l_sum = [], []
            for s in (0, 1):
                d = gg[s, h] * (ghost_rows[s, h] - side_row(temp, s, h, 1))
                dx[s, h] = d
                f_sum.append(jnp.sum(uvx[s, 0, h] * d, axis=0, keepdims=True))
                l_sum.append(jnp.sum(uvx[s, 1, h] * d, axis=0, keepdims=True))
            for out, old, sums in ((nf, bf, f_sum), (nl, bl, l_sum)):
                add = jnp.where(row == 0, sums[0], jnp.where(row == X - 1, sums[1], zero))
                out.append(old[h] + add)
        return nf, nl

    def add_rows(ref, rows_ref):
        view = ref.reshape(2, L * X, W)
        for h in (0, 1):
            for s, r in ((0, 0), (1, X - 1)):
                at = pl.ds(r, L, stride=X)
                view[h, at, :] = view[h, at, :] + rows_ref[s, h]

    def block_solve():
        def forward(i, carry):
            t, b = carry
            m = L - 1 - i
            base[:, i] = ip[:, i] * t
            base[:, m] = ip[:, m] * b
            return rhs[:, i + 1] + el[:, i] * t, rhs[:, m - 1] + el[:, m] * b

        t, b = loop(HALF - 1, forward, (rhs[:, 0], rhs[:, L - 1]), 4)
        t, b = mid[0] * t + mid[1] * b, mid[1] * t + mid[2] * b
        base[:, HALF - 1], base[:, HALF] = t, b

        def backward(i, carry):
            t, b = carry
            l, m = HALF - 2 - i, HALF + 1 + i
            t = base[:, l] + el[:, l] * t
            b = base[:, m] + el[:, m] * b
            base[:, l], base[:, m] = t, b
            return t, b

        loop(HALF - 1, backward, (t, b), 4)

    def correct(qt, qb, last):
        def body(i, _):
            t = base[:, i] + (us[:, i] * qt + vs[:, i] * qb)
            temp[:, i + 1] = t
            if last:
                t_end[:, i] = t
            return 0

        loop(L, body, 0, 4)

    def creep_tables(i, _):
        for h in (0, 1):
            at = pl.ds(i * 2, 2)
            c = code[h, at]
            md[h, at] = lookup(c, mod_table)
            ex[h, at] = lookup(c, expand_table)
            fl[h, at] = jnp.where(flag[h, at] == 1, jnp.float32(RATE), zero)
        return 0

    def creep_cell(t, c, hd, m, e, im, active):
        load = im - e * t
        s = m * (load - c)
        z = jnp.abs(s) * (rcp(hd) * jnp.float32(0.5 * LOG2E))
        d = jnp.exp2(z - 1.0) - jnp.exp2(-1.0 - z)
        arr = jnp.exp2(jnp.float32(0.5 * LOG2E) * jnp.tanh(0.25 * t + jnp.float32(HALF_LN2)))
        rate = (active * arr) * d
        q = jnp.exp2(jnp.float32(-0.1 * LOG2E) * jnp.log(0.5 + d))
        gap = 1.0 - (0.5 * hd) * q
        size = jnp.abs(gap)
        root = size * lax.rsqrt(jnp.maximum(size, jnp.float32(1e-30)))
        cn = c + jnp.where(s < 0.0, -rate, rate)
        return cn, hd + (gap * root) * rate, m * (load - cn)

    state = (cre, har, md, ex, imp, fl)

    def creep():
        def body(i, _):
            cre[:, i], har[:, i], _s = creep_cell(temp[:, i + 1], *[a[:, i] for a in state])
            return 0

        loop(L, body, 0, 4)

    def last_creep(h):
        def body(i, _):
            cre[h, i], har[h, i], stress[h, i + 1] = creep_cell(
                temp[h, i + 1], *[a[h, i] for a in state]
            )
            return 0

        loop(L, body, 0, 8)

    hy_ref = ys.at[1]
    loaded("src")
    for n in range(TSTEPS):
        bf, bl = right_side(hy_ref)
        if n == 0:
            for m in start[:2]:
                m.wait_recv()
            for s in (0, 1):
                wide = jnp.where(p == (0 if s == 0 else np_ - 1), zero, lat)
                for h in (0, 1):
                    gg[s, h] = wide * rcp(sx[s, 0, h] + xs[s, 0, h])
            bf, bl = ghost_terms(xs.at[:, 1], bf, bl)
        else:
            for m in bases[:2] + fluxes[:2]:
                m.wait_recv()
            for side, at in ((0, 7), (1, 0)):
                for h in (0, 1):
                    ghost[side, h] = bxr[n - 1, side, h] + (
                        uvxr[side, 0, h] * qx[n - 1, side, 0, h, at : at + 1, :]
                        + uvxr[side, 1, h] * qx[n - 1, side, 1, h, at : at + 1, :]
                    )
            bf, bl = ghost_terms(ghost, bf, bl)
        for h in (0, 1):
            abuf[n, k, 0, h] = bf[h]
            abuf[n, k, 1, h] = bl[h]
        ends = [
            send(M_A + 3 * n + o, abuf.at[n, k], abuf.at[n, k], others[o]) for o in range(3)
        ]
        add_rows(rhs, dx)
        block_solve()
        more = n < TSTEPS - 1
        if more:
            for side in (0, 1):
                pack_rows(base, bx.at[n, side], side, 0)
            pack_column(base, 0, by.at[n])
            bases = [
                send(M_B + 3 * n, bx.at[n, 1], bxr.at[n, 0], up),
                send(M_B + 3 * n + 1, bx.at[n, 0], bxr.at[n, 1], down),
                send(M_B + 3 * n + 2, by.at[n], byr.at[n], mate),
            ]
        if n == 0:
            loaded("flag")
            loop(L // 2, creep_tables, 0, 2)
            for m in spread:
                m.wait_recv()
            a1 = planes[0, 1] + planes[1, 0]
            a2 = planes[1, 1] + planes[2, 0]
            a3 = planes[2, 1] + planes[3, 0]
            b1, b2 = planes[1, 2], planes[2, 2]
            d12 = a1 * a2 - b1 * b1
            idet = rcp(d12 * a3 - a1 * (b2 * b2))
            v11, v12, v13 = (a2 * a3 - b2 * b2) * idet, b1 * a3 * idet, b1 * b2 * idet
            v22, v23, v33 = a1 * a3 * idet, a1 * b2 * idet, d12 * idet
            table = ((v11, v12, v13), (v12, v22, v23), (v13, v23, v33))
            for j in range(3):
                for r, shift, sign in ((0, 0, 1.0), (1, 1, -1.0)):
                    at = k + shift
                    v = jnp.where(
                        at == 1, table[0][j],
                        jnp.where(at == 2, table[1][j], jnp.where(at == 3, table[2][j], zero)),
                    )
                    red[r, j] = v * sign
        else:
            if n == 1:
                for name in ("imp", "cre", "har"):
                    loaded(name)
            creep()
        for m in ends:
            m.wait_recv()
        r = [abuf[n, j, 1] - abuf[n, j + 1, 0] for j in range(3)]
        qt, qb = [
            red[s, 0] * r[0] + red[s, 1] * r[1] + red[s, 2] * r[2] for s in (0, 1)
        ]
        if more:
            qbuf[n, 0], qbuf[n, 1] = qt, qb
            fluxes = [
                send(M_C + 3 * n, qbuf.at[n, :, :, pl.ds(8, 8)], qx.at[n, 0], up),
                send(M_C + 3 * n + 1, qbuf.at[n, :, :, pl.ds(0, 8)], qx.at[n, 1], down),
                send(M_C + 3 * n + 2, qbuf.at[n, :, 1 - f], qy.at[n], mate),
            ]
        correct(qt, qb, not more)
        if more:
            if n == 0:
                for m in uv:
                    m.wait_recv()
            bases[2].wait_recv()
            fluxes[2].wait_recv()
            col = [
                jnp.broadcast_to(pltpu.roll(qy[n, s], f, axis=1)[:, 0:1], (X, W)) for s in (0, 1)
            ]
            ghosty[...] = byr[n] + (uvyr[0] * col[0] + uvyr[1] * col[1])
            hy_ref = ghosty

    for s in (0, 1):
        for h in (0, 1):
            fx[s, h] = creep_cell(
                side_row(temp, s, h, 1), *[side_row(a, s, h, 0) for a in state]
            )[2]
    for j, l in ((0, 0), (1, L - 1)):
        zs[j] = creep_cell(temp[:, l + 1], *[a[:, l] for a in state])[2]
    edges = [
        send(M_F, fx.at[1], fxr.at[0], up),
        send(M_F + 1, fx.at[0], fxr.at[1], down),
        send(M_F + 3, zs.at[1], zm, others[0]),
        send(M_F + 4, zs.at[0], zp, others[2]),
    ]
    last_creep(1 - f)
    pack_column(stress, 1, fy)
    beside = send(M_F + 2, fy, fyr, mate)
    last_creep(f)

    beside.wait_recv()

    def residual(l, _):
        hy = column_of(fyr, l)
        sc = (stress[0, l + 1], stress[1, l + 1])
        ysh = y_shifts(
            sc[0], sc[1], jnp.where(first_col, zero, hy), jnp.where(last_col, zero, hy)
        )
        for h in (0, 1):
            sm, sp = x_shifts(stress, h, l)
            sm, sp = jnp.where(row == 0, zero, sm), jnp.where(row == X - 1, zero, sp)
            rhs[h, l] = (
                ((stress[h, l + 2] + stress[h, l]) + (sm + sp))
                + (ysh[h][0] + ysh[h][1])
            ) - 6.0 * sc[h]
        return 0

    loop(L, residual, 0, 8)
    for m in edges:
        m.wait_recv()
    rhs[:, 0] = rhs[:, 0] + jnp.where(k == 0, zero, zm[...])
    rhs[:, L - 1] = rhs[:, L - 1] + jnp.where(k == ns - 1, zero, zp[...])
    ghost[0] = jnp.where(p == 0, zero, fxr[0])
    ghost[1] = jnp.where(p == np_ - 1, zero, fxr[1])
    add_rows(rhs, ghost)
    for m in sent:
        m.wait_send()


def write_out(temp, cre, har, res, t_out, c_out, h_out, s_out, sem):
    copies = []
    for i, (vm, hbm) in enumerate(
        ((temp, t_out), (cre, c_out), (har, h_out), (res, s_out))
    ):
        for h in (0, 1):
            copies.append(pltpu.make_async_copy(
                vm.at[h], hbm.at[:, :, pl.ds(W * h, W)], sem.at[i, h]
            ))
    for cp in copies:
        cp.start()
    for cp in copies:
        cp.wait()


def per_device(*args):
    f32 = jnp.float32
    block = (2, L, X, W)
    tall = (2, L + 2, X, W)

    def vm(*shape):
        return pltpu.VMEM(shape, f32)

    scratch = [
        pltpu.VMEM(block, jnp.int32), pltpu.VMEM(block, jnp.int32), vm(*tall),
        vm(*block), vm(*block),
        vm(*tall),
        *[vm(*block) for _ in range(14)],
        vm(*tall),
        vm(3, 2, X, W), vm(2, 3, 2, X, W),
        vm(4, 3, 2, X, W), vm(TSTEPS, 4, 2, 2, X, W), vm(2, 2, 2, X, W),
        vm(2, 2, 2, L, W), vm(2, X, W), vm(2, 2, 2, L, W), vm(2, X, W),
        vm(2, X, W),
        vm(2, 2, 2, L, W), vm(2, X, W), vm(2, 2, 2, L, W), vm(2, X, W),
        vm(2, 2, 2, L, W), vm(2, X, W), vm(2, 2, 2, L, W), vm(2, X, W),
        vm(2, 2, 2, 2, 8, W), vm(2, 2, X, W),
        vm(2, 2, L, W), vm(X, W),
        vm(2, 2, L, W), vm(X, W), vm(2, 2, L, W), vm(X, W),
        vm(2, 2, X, W), vm(2, X, W), vm(2, X, W),
        vm(2, 2, L, W), vm(2, 2, L, W),
        pltpu.SemaphoreType.DMA((7, 2)),
        pltpu.SemaphoreType.DMA((N_MSG,)), pltpu.SemaphoreType.DMA((N_MSG,)),
    ]
    shape = args[0].shape
    results = pl.pallas_call(
        kernel,
        out_shape=[jax.ShapeDtypeStruct(s, f32) for s in (block,) * 4],
        in_specs=[pl.BlockSpec(memory_space=pltpu.HBM)] * 7,
        out_specs=[pl.BlockSpec(memory_space=pltpu.VMEM)] * 4,
        scratch_shapes=scratch,
        compiler_params=pltpu.CompilerParams(
            collective_id=0, has_side_effects=True, vmem_limit_bytes=49 << 20
        ),
        name="thermal_creep_step",
    )(*args)
    return pl.pallas_call(
        write_out,
        out_shape=[jax.ShapeDtypeStruct(shape, f32)] * 4,
        in_specs=[pl.BlockSpec(memory_space=pltpu.VMEM)] * 4,
        out_specs=[pl.BlockSpec(memory_space=pltpu.HBM)] * 4,
        scratch_shapes=[pltpu.SemaphoreType.DMA((4, 2))],
        compiler_params=pltpu.CompilerParams(vmem_limit_bytes=16 << 20),
        name="write_out",
    )(*results)


def solution(mesh):
    spec = P("stack", "plane", "phys")
    return jax.shard_map(
        per_device, mesh=mesh, in_specs=(spec,) * 7, out_specs=(spec,) * 4, check_vma=False
    )
```

```python
import functools

import jax
import jax.numpy as jnp
from jax import lax
from jax.experimental import pallas as pl
from jax.experimental.pallas import tpu as pltpu
from jax.sharding import PartitionSpec as P

MESH = pl.DeviceIdType.MESH
TSTEPS = 3
L, X, W = 64, 16, 128
HALF = L // 2

k_table = (4.0, 0.6, 2.5, 1.2, 0.8)
cap_table = (1.6, 1.8, 1.7, 2.0, 1.9)
mod_table = (1.5, 0.6, 0.9, 1.2, 0.8)
expand_table = (0.1, 0.3, 0.25, 0.15, 0.2)
half_resistance = tuple(0.5 / k for k in k_table)
capacities = tuple(0.0003 * c for c in cap_table)
LAT = 1.2e-05
H_CONV = 0.05
LOG2E = 1.4426950408889634
HALF_LN2 = 0.34657359027997264
RATE = 0.05 * 0.22313016014842982

M_START, M_RZ, M_S, M_UV, M_A, M_B, M_C, M_F = 0, 3, 4, 7, 10, 19, 25, 31
N_MSG = 36


def rcp(x):
    return pl.reciprocal(x)


def lookup(c, t):
    low = jnp.where(c < 1, jnp.float32(t[0]), jnp.float32(t[1]))
    top = jnp.where(c < 4, jnp.float32(t[3]), jnp.float32(t[4]))
    return jnp.where(c < 2, low, jnp.where(c < 3, jnp.float32(t[2]), top))


def flat(ref):
    return ref.reshape(2, (L + 2) * X, W)


def shifted(ref, h, l, off):
    return flat(ref)[h, pl.ds(l * X + X + off, X), :]


def loop(n, body, carry, unroll):
    return lax.fori_loop(0, n, body, carry, unroll=unroll)


def kernel(
    t_in, src_in, code_in, flag_in, imp_in, cre_in, har_in,
    t_end, cre, har, rhs,
    code, flag, temp, src, imp,
    rk, cap, ip, el, us, vs, gxm, gxp, gym, gyp, c0, base, md, ex, fl, stress,
    mid, red, planes, abuf, qbuf,
    sx, sy, xs, ys, rz, uvx, uvy, uvxr, uvyr, bx, by, bxr, byr, qx, qy,
    ghost, ghosty, fx, fy, fxr, fyr, zs, zm, zp, gg, dx, pc, qend,
    in_sem, ss, rs,
):
    k = lax.axis_index("stack")
    p = lax.axis_index("plane")
    f = lax.axis_index("phys")
    ns, np_ = 4, 32
    up = {"plane": lax.rem(p + 1, np_)}
    down = {"plane": lax.rem(p + np_ - 1, np_)}
    mate = {"phys": 1 - f}
    others = [{"stack": lax.rem(k + o, ns)} for o in (1, 2, 3)]
    first_col, last_col = f == 0, f == 1

    def dev(where):
        return (where.get("stack", k), where.get("plane", p), where.get("phys", f))

    barrier = pltpu.get_barrier_semaphore()
    peers = [up, down, mate] + others
    for w in peers:
        pl.semaphore_signal(barrier, inc=1, device_id=dev(w), device_id_type=MESH)

    loads = {}
    for i, (name, hbm, vm, off) in enumerate((
        ("code", code_in, code, 0), ("temp", t_in, temp, 1), ("src", src_in, src, 0),
        ("flag", flag_in, flag, 0), ("imp", imp_in, imp, 0), ("cre", cre_in, cre, 0),
        ("har", har_in, har, 0),
    )):
        loads[name] = []
        for h in (0, 1):
            cp = pltpu.make_async_copy(
                hbm.at[:, :, pl.ds(W * h, W)], vm.at[h, pl.ds(off, L)], in_sem.at[i, h]
            )
            loads[name].append(cp)

    def load(*names):
        for name in names:
            for cp in loads[name]:
                cp.start()

    load("code", "temp")

    def loaded(name):
        for cp in loads[name]:
            cp.wait()

    def message(i, s, d, where):
        return pltpu.make_async_remote_copy(
            src_ref=s, dst_ref=d, send_sem=ss.at[i], recv_sem=rs.at[i],
            device_id=dev(where), device_id_type=MESH,
        )

    sent = []

    def send(i, s, d, where):
        m = message(i, s, d, where)
        m.start()
        sent.append(m)
        return m

    row = lax.broadcasted_iota(jnp.int32, (X, W), 0)
    lane = lax.broadcasted_iota(jnp.int32, (X, W), 1)
    zero = jnp.float32(0.0)

    blank = jnp.zeros((2, X, W), jnp.float32)
    for edge in (0, L + 1):
        rk[:, edge], temp[:, edge], stress[:, edge] = blank + 1.0, blank, blank

    loaded("code")
    load("src")

    def tables(i, _):
        for h in (0, 1):
            c = code[h, pl.ds(i * 2, 2)]
            rk[h, pl.ds(i * 2 + 1, 2)] = lookup(c, half_resistance)
            cap[h, pl.ds(i * 2, 2)] = lookup(c, capacities)
        return 0

    loop(L // 2, tables, 0, 4)

    def pack_rows(ref, dst, side, off):
        r = 0 if side == 0 else X - 1
        n = ref.shape[1]
        view = ref.reshape(2, n * X, W)
        for h in (0, 1):
            dst[h] = view[h, pl.ds(off * X + r, L, stride=X), :]

    def pack_column(ref, off, dst):
        def body(l, acc):
            v = pltpu.roll(ref[1 - f, l + off], lax.rem(l + 1 - f, W), axis=1)
            return jnp.where(lane == l, v, acc)

        dst[...] = loop(L, body, jnp.zeros((X, W), jnp.float32), L)

    loaded("temp")
    load("flag", "imp", "cre", "har")
    for side in (0, 1):
        pack_rows(rk, sx.at[side, 0], side, 1)
        pack_rows(temp, sx.at[side, 1], side, 1)
    pl.semaphore_wait(barrier, len(peers))
    start = [
        send(M_START, sx.at[1], xs.at[0], up),
        send(M_START + 1, sx.at[0], xs.at[1], down),
    ]
    to_below = send(M_RZ, rk.at[:, L], rz, others[0])
    pack_column(rk, 1, sy.at[0])
    pack_column(temp, 1, sy.at[1])
    start.append(send(M_START + 2, sy, ys, mate))

    one = jnp.ones((2, X, W), jnp.float32)
    top_cap = cap[:, 0] + jnp.where(k == 0, jnp.float32(H_CONV), zero)
    bottom_cap = cap[:, L - 1] + jnp.where(k == ns - 1, jnp.float32(H_CONV), zero)

    def eliminate(i, carry):
        dt, nt, wt, db, nb, wb = carry
        m = L - 1 - i
        g = rcp(rk[:, i + 1] + rk[:, i + 2])
        dn = g * dt + nt
        nn = cap[:, i + 1] * dn + g * nt
        ipv = dt * rcp(dn)
        e = g * ipv
        ip[:, i] = ipv
        el[:, i] = e
        us[:, i] = ipv * wt
        gb = rcp(rk[:, m + 1] + rk[:, m])
        dbn = gb * db + nb
        nbn = cap[:, m - 1] * dbn + gb * nb
        ipb = db * rcp(dbn)
        eb = gb * ipb
        ip[:, m] = ipb
        el[:, m] = eb
        vs[:, m] = ipb * wb
        return dn, nn, e * wt, dbn, nbn, eb * wb

    dt, nt, wt, db, nb, wb = loop(
        HALF - 1, eliminate, (one, top_cap, one, one, bottom_cap, one), 4
    )
    st, sb = nt * rcp(dt), nb * rcp(db)
    gm = rcp(rk[:, HALF] + rk[:, HALF + 1])
    idet = rcp(st * sb + gm * (st + sb))
    m11, m12, m22 = (sb + gm) * idet, gm * idet, (st + gm) * idet
    mid[0], mid[1], mid[2] = m11, m12, m22
    ut, ub, vt, vb = m11 * wt, m12 * wt, m12 * wb, m22 * wb
    us[:, HALF - 1], us[:, HALF], vs[:, HALF - 1], vs[:, HALF] = ut, ub, vt, vb

    def spikes(i, carry):
        ut, ub, vt, vb = carry
        l, m = HALF - 2 - i, HALF + 1 + i
        e, eb = el[:, l], el[:, m]
        ut = us[:, l] + e * ut
        vt = e * vt
        ub = eb * ub
        vb = vs[:, m] + eb * vb
        us[:, l], vs[:, l], us[:, m], vs[:, m] = ut, vt, ub, vb
        return ut, ub, vt, vb

    ut, ub, vt, vb = loop(HALF - 1, spikes, (ut, ub, vt, vb), 4)
    to_below.wait_recv()
    planes[k, 0] = ut + rz[...] + rk[:, 1]
    planes[k, 1] = vb
    planes[k, 2] = ub
    spread = [
        send(M_S + o, planes.at[k], planes.at[k], others[o]) for o in range(3)
    ]

    def x_shifts(ref, h, l):
        return shifted(ref, h, l, -1), shifted(ref, h, l, 1)

    def column_of(hy, l):
        v = pltpu.roll(hy[...], lax.rem(W - l, W), axis=1)
        return jnp.broadcast_to(v[:, 0:1], (X, W))

    def y_shifts(v0, v1, e0, e1):
        r0, r1 = pltpu.roll(v0, 1, axis=1), pltpu.roll(v1, 1, axis=1)
        q0, q1 = pltpu.roll(v0, W - 1, axis=1), pltpu.roll(v1, W - 1, axis=1)
        return (
            (jnp.where(lane == 0, e0, r0), jnp.where(lane == W - 1, q1, q0)),
            (jnp.where(lane == 0, r0, r1), jnp.where(lane == W - 1, e1, q1)),
        )

    start[2].wait_recv()
    lat = jnp.float32(LAT)
    sxm = jnp.where(row == 0, zero, lat)
    sxp = jnp.where(row == X - 1, zero, lat)
    sym = (jnp.where((lane == 0) & first_col, zero, lat), lat)
    syp = (lat, jnp.where((lane == W - 1) & last_col, zero, lat))

    def lateral(l, _):
        hy = column_of(ys.at[0], l)
        kc = (rk[0, l + 1], rk[1, l + 1])
        ysh = y_shifts(kc[0], kc[1], hy, hy)
        for h in (0, 1):
            km, kp = x_shifts(rk, h, l)
            a = sxm * rcp(kc[h] + km)
            b = sxp * rcp(kc[h] + kp)
            c = sym[h] * rcp(kc[h] + ysh[h][0])
            d = syp[h] * rcp(kc[h] + ysh[h][1])
            gxm[h, l], gxp[h, l], gym[h, l], gyp[h, l] = a, b, c, d
            c0[h, l] = cap[h, l] - ((a + b) + (c + d))
        return 0

    loop(L, lateral, 0, 8)

    for side in (0, 1):
        pack_rows(us, uvx.at[side, 0], side, 0)
        pack_rows(vs, uvx.at[side, 1], side, 0)
    pack_column(us, 0, uvy.at[0])
    pack_column(vs, 0, uvy.at[1])
    uv = [
        send(M_UV, uvx.at[1], uvxr.at[0], up),
        send(M_UV + 1, uvx.at[0], uvxr.at[1], down),
        send(M_UV + 2, uvy, uvyr, mate),
    ]

    def right_side(hy_ref):
        def body(l, carry):
            bf, bl = carry
            hy = column_of(hy_ref, l)
            tc = (temp[0, l + 1], temp[1, l + 1])
            ysh = y_shifts(tc[0], tc[1], hy, hy)
            nf, nl = [], []
            for h in (0, 1):
                tm, tp = x_shifts(temp, h, l)
                d = (c0[h, l] * tc[h] + src[h, l]) + (
                    (gxm[h, l] * tm + gxp[h, l] * tp)
                    + (gym[h, l] * ysh[h][0] + gyp[h, l] * ysh[h][1])
                )
                rhs[h, l] = d
                nf.append(bf[h] + us[h, l] * d)
                nl.append(bl[h] + vs[h, l] * d)
            return tuple(nf), tuple(nl)

        z = jnp.zeros((X, W), jnp.float32)
        return loop(L, body, ((z, z), (z, z)), 8)

    def side_row(ref, s, h, off):
        view = ref.reshape(2, ref.shape[1] * X, W)
        return view[h, pl.ds(off * X + (0 if s == 0 else X - 1), L, stride=X), :]

    def ghost_terms(ghost_rows, bf, bl):
        nf, nl = [], []
        for h in (0, 1):
            f_sum, l_sum = [], []
            for s in (0, 1):
                d = gg[s, h] * (ghost_rows[s, h] - side_row(temp, s, h, 1))
                dx[s, h] = d
                f_sum.append(jnp.sum(uvx[s, 0, h] * d, axis=0, keepdims=True))
                l_sum.append(jnp.sum(uvx[s, 1, h] * d, axis=0, keepdims=True))
            for out, old, sums in ((nf, bf, f_sum), (nl, bl, l_sum)):
                add = jnp.where(row == 0, sums[0], jnp.where(row == X - 1, sums[1], zero))
                out.append(old[h] + add)
        return nf, nl

    def add_rows(ref, rows_ref):
        view = ref.reshape(2, L * X, W)
        for h in (0, 1):
            for s, r in ((0, 0), (1, X - 1)):
                at = pl.ds(r, L, stride=X)
                view[h, at, :] = view[h, at, :] + rows_ref[s, h]

    def block_solve():
        def forward(i, carry):
            t, b = carry
            m = L - 1 - i
            base[:, i] = ip[:, i] * t
            base[:, m] = ip[:, m] * b
            return rhs[:, i + 1] + el[:, i] * t, rhs[:, m - 1] + el[:, m] * b

        t, b = loop(HALF - 1, forward, (rhs[:, 0], rhs[:, L - 1]), 4)
        t, b = mid[0] * t + mid[1] * b, mid[1] * t + mid[2] * b
        base[:, HALF - 1], base[:, HALF] = t, b

        def backward(i, carry):
            t, b = carry
            l, m = HALF - 2 - i, HALF + 1 + i
            t = base[:, l] + el[:, l] * t
            b = base[:, m] + el[:, m] * b
            base[:, l], base[:, m] = t, b
            return t, b

        loop(HALF - 1, backward, (t, b), 4)

    def solved(i, qt, qb):
        return base[:, i] + (us[:, i] * qt + vs[:, i] * qb)

    def correct(qt, qb):
        def body(i, _):
            temp[:, i + 1] = solved(i, qt, qb)
            return 0

        loop(L, body, 0, 4)

    def creep_tables(i, _):
        for h in (0, 1):
            at = pl.ds(i * 2, 2)
            c = code[h, at]
            md[h, at] = lookup(c, mod_table)
            ex[h, at] = lookup(c, expand_table)
            fl[h, at] = jnp.where(flag[h, at] == 1, jnp.float32(RATE), zero)
        return 0

    def creep_cell(t, c, hd, m, e, im, active):
        load = im - e * t
        s = m * (load - c)
        z = jnp.abs(s) * (rcp(hd) * jnp.float32(0.5 * LOG2E))
        d = jnp.exp2(z - 1.0) - jnp.exp2(-1.0 - z)
        arr = jnp.exp2(jnp.float32(0.5 * LOG2E) * jnp.tanh(0.25 * t + jnp.float32(HALF_LN2)))
        rate = (active * arr) * d
        q = jnp.exp2(jnp.float32(-0.1 * LOG2E) * jnp.log(0.5 + d))
        gap = 1.0 - (0.5 * hd) * q
        size = jnp.abs(gap)
        root = size * lax.rsqrt(jnp.maximum(size, jnp.float32(1e-30)))
        cn = c + jnp.where(s < 0.0, -rate, rate)
        return cn, hd + (gap * root) * rate, m * (load - cn)

    state = (cre, har, md, ex, imp, fl)

    def creep():
        def body(i, _):
            cre[:, i], har[:, i], _s = creep_cell(temp[:, i + 1], *[a[:, i] for a in state])
            return 0

        loop(L, body, 0, 4)

    hy_ref = ys.at[1]
    loaded("src")
    for n in range(TSTEPS):
        bf, bl = right_side(hy_ref)
        if n == 0:
            for m in start[:2]:
                m.wait_recv()
            for s in (0, 1):
                wide = jnp.where(p == (0 if s == 0 else np_ - 1), zero, lat)
                for h in (0, 1):
                    gg[s, h] = wide * rcp(sx[s, 0, h] + xs[s, 0, h])
            bf, bl = ghost_terms(xs.at[:, 1], bf, bl)
        else:
            for m in bases[:2] + fluxes[:2]:
                m.wait_recv()
            for side, at in ((0, 7), (1, 0)):
                for h in (0, 1):
                    ghost[side, h] = bxr[n - 1, side, h] + (
                        uvxr[side, 0, h] * qx[n - 1, side, 0, h, at : at + 1, :]
                        + uvxr[side, 1, h] * qx[n - 1, side, 1, h, at : at + 1, :]
                    )
            bf, bl = ghost_terms(ghost, bf, bl)
        for h in (0, 1):
            abuf[n, k, 0, h] = bf[h]
            abuf[n, k, 1, h] = bl[h]
        ends = [
            send(M_A + 3 * n + o, abuf.at[n, k], abuf.at[n, k], others[o]) for o in range(3)
        ]
        add_rows(rhs, dx)
        block_solve()
        more = n < TSTEPS - 1
        if more:
            for side in (0, 1):
                pack_rows(base, bx.at[n, side], side, 0)
            pack_column(base, 0, by.at[n])
            bases = [
                send(M_B + 3 * n, bx.at[n, 1], bxr.at[n, 0], up),
                send(M_B + 3 * n + 1, bx.at[n, 0], bxr.at[n, 1], down),
                send(M_B + 3 * n + 2, by.at[n], byr.at[n], mate),
            ]
        if n == 0:
            loaded("flag")
            loop(L // 2, creep_tables, 0, 2)
            loaded("imp")
            for j, a in enumerate((md, ex, imp, fl)):
                pack_column(a, 0, pc.at[2 + j])
            for m in spread:
                m.wait_recv()
            a1 = planes[0, 1] + planes[1, 0]
            a2 = planes[1, 1] + planes[2, 0]
            a3 = planes[2, 1] + planes[3, 0]
            b1, b2 = planes[1, 2], planes[2, 2]
            d12 = a1 * a2 - b1 * b1
            idet = rcp(d12 * a3 - a1 * (b2 * b2))
            v11, v12, v13 = (a2 * a3 - b2 * b2) * idet, b1 * a3 * idet, b1 * b2 * idet
            v22, v23, v33 = a1 * a3 * idet, a1 * b2 * idet, d12 * idet
            table = ((v11, v12, v13), (v12, v22, v23), (v13, v23, v33))
            for j in range(3):
                for r, shift, sign in ((0, 0, 1.0), (1, 1, -1.0)):
                    at = k + shift
                    v = jnp.where(
                        at == 1, table[0][j],
                        jnp.where(at == 2, table[1][j], jnp.where(at == 3, table[2][j], zero)),
                    )
                    red[r, j] = v * sign
        else:
            if n == 1:
                for name in ("cre", "har"):
                    loaded(name)
            creep()
            if not more:
                pack_column(base, 0, pc.at[6])
                pack_column(cre, 0, pc.at[0])
                pack_column(har, 0, pc.at[1])
        for m in ends:
            m.wait_recv()
        r = [abuf[n, j, 1] - abuf[n, j + 1, 0] for j in range(3)]
        qt, qb = [
            red[s, 0] * r[0] + red[s, 1] * r[1] + red[s, 2] * r[2] for s in (0, 1)
        ]
        if more:
            qbuf[n, 0], qbuf[n, 1] = qt, qb
            fluxes = [
                send(M_C + 3 * n, qbuf.at[n, :, :, pl.ds(8, 8)], qx.at[n, 0], up),
                send(M_C + 3 * n + 1, qbuf.at[n, :, :, pl.ds(0, 8)], qx.at[n, 1], down),
                send(M_C + 3 * n + 2, qbuf.at[n, :, 1 - f], qy.at[n], mate),
            ]
        if more:
            correct(qt, qb)
            if n == 0:
                for m in uv:
                    m.wait_recv()
            bases[2].wait_recv()
            fluxes[2].wait_recv()
            col = [
                jnp.broadcast_to(pltpu.roll(qy[n, s], f, axis=1)[:, 0:1], (X, W)) for s in (0, 1)
            ]
            ghosty[...] = byr[n] + (uvyr[0] * col[0] + uvyr[1] * col[1])
            hy_ref = ghosty

    qend[0], qend[1] = qt, qb
    col = [
        jnp.broadcast_to(pltpu.roll(qend[j, 1 - f], 1 - f, axis=1)[:, 0:1], (X, W)) for j in (0, 1)
    ]
    tc = pc[6] + (uvy[0] * col[0] + uvy[1] * col[1])
    used = jnp.where(lane < L, pc[1], jnp.float32(1.0))
    fy[...] = creep_cell(tc, pc[0], used, *[pc[2 + j] for j in range(4)])[2]
    beside = send(M_F + 2, fy, fyr, mate)
    for s, r in ((0, 0), (1, X - 1)):
        for h in (0, 1):
            t = side_row(base, s, h, 0) + (
                uvx[s, 0, h] * qend[0, h, r : r + 1, :] + uvx[s, 1, h] * qend[1, h, r : r + 1, :]
            )
            fx[s, h] = creep_cell(t, *[side_row(a, s, h, 0) for a in state])[2]
    for j, l in ((0, 0), (1, L - 1)):
        zs[j] = creep_cell(solved(l, qt, qb), *[a[:, l] for a in state])[2]
    edges = [
        send(M_F, fx.at[1], fxr.at[0], up),
        send(M_F + 1, fx.at[0], fxr.at[1], down),
        send(M_F + 3, zs.at[1], zm, others[0]),
        send(M_F + 4, zs.at[0], zp, others[2]),
    ]

    lag = 8

    def last_creep(i):
        t = solved(i, qt, qb)
        t_end[:, i] = t
        cre[:, i], har[:, i], stress[:, i + 1] = creep_cell(t, *[a[:, i] for a in state])

    def residual(l):
        hy = column_of(fyr, l)
        sc = (stress[0, l + 1], stress[1, l + 1])
        ysh = y_shifts(
            sc[0], sc[1], jnp.where(first_col, zero, hy), jnp.where(last_col, zero, hy)
        )
        for h in (0, 1):
            sm, sp = x_shifts(stress, h, l)
            sm, sp = jnp.where(row == 0, zero, sm), jnp.where(row == X - 1, zero, sp)
            rhs[h, l] = (
                ((stress[h, l + 2] + stress[h, l]) + (sm + sp))
                + (ysh[h][0] + ysh[h][1])
            ) - 6.0 * sc[h]

    def first_layers(i, _):
        last_creep(i)
        return 0

    def both(i, _):
        last_creep(i + lag)
        residual(i)
        return 0

    def last_layers(i, _):
        residual(i + L - lag)
        return 0

    loop(lag, first_layers, 0, 4)
    beside.wait_recv()
    loop(L - lag, both, 0, 4)
    loop(lag, last_layers, 0, 8)
    for m in edges:
        m.wait_recv()
    rhs[:, 0] = rhs[:, 0] + jnp.where(k == 0, zero, zm[...])
    rhs[:, L - 1] = rhs[:, L - 1] + jnp.where(k == ns - 1, zero, zp[...])
    ghost[0] = jnp.where(p == 0, zero, fxr[0])
    ghost[1] = jnp.where(p == np_ - 1, zero, fxr[1])
    add_rows(rhs, ghost)
    for m in sent:
        m.wait_send()


def write_out(temp, cre, har, res, t_out, c_out, h_out, s_out, sem):
    copies = []
    for i, (vm, hbm) in enumerate(
        ((temp, t_out), (cre, c_out), (har, h_out), (res, s_out))
    ):
        for h in (0, 1):
            copies.append(pltpu.make_async_copy(
                vm.at[h], hbm.at[:, :, pl.ds(W * h, W)], sem.at[i, h]
            ))
    for cp in copies:
        cp.start()
    for cp in copies:
        cp.wait()


def per_device(*args):
    f32 = jnp.float32
    block = (2, L, X, W)
    tall = (2, L + 2, X, W)

    def vm(*shape):
        return pltpu.VMEM(shape, f32)

    scratch = [
        pltpu.VMEM(block, jnp.int32), pltpu.VMEM(block, jnp.int32), vm(*tall),
        vm(*block), vm(*block),
        vm(*tall),
        *[vm(*block) for _ in range(14)],
        vm(*tall),
        vm(3, 2, X, W), vm(2, 3, 2, X, W),
        vm(4, 3, 2, X, W), vm(TSTEPS, 4, 2, 2, X, W), vm(2, 2, 2, X, W),
        vm(2, 2, 2, L, W), vm(2, X, W), vm(2, 2, 2, L, W), vm(2, X, W),
        vm(2, X, W),
        vm(2, 2, 2, L, W), vm(2, X, W), vm(2, 2, 2, L, W), vm(2, X, W),
        vm(2, 2, 2, L, W), vm(2, X, W), vm(2, 2, 2, L, W), vm(2, X, W),
        vm(2, 2, 2, 2, 8, W), vm(2, 2, X, W),
        vm(2, 2, L, W), vm(X, W),
        vm(2, 2, L, W), vm(X, W), vm(2, 2, L, W), vm(X, W),
        vm(2, 2, X, W), vm(2, X, W), vm(2, X, W),
        vm(2, 2, L, W), vm(2, 2, L, W),
        vm(7, X, W), vm(2, 2, X, W),
        pltpu.SemaphoreType.DMA((7, 2)),
        pltpu.SemaphoreType.DMA((N_MSG,)), pltpu.SemaphoreType.DMA((N_MSG,)),
    ]
    shape = args[0].shape
    results = pl.pallas_call(
        kernel,
        out_shape=[jax.ShapeDtypeStruct(s, f32) for s in (block,) * 4],
        in_specs=[pl.BlockSpec(memory_space=pltpu.HBM)] * 7,
        out_specs=[pl.BlockSpec(memory_space=pltpu.VMEM)] * 4,
        scratch_shapes=scratch,
        compiler_params=pltpu.CompilerParams(
            collective_id=0, has_side_effects=True, vmem_limit_bytes=49 << 20
        ),
        name="thermal_creep_step",
    )(*args)
    return pl.pallas_call(
        write_out,
        out_shape=[jax.ShapeDtypeStruct(shape, f32)] * 4,
        in_specs=[pl.BlockSpec(memory_space=pltpu.VMEM)] * 4,
        out_specs=[pl.BlockSpec(memory_space=pltpu.HBM)] * 4,
        scratch_shapes=[pltpu.SemaphoreType.DMA((4, 2))],
        compiler_params=pltpu.CompilerParams(vmem_limit_bytes=16 << 20),
        name="write_out",
    )(*results)


def solution(mesh):
    spec = P("stack", "plane", "phys")
    return jax.shard_map(
        per_device, mesh=mesh, in_specs=(spec,) * 7, out_specs=(spec,) * 4, check_vma=False
    )
```

```python
import functools

import jax
import jax.numpy as jnp
from jax import lax
from jax.experimental import pallas as pl
from jax.experimental.pallas import tpu as pltpu
from jax.sharding import PartitionSpec as P

MESH = pl.DeviceIdType.MESH
TSTEPS = 3
L, X, W = 64, 16, 128
HALF = L // 2

k_table = (4.0, 0.6, 2.5, 1.2, 0.8)
cap_table = (1.6, 1.8, 1.7, 2.0, 1.9)
mod_table = (1.5, 0.6, 0.9, 1.2, 0.8)
expand_table = (0.1, 0.3, 0.25, 0.15, 0.2)
half_resistance = tuple(0.5 / k for k in k_table)
capacities = tuple(0.0003 * c for c in cap_table)
LAT = 1.2e-05
H_CONV = 0.05
LOG2E = 1.4426950408889634
HALF_LN2 = 0.34657359027997264
RATE = 0.05 * 0.22313016014842982

M_START, M_RZ, M_S, M_UV, M_A, M_B, M_C, M_F = 0, 3, 4, 7, 10, 19, 25, 31
M_GS, M_GA = 36, 44
N_MSG = 60


def rcp(x):
    return pl.reciprocal(x)


def lookup(c, t):
    low = jnp.where(c < 1, jnp.float32(t[0]), jnp.float32(t[1]))
    top = jnp.where(c < 4, jnp.float32(t[3]), jnp.float32(t[4]))
    return jnp.where(c < 2, low, jnp.where(c < 3, jnp.float32(t[2]), top))


def flat(ref):
    return ref.reshape(2, (L + 2) * X, W)


def shifted(ref, h, l, off):
    return flat(ref)[h, pl.ds(l * X + X + off, X), :]


def loop(n, body, carry, unroll):
    return lax.fori_loop(0, n, body, carry, unroll=unroll)


def kernel(
    t_in, src_in, code_in, flag_in, imp_in, cre_in, har_in,
    t_end, cre, har, rhs,
    code, flag, temp, src, imp,
    rk, cap, ip, el, us, vs, gxm, gxp, gym, gyp, c0, base, md, ex, fl, stress,
    mid, red, planes, abuf, qbuf,
    sx, sy, xs, ys, rz, uvx, uvy, uvxr, uvyr, bx, by, bxr, byr, qy,
    ghost, fx, fy, fxr, fyr, zs, zm, zp, gg, dx, pc, qend,
    gs_out, gs, ga_out, ga, gred, ggy, dy,
    in_sem, ss, rs,
):
    k = lax.axis_index("stack")
    p = lax.axis_index("plane")
    f = lax.axis_index("phys")
    ns, np_ = 4, 32
    up = {"plane": lax.rem(p + 1, np_)}
    down = {"plane": lax.rem(p + np_ - 1, np_)}
    mate = {"phys": 1 - f}
    others = [{"stack": lax.rem(k + o, ns)} for o in (1, 2, 3)]
    first_col, last_col = f == 0, f == 1

    def dev(where):
        return (where.get("stack", k), where.get("plane", p), where.get("phys", f))

    barrier = pltpu.get_barrier_semaphore()
    aside = [
        [{"stack": lax.rem(k + o, ns), **side} for o in range(4)] for side in (down, up)
    ]
    peers = [mate] + others + aside[0] + aside[1]
    for w in peers:
        pl.semaphore_signal(barrier, inc=1, device_id=dev(w), device_id_type=MESH)

    loads = {}
    for i, (name, hbm, vm, off) in enumerate((
        ("code", code_in, code, 0), ("temp", t_in, temp, 1), ("src", src_in, src, 0),
        ("flag", flag_in, flag, 0), ("imp", imp_in, imp, 0), ("cre", cre_in, cre, 0),
        ("har", har_in, har, 0),
    )):
        loads[name] = []
        for h in (0, 1):
            cp = pltpu.make_async_copy(
                hbm.at[:, :, pl.ds(W * h, W)], vm.at[h, pl.ds(off, L)], in_sem.at[i, h]
            )
            loads[name].append(cp)

    def load(*names):
        for name in names:
            for cp in loads[name]:
                cp.start()

    load("code", "temp")

    def loaded(name):
        for cp in loads[name]:
            cp.wait()

    def message(i, s, d, where):
        return pltpu.make_async_remote_copy(
            src_ref=s, dst_ref=d, send_sem=ss.at[i], recv_sem=rs.at[i],
            device_id=dev(where), device_id_type=MESH,
        )

    sent = []

    def send(i, s, d, where):
        m = message(i, s, d, where)
        m.start()
        sent.append(m)
        return m

    row = lax.broadcasted_iota(jnp.int32, (X, W), 0)
    lane = lax.broadcasted_iota(jnp.int32, (X, W), 1)
    zero = jnp.float32(0.0)

    blank = jnp.zeros((2, X, W), jnp.float32)
    for edge in (0, L + 1):
        rk[:, edge], temp[:, edge], stress[:, edge] = blank + 1.0, blank, blank

    loaded("code")
    load("src")

    def tables(i, _):
        for h in (0, 1):
            c = code[h, pl.ds(i * 2, 2)]
            rk[h, pl.ds(i * 2 + 1, 2)] = lookup(c, half_resistance)
            cap[h, pl.ds(i * 2, 2)] = lookup(c, capacities)
        return 0

    loop(L // 2, tables, 0, 4)

    def pack_rows(ref, dst, side, off):
        r = 0 if side == 0 else X - 1
        n = ref.shape[1]
        view = ref.reshape(2, n * X, W)
        for h in (0, 1):
            dst[h] = view[h, pl.ds(off * X + r, L, stride=X), :]

    def pack_column(ref, off, dst):
        def body(l, acc):
            v = pltpu.roll(ref[1 - f, l + off], lax.rem(l + 1 - f, W), axis=1)
            return jnp.where(lane == l, v, acc)

        dst[...] = loop(L, body, jnp.zeros((X, W), jnp.float32), L)

    loaded("temp")
    load("flag", "imp", "cre", "har")
    for side in (0, 1):
        pack_rows(rk, sx.at[side, 0], side, 1)
        pack_rows(temp, sx.at[side, 1], side, 1)
    pl.semaphore_wait(barrier, len(peers))
    start = [
        send(M_START, sx.at[1], xs.at[0], up),
        send(M_START + 1, sx.at[0], xs.at[1], down),
    ]
    to_below = send(M_RZ, rk.at[:, L], rz, others[0])
    pack_column(rk, 1, sy.at[0])
    pack_column(temp, 1, sy.at[1])
    start.append(send(M_START + 2, sy, ys, mate))

    one = jnp.ones((2, X, W), jnp.float32)
    top_cap = cap[:, 0] + jnp.where(k == 0, jnp.float32(H_CONV), zero)
    bottom_cap = cap[:, L - 1] + jnp.where(k == ns - 1, jnp.float32(H_CONV), zero)

    def eliminate(i, carry):
        dt, nt, wt, db, nb, wb = carry
        m = L - 1 - i
        g = rcp(rk[:, i + 1] + rk[:, i + 2])
        dn = g * dt + nt
        nn = cap[:, i + 1] * dn + g * nt
        ipv = dt * rcp(dn)
        e = g * ipv
        ip[:, i] = ipv
        el[:, i] = e
        us[:, i] = ipv * wt
        gb = rcp(rk[:, m + 1] + rk[:, m])
        dbn = gb * db + nb
        nbn = cap[:, m - 1] * dbn + gb * nb
        ipb = db * rcp(dbn)
        eb = gb * ipb
        ip[:, m] = ipb
        el[:, m] = eb
        vs[:, m] = ipb * wb
        return dn, nn, e * wt, dbn, nbn, eb * wb

    dt, nt, wt, db, nb, wb = loop(
        HALF - 1, eliminate, (one, top_cap, one, one, bottom_cap, one), 4
    )
    st, sb = nt * rcp(dt), nb * rcp(db)
    gm = rcp(rk[:, HALF] + rk[:, HALF + 1])
    idet = rcp(st * sb + gm * (st + sb))
    m11, m12, m22 = (sb + gm) * idet, gm * idet, (st + gm) * idet
    mid[0], mid[1], mid[2] = m11, m12, m22
    ut, ub, vt, vb = m11 * wt, m12 * wt, m12 * wb, m22 * wb
    us[:, HALF - 1], us[:, HALF], vs[:, HALF - 1], vs[:, HALF] = ut, ub, vt, vb

    def spikes(i, carry):
        ut, ub, vt, vb = carry
        l, m = HALF - 2 - i, HALF + 1 + i
        e, eb = el[:, l], el[:, m]
        ut = us[:, l] + e * ut
        vt = e * vt
        ub = eb * ub
        vb = vs[:, m] + eb * vb
        us[:, l], vs[:, l], us[:, m], vs[:, m] = ut, vt, ub, vb
        return ut, ub, vt, vb

    ut, ub, vt, vb = loop(HALF - 1, spikes, (ut, ub, vt, vb), 4)
    to_below.wait_recv()
    planes[k, 0] = ut + rz[...] + rk[:, 1]
    planes[k, 1] = vb
    planes[k, 2] = ub
    spread = [
        send(M_S + o, planes.at[k], planes.at[k], others[o]) for o in range(3)
    ]

    eight = lax.broadcasted_iota(jnp.int32, (8, W), 0)

    def tile(rows_):
        out = jnp.zeros((8, W), jnp.float32)
        for i, r in enumerate(rows_):
            out = jnp.where(eight == i, r, out)
        return out

    def send_rows(first, out, into):
        return [
            send(first + 4 * side + o, out.at[side], into.at[1 - side, k], aside[side][o])
            for side in (0, 1) for o in range(4)
        ]

    for side, r in ((0, 0), (1, X - 1)):
        gs_out[side] = tile([planes[k, i, h, r : r + 1, :] for i in range(3) for h in (0, 1)])
    spread += send_rows(M_GS, gs_out, gs)

    def x_shifts(ref, h, l):
        return shifted(ref, h, l, -1), shifted(ref, h, l, 1)

    def column_of(hy, l):
        v = pltpu.roll(hy[...], lax.rem(W - l, W), axis=1)
        return jnp.broadcast_to(v[:, 0:1], (X, W))

    def y_shifts(v0, v1, edges=None):
        r0, r1 = pltpu.roll(v0, 1, axis=1), pltpu.roll(v1, 1, axis=1)
        q0, q1 = pltpu.roll(v0, W - 1, axis=1), pltpu.roll(v1, W - 1, axis=1)
        m1, p0 = jnp.where(lane == 0, r0, r1), jnp.where(lane == W - 1, q1, q0)
        if edges is None:
            return (r0, p0), (m1, q1)
        return (
            (jnp.where(lane == 0, edges[0], r0), p0),
            (m1, jnp.where(lane == W - 1, edges[1], q1)),
        )

    lat = jnp.float32(LAT)
    sxm = jnp.where(row == 0, zero, lat)
    sxp = jnp.where(row == X - 1, zero, lat)
    sym = (jnp.where(lane == 0, zero, lat), lat)
    syp = (lat, jnp.where(lane == W - 1, zero, lat))

    def lateral(l, _):
        kc = (rk[0, l + 1], rk[1, l + 1])
        ysh = y_shifts(kc[0], kc[1])
        for h in (0, 1):
            km, kp = x_shifts(rk, h, l)
            a = sxm * rcp(kc[h] + km)
            b = sxp * rcp(kc[h] + kp)
            c = sym[h] * rcp(kc[h] + ysh[h][0])
            d = syp[h] * rcp(kc[h] + ysh[h][1])
            gxm[h, l], gxp[h, l], gym[h, l], gyp[h, l] = a, b, c, d
            c0[h, l] = cap[h, l] - ((a + b) + (c + d))
        return 0

    loop(L, lateral, 0, 8)

    for side in (0, 1):
        pack_rows(us, uvx.at[side, 0], side, 0)
        pack_rows(vs, uvx.at[side, 1], side, 0)
    pack_column(us, 0, uvy.at[0])
    pack_column(vs, 0, uvy.at[1])
    uv = [
        send(M_UV, uvx.at[1], uvxr.at[0], up),
        send(M_UV + 1, uvx.at[0], uvxr.at[1], down),
        send(M_UV + 2, uvy, uvyr, mate),
    ]

    def right_side():
        def body(l, carry):
            bf, bl = carry
            tc = (temp[0, l + 1], temp[1, l + 1])
            ysh = y_shifts(tc[0], tc[1])
            nf, nl = [], []
            for h in (0, 1):
                tm, tp = x_shifts(temp, h, l)
                d = (c0[h, l] * tc[h] + src[h, l]) + (
                    (gxm[h, l] * tm + gxp[h, l] * tp)
                    + (gym[h, l] * ysh[h][0] + gyp[h, l] * ysh[h][1])
                )
                rhs[h, l] = d
                nf.append(bf[h] + us[h, l] * d)
                nl.append(bl[h] + vs[h, l] * d)
            return tuple(nf), tuple(nl)

        z = jnp.zeros((X, W), jnp.float32)
        return loop(L, body, ((z, z), (z, z)), 8)

    def side_row(ref, s, h, off):
        view = ref.reshape(2, ref.shape[1] * X, W)
        return view[h, pl.ds(off * X + (0 if s == 0 else X - 1), L, stride=X), :]

    edge_lane = (W - 1) * (1 - f)
    edge_masks = ((lane == 0) & last_col, (lane == W - 1) & first_col)

    def add_column():
        def body(l, _):
            hy = column_of(dy, l)
            rhs[1 - f, l] = rhs[1 - f, l] + jnp.where(lane == edge_lane, hy, zero)
            return 0

        loop(L, body, 0, 8)

    def edge_column(q, j, shift):
        return jnp.broadcast_to(pltpu.roll(q[j], shift, axis=1)[:, 0:1], (X, W))

    def ghost_terms(ghost_rows, ghost_column, own_column, bf, bl):
        d = jnp.where(lane < L, ggy[...] * (ghost_column - own_column), zero)
        dy[...] = d
        sums = [jnp.sum(uvy[j] * d, axis=1, keepdims=True) for j in (0, 1)]
        bf, bl = [
            [old[h] + jnp.where(edge_masks[h], sums[j], zero) for h in (0, 1)]
            for j, old in ((0, bf), (1, bl))
        ]
        nf, nl = [], []
        for h in (0, 1):
            f_sum, l_sum = [], []
            for s in (0, 1):
                d = gg[s, h] * (ghost_rows[s, h] - side_row(temp, s, h, 1))
                dx[s, h] = d
                f_sum.append(jnp.sum(uvx[s, 0, h] * d, axis=0, keepdims=True))
                l_sum.append(jnp.sum(uvx[s, 1, h] * d, axis=0, keepdims=True))
            for out, old, sums in ((nf, bf, f_sum), (nl, bl, l_sum)):
                add = jnp.where(row == 0, sums[0], jnp.where(row == X - 1, sums[1], zero))
                out.append(old[h] + add)
        return nf, nl

    def add_rows(ref, rows_ref):
        view = ref.reshape(2, L * X, W)
        for h in (0, 1):
            for s, r in ((0, 0), (1, X - 1)):
                at = pl.ds(r, L, stride=X)
                view[h, at, :] = view[h, at, :] + rows_ref[s, h]

    def block_solve():
        def forward(i, carry):
            t, b = carry
            m = L - 1 - i
            base[:, i] = ip[:, i] * t
            base[:, m] = ip[:, m] * b
            return rhs[:, i + 1] + el[:, i] * t, rhs[:, m - 1] + el[:, m] * b

        t, b = loop(HALF - 1, forward, (rhs[:, 0], rhs[:, L - 1]), 4)
        t, b = mid[0] * t + mid[1] * b, mid[1] * t + mid[2] * b
        base[:, HALF - 1], base[:, HALF] = t, b

        def backward(i, carry):
            t, b = carry
            l, m = HALF - 2 - i, HALF + 1 + i
            t = base[:, l] + el[:, l] * t
            b = base[:, m] + el[:, m] * b
            base[:, l], base[:, m] = t, b
            return t, b

        loop(HALF - 1, backward, (t, b), 4)

    def solved(i, qt, qb):
        return base[:, i] + (us[:, i] * qt + vs[:, i] * qb)

    def correct(qt, qb):
        def body(i, _):
            temp[:, i + 1] = solved(i, qt, qb)
            return 0

        loop(L, body, 0, 4)

    def creep_tables(i, _):
        for h in (0, 1):
            at = pl.ds(i * 2, 2)
            c = code[h, at]
            md[h, at] = lookup(c, mod_table)
            ex[h, at] = lookup(c, expand_table)
            fl[h, at] = jnp.where(flag[h, at] == 1, jnp.float32(RATE), zero)
        return 0

    def creep_cell(t, c, hd, m, e, im, active):
        load = im - e * t
        s = m * (load - c)
        z = jnp.abs(s) * (rcp(hd) * jnp.float32(0.5 * LOG2E))
        d = jnp.exp2(z - 1.0) - jnp.exp2(-1.0 - z)
        arr = jnp.exp2(jnp.float32(0.5 * LOG2E) * jnp.tanh(0.25 * t + jnp.float32(HALF_LN2)))
        rate = (active * arr) * d
        q = jnp.exp2(jnp.float32(-0.1 * LOG2E) * jnp.log(0.5 + d))
        gap = 1.0 - (0.5 * hd) * q
        size = jnp.abs(gap)
        root = size * lax.rsqrt(jnp.maximum(size, jnp.float32(1e-30)))
        cn = c + jnp.where(s < 0.0, -rate, rate)
        return cn, hd + (gap * root) * rate, m * (load - cn)

    state = (cre, har, md, ex, imp, fl)

    def creep():
        def body(i, _):
            cre[:, i], har[:, i], _s = creep_cell(temp[:, i + 1], *[a[:, i] for a in state])
            return 0

        loop(L, body, 0, 4)

    def interface_system(part, put):
        a1 = part(0, 1) + part(1, 0)
        a2 = part(1, 1) + part(2, 0)
        a3 = part(2, 1) + part(3, 0)
        b1, b2 = part(1, 2), part(2, 2)
        d12 = a1 * a2 - b1 * b1
        idet = rcp(d12 * a3 - a1 * (b2 * b2))
        v11, v12, v13 = (a2 * a3 - b2 * b2) * idet, b1 * a3 * idet, b1 * b2 * idet
        v22, v23, v33 = a1 * a3 * idet, a1 * b2 * idet, d12 * idet
        table = ((v11, v12, v13), (v12, v22, v23), (v13, v23, v33))
        for j in range(3):
            for r, sign in ((0, 1.0), (1, -1.0)):
                at = k + r
                v = jnp.where(
                    at == 1, table[0][j],
                    jnp.where(at == 2, table[1][j], jnp.where(at == 3, table[2][j], zero)),
                )
                put(r, j, v * sign)

    loaded("src")
    for n in range(TSTEPS):
        bf, bl = right_side()
        if n == 0:
            for m in start:
                m.wait_recv()
            for s in (0, 1):
                wide = jnp.where(p == (0 if s == 0 else np_ - 1), zero, lat)
                for h in (0, 1):
                    gg[s, h] = wide * rcp(sx[s, 0, h] + xs[s, 0, h])
            ggy[...] = jnp.where(lane < L, lat * rcp(sy[0] + ys[0]), zero)
            bf, bl = ghost_terms(xs.at[:, 1], ys[1], sy[1], bf, bl)
        else:
            if n == 1:
                for m in uv:
                    m.wait_recv()
            for m in bases + beside_flux + ghost_ends:
                m.wait_recv()
            for side in (0, 1):
                d = [ga[n - 1, side, j, 2:4, :] - ga[n - 1, side, j + 1, 0:2, :] for j in range(3)]
                qg = [
                    gred[side, r, 0, 0:2, :] * d[0] + gred[side, r, 1, 0:2, :] * d[1]
                    + gred[side, r, 2, 0:2, :] * d[2]
                    for r in (0, 1)
                ]
                for h in (0, 1):
                    ghost[side, h] = bxr[n - 1, side, h] + (
                        uvxr[side, 0, h] * qg[0][h : h + 1, :] + uvxr[side, 1, h] * qg[1][h : h + 1, :]
                    )
            far = [edge_column(qy.at[n - 1], j, f) for j in (0, 1)]
            near = [edge_column(qbuf.at[n - 1, :, 1 - f], j, 1 - f) for j in (0, 1)]
            bf, bl = ghost_terms(
                ghost,
                byr[n - 1] + (uvyr[0] * far[0] + uvyr[1] * far[1]),
                by[n - 1] + (uvy[0] * near[0] + uvy[1] * near[1]),
                bf, bl,
            )
        for h in (0, 1):
            abuf[n, k, 0, h] = bf[h]
            abuf[n, k, 1, h] = bl[h]
        ends = [
            send(M_A + 3 * n + o, abuf.at[n, k], abuf.at[n, k], others[o]) for o in range(3)
        ]
        more = n < TSTEPS - 1
        if more:
            for side, r in ((0, 0), (1, X - 1)):
                ga_out[n, side] = tile([v[h][r : r + 1, :] for v in (bf, bl) for h in (0, 1)])
            ghost_ends = send_rows(M_GA + 8 * n, ga_out.at[n], ga.at[n])
        add_rows(rhs, dx)
        add_column()
        block_solve()
        if more:
            for side in (0, 1):
                pack_rows(base, bx.at[n, side], side, 0)
            pack_column(base, 0, by.at[n])
            bases = [
                send(M_B + 3 * n, bx.at[n, 1], bxr.at[n, 0], up),
                send(M_B + 3 * n + 1, bx.at[n, 0], bxr.at[n, 1], down),
                send(M_B + 3 * n + 2, by.at[n], byr.at[n], mate),
            ]
        if n == 0:
            loaded("flag")
            loop(L // 2, creep_tables, 0, 2)
            loaded("imp")
            for j, a in enumerate((md, ex, imp, fl)):
                pack_column(a, 0, pc.at[2 + j])
            for m in spread:
                m.wait_recv()
            interface_system(
                lambda j, i: planes[j, i], lambda r, j, v: red.__setitem__((r, j), v)
            )
            for side in (0, 1):
                interface_system(
                    lambda j, i, side=side: gs[side, j, 2 * i : 2 * i + 2, :],
                    lambda r, j, v, side=side: gred.__setitem__((side, r, j, slice(0, 2)), v),
                )
        else:
            if n == 1:
                for name in ("cre", "har"):
                    loaded(name)
            creep()
            if not more:
                pack_column(base, 0, pc.at[6])
                pack_column(cre, 0, pc.at[0])
                pack_column(har, 0, pc.at[1])
        for m in ends:
            m.wait_recv()
        r = [abuf[n, j, 1] - abuf[n, j + 1, 0] for j in range(3)]
        qt, qb = [
            red[s, 0] * r[0] + red[s, 1] * r[1] + red[s, 2] * r[2] for s in (0, 1)
        ]
        if more:
            qbuf[n, 0], qbuf[n, 1] = qt, qb
            beside_flux = [send(M_C + 3 * n + 2, qbuf.at[n, :, 1 - f], qy.at[n], mate)]
        if more:
            correct(qt, qb)

    qend[0], qend[1] = qt, qb
    for s, r in ((0, 0), (1, X - 1)):
        for h in (0, 1):
            t = side_row(base, s, h, 0) + (
                uvx[s, 0, h] * qend[0, h, r : r + 1, :] + uvx[s, 1, h] * qend[1, h, r : r + 1, :]
            )
            fx[s, h] = creep_cell(t, *[side_row(a, s, h, 0) for a in state])[2]
    for j, l in ((0, 0), (1, L - 1)):
        zs[j] = creep_cell(solved(l, qt, qb), *[a[:, l] for a in state])[2]
    edges = [
        send(M_F, fx.at[1], fxr.at[0], up),
        send(M_F + 1, fx.at[0], fxr.at[1], down),
        send(M_F + 3, zs.at[1], zm, others[0]),
        send(M_F + 4, zs.at[0], zp, others[2]),
    ]
    col = [
        jnp.broadcast_to(pltpu.roll(qend[j, 1 - f], 1 - f, axis=1)[:, 0:1], (X, W)) for j in (0, 1)
    ]
    tc = pc[6] + (uvy[0] * col[0] + uvy[1] * col[1])
    used = jnp.where(lane < L, pc[1], jnp.float32(1.0))
    fy[...] = creep_cell(tc, pc[0], used, *[pc[2 + j] for j in range(4)])[2]
    beside = send(M_F + 2, fy, fyr, mate)

    lag = 16

    def last_creep(i):
        t = solved(i, qt, qb)
        t_end[:, i] = t
        cre[:, i], har[:, i], stress[:, i + 1] = creep_cell(t, *[a[:, i] for a in state])

    def residual(l):
        hy = column_of(fyr, l)
        sc = (stress[0, l + 1], stress[1, l + 1])
        ysh = y_shifts(
            sc[0], sc[1], (jnp.where(first_col, zero, hy), jnp.where(last_col, zero, hy))
        )
        for h in (0, 1):
            sm, sp = x_shifts(stress, h, l)
            sm, sp = jnp.where(row == 0, zero, sm), jnp.where(row == X - 1, zero, sp)
            rhs[h, l] = (
                ((stress[h, l + 2] + stress[h, l]) + (sm + sp))
                + (ysh[h][0] + ysh[h][1])
            ) - 6.0 * sc[h]

    def first_layers(i, _):
        last_creep(i)
        return 0

    def both(i, _):
        last_creep(i + lag)
        residual(i)
        return 0

    def last_layers(i, _):
        residual(i + L - lag)
        return 0

    loop(lag, first_layers, 0, 4)
    beside.wait_recv()
    loop(L - lag, both, 0, 4)
    loop(lag, last_layers, 0, 8)
    for m in edges:
        m.wait_recv()
    rhs[:, 0] = rhs[:, 0] + jnp.where(k == 0, zero, zm[...])
    rhs[:, L - 1] = rhs[:, L - 1] + jnp.where(k == ns - 1, zero, zp[...])
    ghost[0] = jnp.where(p == 0, zero, fxr[0])
    ghost[1] = jnp.where(p == np_ - 1, zero, fxr[1])
    add_rows(rhs, ghost)
    for m in sent:
        m.wait_send()


def write_out(temp, cre, har, res, t_out, c_out, h_out, s_out, sem):
    copies = []
    for i, (vm, hbm) in enumerate(
        ((temp, t_out), (cre, c_out), (har, h_out), (res, s_out))
    ):
        for h in (0, 1):
            copies.append(pltpu.make_async_copy(
                vm.at[h], hbm.at[:, :, pl.ds(W * h, W)], sem.at[i, h]
            ))
    for cp in copies:
        cp.start()
    for cp in copies:
        cp.wait()


def per_device(*args):
    f32 = jnp.float32
    block = (2, L, X, W)
    tall = (2, L + 2, X, W)

    def vm(*shape):
        return pltpu.VMEM(shape, f32)

    scratch = [
        pltpu.VMEM(block, jnp.int32), pltpu.VMEM(block, jnp.int32), vm(*tall),
        vm(*block), vm(*block),
        vm(*tall),
        *[vm(*block) for _ in range(14)],
        vm(*tall),
        vm(3, 2, X, W), vm(2, 3, 2, X, W),
        vm(4, 3, 2, X, W), vm(TSTEPS, 4, 2, 2, X, W), vm(2, 2, 2, X, W),
        vm(2, 2, 2, L, W), vm(2, X, W), vm(2, 2, 2, L, W), vm(2, X, W),
        vm(2, X, W),
        vm(2, 2, 2, L, W), vm(2, X, W), vm(2, 2, 2, L, W), vm(2, X, W),
        vm(2, 2, 2, L, W), vm(2, X, W), vm(2, 2, 2, L, W), vm(2, X, W),
        vm(2, 2, X, W),
        vm(2, 2, L, W),
        vm(2, 2, L, W), vm(X, W), vm(2, 2, L, W), vm(X, W),
        vm(2, 2, X, W), vm(2, X, W), vm(2, X, W),
        vm(2, 2, L, W), vm(2, 2, L, W),
        vm(7, X, W), vm(2, 2, X, W),
        vm(2, 8, W), vm(2, 4, 8, W), vm(2, 2, 8, W), vm(2, 2, 4, 8, W),
        vm(2, 2, 3, 8, W), vm(X, W), vm(X, W),
        pltpu.SemaphoreType.DMA((7, 2)),
        pltpu.SemaphoreType.DMA((N_MSG,)), pltpu.SemaphoreType.DMA((N_MSG,)),
    ]
    shape = args[0].shape
    results = pl.pallas_call(
        kernel,
        out_shape=[jax.ShapeDtypeStruct(s, f32) for s in (block,) * 4],
        in_specs=[pl.BlockSpec(memory_space=pltpu.HBM)] * 7,
        out_specs=[pl.BlockSpec(memory_space=pltpu.VMEM)] * 4,
        scratch_shapes=scratch,
        compiler_params=pltpu.CompilerParams(
            collective_id=0, has_side_effects=True, vmem_limit_bytes=49 << 20
        ),
        name="thermal_creep_step",
    )(*args)
    return pl.pallas_call(
        write_out,
        out_shape=[jax.ShapeDtypeStruct(shape, f32)] * 4,
        in_specs=[pl.BlockSpec(memory_space=pltpu.VMEM)] * 4,
        out_specs=[pl.BlockSpec(memory_space=pltpu.HBM)] * 4,
        scratch_shapes=[pltpu.SemaphoreType.DMA((4, 2))],
        compiler_params=pltpu.CompilerParams(vmem_limit_bytes=16 << 20),
        name="write_out",
    )(*results)


def solution(mesh):
    spec = P("stack", "plane", "phys")
    return jax.shard_map(
        per_device, mesh=mesh, in_specs=(spec,) * 7, out_specs=(spec,) * 4, check_vma=False
    )
```

```python
import functools

import jax
import jax.numpy as jnp
from jax import lax
from jax.experimental import pallas as pl
from jax.experimental.pallas import tpu as pltpu
from jax.sharding import PartitionSpec as P

MESH = pl.DeviceIdType.MESH
TSTEPS = 3
L, X, W = 64, 16, 128
HALF = L // 2

k_table = (4.0, 0.6, 2.5, 1.2, 0.8)
cap_table = (1.6, 1.8, 1.7, 2.0, 1.9)
mod_table = (1.5, 0.6, 0.9, 1.2, 0.8)
expand_table = (0.1, 0.3, 0.25, 0.15, 0.2)
half_resistance = tuple(0.5 / k for k in k_table)
capacities = tuple(0.0003 * c for c in cap_table)
LAT = 1.2e-05
H_CONV = 0.05
LOG2E = 1.4426950408889634
HALF_LN2 = 0.34657359027997264
RATE = 0.05 * 0.22313016014842982

M_START, M_RZ, M_S, M_UV, M_A, M_B, M_C, M_F = 0, 3, 4, 7, 10, 19, 25, 31
M_GS, M_GA = 36, 44
N_MSG = 60


def rcp(x):
    return pl.reciprocal(x)


def lookup(c, t):
    low = jnp.where(c < 1, jnp.float32(t[0]), jnp.float32(t[1]))
    top = jnp.where(c < 4, jnp.float32(t[3]), jnp.float32(t[4]))
    return jnp.where(c < 2, low, jnp.where(c < 3, jnp.float32(t[2]), top))


def flat(ref):
    return ref.reshape(2, (L + 2) * X, W)


def shifted(ref, h, l, off):
    return flat(ref)[h, pl.ds(l * X + X + off, X), :]


def loop(n, body, carry, unroll):
    return lax.fori_loop(0, n, body, carry, unroll=unroll)


def kernel(
    t_in, src_in, code_in, flag_in, imp_in, cre_in, har_in,
    t_end, cre, har, rhs,
    code, flag, temp, src, imp,
    rk, cap, ip, el, us, vs, gxm, gxp, gym, gyp, c0, base, md, ex, fl, stress,
    mid, red, planes, abuf, qbuf,
    sx, sy, xs, ys, rz, uvx, uvy, uvxr, uvyr, bx, by, bxr, byr, qy,
    ghost, fx, fy, fxr, fyr, zs, zm, zp, gg, dx, pc, qend,
    gs_out, gs, ga_out, ga, gred, ggy, dy,
    in_sem, ss, rs,
):
    k = lax.axis_index("stack")
    p = lax.axis_index("plane")
    f = lax.axis_index("phys")
    ns, np_ = 4, 32
    up = {"plane": lax.rem(p + 1, np_)}
    down = {"plane": lax.rem(p + np_ - 1, np_)}
    mate = {"phys": 1 - f}
    others = [{"stack": lax.rem(k + o, ns)} for o in (1, 2, 3)]
    first_col, last_col = f == 0, f == 1

    def dev(where):
        return (where.get("stack", k), where.get("plane", p), where.get("phys", f))

    barrier = pltpu.get_barrier_semaphore()
    aside = [
        [{"stack": lax.rem(k + o, ns), **side} for o in range(4)] for side in (down, up)
    ]
    peers = [mate] + others + aside[0] + aside[1]
    for w in peers:
        pl.semaphore_signal(barrier, inc=1, device_id=dev(w), device_id_type=MESH)

    loads = {}
    for i, (name, hbm, vm, off) in enumerate((
        ("code", code_in, code, 0), ("temp", t_in, temp, 1), ("src", src_in, src, 0),
        ("flag", flag_in, flag, 0), ("imp", imp_in, imp, 0), ("cre", cre_in, cre, 0),
        ("har", har_in, har, 0),
    )):
        loads[name] = []
        for h in (0, 1):
            cp = pltpu.make_async_copy(
                hbm.at[:, :, pl.ds(W * h, W)], vm.at[h, pl.ds(off, L)], in_sem.at[i, h]
            )
            loads[name].append(cp)

    def load(*names):
        for name in names:
            for cp in loads[name]:
                cp.start()

    load("code", "temp")

    def loaded(name):
        for cp in loads[name]:
            cp.wait()

    def message(i, s, d, where):
        return pltpu.make_async_remote_copy(
            src_ref=s, dst_ref=d, send_sem=ss.at[i], recv_sem=rs.at[i],
            device_id=dev(where), device_id_type=MESH,
        )

    sent = []

    def send(i, s, d, where):
        m = message(i, s, d, where)
        m.start()
        sent.append(m)
        return m

    row = lax.broadcasted_iota(jnp.int32, (X, W), 0)
    lane = lax.broadcasted_iota(jnp.int32, (X, W), 1)
    zero = jnp.float32(0.0)

    blank = jnp.zeros((2, X, W), jnp.float32)
    for edge in (0, L + 1):
        rk[:, edge], temp[:, edge], stress[:, edge] = blank + 1.0, blank, blank

    loaded("code")
    load("src")

    def tables(i, _):
        for h in (0, 1):
            c = code[h, pl.ds(i * 2, 2)]
            rk[h, pl.ds(i * 2 + 1, 2)] = lookup(c, half_resistance)
            cap[h, pl.ds(i * 2, 2)] = lookup(c, capacities)
        return 0

    loop(L // 2, tables, 0, 4)

    def pack_rows(ref, dst, side, off):
        r = 0 if side == 0 else X - 1
        n = ref.shape[1]
        view = ref.reshape(2, n * X, W)
        for h in (0, 1):
            dst[h] = view[h, pl.ds(off * X + r, L, stride=X), :]

    def pack_columns(*items):
        def body(l, acc):
            shift = lax.rem(l + 1 - f, W)
            return tuple(
                jnp.where(lane == l, pltpu.roll(ref[1 - f, l + off], shift, axis=1), old)
                for old, (ref, off, _) in zip(acc, items)
            )

        z = jnp.zeros((X, W), jnp.float32)
        for value, (_, _, dst) in zip(loop(L, body, (z,) * len(items), L), items):
            dst[...] = value

    loaded("temp")
    load("flag", "imp", "cre", "har")
    for side in (0, 1):
        pack_rows(rk, sx.at[side, 0], side, 1)
        pack_rows(temp, sx.at[side, 1], side, 1)
    pl.semaphore_wait(barrier, len(peers))
    start = [
        send(M_START, sx.at[1], xs.at[0], up),
        send(M_START + 1, sx.at[0], xs.at[1], down),
    ]
    to_below = send(M_RZ, rk.at[:, L], rz, others[0])
    pack_columns((rk, 1, sy.at[0]), (temp, 1, sy.at[1]))
    start.append(send(M_START + 2, sy, ys, mate))

    def x_shifts(ref, h, l):
        return shifted(ref, h, l, -1), shifted(ref, h, l, 1)

    def column_of(hy, l):
        v = pltpu.roll(hy[...], lax.rem(W - l, W), axis=1)
        return jnp.broadcast_to(v[:, 0:1], (X, W))

    def y_shifts(v0, v1, edges=None):
        r0, r1 = pltpu.roll(v0, 1, axis=1), pltpu.roll(v1, 1, axis=1)
        q0, q1 = pltpu.roll(v0, W - 1, axis=1), pltpu.roll(v1, W - 1, axis=1)
        m1, p0 = jnp.where(lane == 0, r0, r1), jnp.where(lane == W - 1, q1, q0)
        if edges is None:
            return (r0, p0), (m1, q1)
        return (
            (jnp.where(lane == 0, edges[0], r0), p0),
            (m1, jnp.where(lane == W - 1, edges[1], q1)),
        )

    lat = jnp.float32(LAT)
    sxm = jnp.where(row == 0, zero, lat)
    sxp = jnp.where(row == X - 1, zero, lat)
    sym = (jnp.where(lane == 0, zero, lat), lat)
    syp = (lat, jnp.where(lane == W - 1, zero, lat))

    def lateral(l):
        kc = (rk[0, l + 1], rk[1, l + 1])
        ysh = y_shifts(kc[0], kc[1])
        for h in (0, 1):
            km, kp = x_shifts(rk, h, l)
            a = sxm * rcp(kc[h] + km)
            b = sxp * rcp(kc[h] + kp)
            c = sym[h] * rcp(kc[h] + ysh[h][0])
            d = syp[h] * rcp(kc[h] + ysh[h][1])
            gxm[h, l], gxp[h, l], gym[h, l], gyp[h, l] = a, b, c, d
            c0[h, l] = cap[h, l] - ((a + b) + (c + d))

    one = jnp.ones((2, X, W), jnp.float32)
    top_cap = cap[:, 0] + jnp.where(k == 0, jnp.float32(H_CONV), zero)
    bottom_cap = cap[:, L - 1] + jnp.where(k == ns - 1, jnp.float32(H_CONV), zero)

    def eliminate(i, carry):
        dt, nt, wt, db, nb, wb = carry
        m = L - 1 - i
        g = rcp(rk[:, i + 1] + rk[:, i + 2])
        dn = g * dt + nt
        nn = cap[:, i + 1] * dn + g * nt
        ipv = dt * rcp(dn)
        e = g * ipv
        ip[:, i] = ipv
        el[:, i] = e
        us[:, i] = ipv * wt
        gb = rcp(rk[:, m + 1] + rk[:, m])
        dbn = gb * db + nb
        nbn = cap[:, m - 1] * dbn + gb * nb
        ipb = db * rcp(dbn)
        eb = gb * ipb
        ip[:, m] = ipb
        el[:, m] = eb
        vs[:, m] = ipb * wb
        lateral(i)
        lateral(m)
        return dn, nn, e * wt, dbn, nbn, eb * wb

    dt, nt, wt, db, nb, wb = loop(
        HALF - 1, eliminate, (one, top_cap, one, one, bottom_cap, one), 4
    )
    st, sb = nt * rcp(dt), nb * rcp(db)
    gm = rcp(rk[:, HALF] + rk[:, HALF + 1])
    idet = rcp(st * sb + gm * (st + sb))
    m11, m12, m22 = (sb + gm) * idet, gm * idet, (st + gm) * idet
    mid[0], mid[1], mid[2] = m11, m12, m22
    ut, ub, vt, vb = m11 * wt, m12 * wt, m12 * wb, m22 * wb
    us[:, HALF - 1], us[:, HALF], vs[:, HALF - 1], vs[:, HALF] = ut, ub, vt, vb

    def spikes(i, carry):
        ut, ub, vt, vb = carry
        l, m = HALF - 2 - i, HALF + 1 + i
        e, eb = el[:, l], el[:, m]
        ut = us[:, l] + e * ut
        vt = e * vt
        ub = eb * ub
        vb = vs[:, m] + eb * vb
        us[:, l], vs[:, l], us[:, m], vs[:, m] = ut, vt, ub, vb
        return ut, ub, vt, vb

    lateral(HALF - 1)
    lateral(HALF)
    ut, ub, vt, vb = loop(HALF - 1, spikes, (ut, ub, vt, vb), 8)
    to_below.wait_recv()
    planes[k, 0] = ut + rz[...] + rk[:, 1]
    planes[k, 1] = vb
    planes[k, 2] = ub
    spread = [
        send(M_S + o, planes.at[k], planes.at[k], others[o]) for o in range(3)
    ]

    eight = lax.broadcasted_iota(jnp.int32, (8, W), 0)

    def tile(rows_):
        out = jnp.zeros((8, W), jnp.float32)
        for i, r in enumerate(rows_):
            out = jnp.where(eight == i, r, out)
        return out

    def send_rows(first, out, into):
        return [
            send(first + 4 * side + o, out.at[side], into.at[1 - side, k], aside[side][o])
            for side in (0, 1) for o in range(4)
        ]

    for side, r in ((0, 0), (1, X - 1)):
        gs_out[side] = tile([planes[k, i, h, r : r + 1, :] for i in range(3) for h in (0, 1)])
    spread += send_rows(M_GS, gs_out, gs)

    for side in (0, 1):
        pack_rows(us, uvx.at[side, 0], side, 0)
        pack_rows(vs, uvx.at[side, 1], side, 0)
    pack_columns((us, 0, uvy.at[0]), (vs, 0, uvy.at[1]))
    uv = [
        send(M_UV, uvx.at[1], uvxr.at[0], up),
        send(M_UV + 1, uvx.at[0], uvxr.at[1], down),
        send(M_UV + 2, uvy, uvyr, mate),
    ]

    def right_side():
        def body(l, carry):
            bf, bl = carry
            tc = (temp[0, l + 1], temp[1, l + 1])
            ysh = y_shifts(tc[0], tc[1])
            nf, nl = [], []
            for h in (0, 1):
                tm, tp = x_shifts(temp, h, l)
                d = (c0[h, l] * tc[h] + src[h, l]) + (
                    (gxm[h, l] * tm + gxp[h, l] * tp)
                    + (gym[h, l] * ysh[h][0] + gyp[h, l] * ysh[h][1])
                )
                rhs[h, l] = d
                nf.append(bf[h] + us[h, l] * d)
                nl.append(bl[h] + vs[h, l] * d)
            return tuple(nf), tuple(nl)

        z = jnp.zeros((X, W), jnp.float32)
        return loop(L, body, ((z, z), (z, z)), 16)

    def side_row(ref, s, h, off):
        view = ref.reshape(2, ref.shape[1] * X, W)
        return view[h, pl.ds(off * X + (0 if s == 0 else X - 1), L, stride=X), :]

    edge_lane = (W - 1) * (1 - f)
    edge_masks = ((lane == 0) & last_col, (lane == W - 1) & first_col)

    def add_column():
        def body(l, _):
            hy = column_of(dy, l)
            rhs[1 - f, l] = rhs[1 - f, l] + jnp.where(lane == edge_lane, hy, zero)
            return 0

        loop(L, body, 0, 8)

    def edge_column(q, j, shift):
        return jnp.broadcast_to(pltpu.roll(q[j], shift, axis=1)[:, 0:1], (X, W))

    def ghost_terms(ghost_rows, ghost_column, own_column, bf, bl):
        d = jnp.where(lane < L, ggy[...] * (ghost_column - own_column), zero)
        dy[...] = d
        sums = [jnp.sum(uvy[j] * d, axis=1, keepdims=True) for j in (0, 1)]
        bf, bl = [
            [old[h] + jnp.where(edge_masks[h], sums[j], zero) for h in (0, 1)]
            for j, old in ((0, bf), (1, bl))
        ]
        nf, nl = [], []
        for h in (0, 1):
            f_sum, l_sum = [], []
            for s in (0, 1):
                d = gg[s, h] * (ghost_rows[s, h] - side_row(temp, s, h, 1))
                dx[s, h] = d
                f_sum.append(jnp.sum(uvx[s, 0, h] * d, axis=0, keepdims=True))
                l_sum.append(jnp.sum(uvx[s, 1, h] * d, axis=0, keepdims=True))
            for out, old, sums in ((nf, bf, f_sum), (nl, bl, l_sum)):
                add = jnp.where(row == 0, sums[0], jnp.where(row == X - 1, sums[1], zero))
                out.append(old[h] + add)
        return nf, nl

    def add_rows(ref, rows_ref):
        view = ref.reshape(2, L * X, W)
        for h in (0, 1):
            for s, r in ((0, 0), (1, X - 1)):
                at = pl.ds(r, L, stride=X)
                view[h, at, :] = view[h, at, :] + rows_ref[s, h]

    def block_solve():
        def forward(i, carry):
            t, b = carry
            m = L - 1 - i
            base[:, i] = ip[:, i] * t
            base[:, m] = ip[:, m] * b
            return rhs[:, i + 1] + el[:, i] * t, rhs[:, m - 1] + el[:, m] * b

        t, b = loop(HALF - 1, forward, (rhs[:, 0], rhs[:, L - 1]), 4)
        t, b = mid[0] * t + mid[1] * b, mid[1] * t + mid[2] * b
        base[:, HALF - 1], base[:, HALF] = t, b

        def backward(i, carry):
            t, b = carry
            l, m = HALF - 2 - i, HALF + 1 + i
            t = base[:, l] + el[:, l] * t
            b = base[:, m] + el[:, m] * b
            base[:, l], base[:, m] = t, b
            return t, b

        loop(HALF - 1, backward, (t, b), 4)

    def solved(i, qt, qb):
        return base[:, i] + (us[:, i] * qt + vs[:, i] * qb)

    def correct(qt, qb):
        def body(i, _):
            temp[:, i + 1] = solved(i, qt, qb)
            return 0

        loop(L, body, 0, 4)

    def creep_tables(i, _):
        for h in (0, 1):
            at = pl.ds(i * 2, 2)
            c = code[h, at]
            md[h, at] = lookup(c, mod_table)
            ex[h, at] = lookup(c, expand_table)
            fl[h, at] = jnp.where(flag[h, at] == 1, jnp.float32(RATE), zero)
        return 0

    def creep_cell(t, c, hd, m, e, im, active):
        load = im - e * t
        s = m * (load - c)
        z = jnp.abs(s) * (rcp(hd) * jnp.float32(0.5 * LOG2E))
        d = jnp.exp2(z - 1.0) - jnp.exp2(-1.0 - z)
        arr = jnp.exp2(jnp.float32(0.5 * LOG2E) * jnp.tanh(0.25 * t + jnp.float32(HALF_LN2)))
        rate = (active * arr) * d
        q = jnp.exp2(jnp.float32(-0.1 * LOG2E) * jnp.log(0.5 + d))
        gap = 1.0 - (0.5 * hd) * q
        size = jnp.abs(gap)
        root = size * lax.rsqrt(jnp.maximum(size, jnp.float32(1e-30)))
        cn = c + jnp.where(s < 0.0, -rate, rate)
        return cn, hd + (gap * root) * rate, m * (load - cn)

    state = (cre, har, md, ex, imp, fl)

    def creep():
        def body(i, _):
            cre[:, i], har[:, i], _s = creep_cell(temp[:, i + 1], *[a[:, i] for a in state])
            return 0

        loop(L, body, 0, 4)

    def interface_system(part, put):
        a1 = part(0, 1) + part(1, 0)
        a2 = part(1, 1) + part(2, 0)
        a3 = part(2, 1) + part(3, 0)
        b1, b2 = part(1, 2), part(2, 2)
        d12 = a1 * a2 - b1 * b1
        idet = rcp(d12 * a3 - a1 * (b2 * b2))
        v11, v12, v13 = (a2 * a3 - b2 * b2) * idet, b1 * a3 * idet, b1 * b2 * idet
        v22, v23, v33 = a1 * a3 * idet, a1 * b2 * idet, d12 * idet
        table = ((v11, v12, v13), (v12, v22, v23), (v13, v23, v33))
        for j in range(3):
            for r, sign in ((0, 1.0), (1, -1.0)):
                at = k + r
                v = jnp.where(
                    at == 1, table[0][j],
                    jnp.where(at == 2, table[1][j], jnp.where(at == 3, table[2][j], zero)),
                )
                put(r, j, v * sign)

    loaded("src")
    for n in range(TSTEPS):
        bf, bl = right_side()
        if n == 0:
            for m in start:
                m.wait_recv()
            for s in (0, 1):
                wide = jnp.where(p == (0 if s == 0 else np_ - 1), zero, lat)
                for h in (0, 1):
                    gg[s, h] = wide * rcp(sx[s, 0, h] + xs[s, 0, h])
            ggy[...] = jnp.where(lane < L, lat * rcp(sy[0] + ys[0]), zero)
            bf, bl = ghost_terms(xs.at[:, 1], ys[1], sy[1], bf, bl)
        else:
            if n == 1:
                for m in uv:
                    m.wait_recv()
            for m in bases + beside_flux + ghost_ends:
                m.wait_recv()
            for side in (0, 1):
                d = [ga[n - 1, side, j, 2:4, :] - ga[n - 1, side, j + 1, 0:2, :] for j in range(3)]
                qg = [
                    gred[side, r, 0, 0:2, :] * d[0] + gred[side, r, 1, 0:2, :] * d[1]
                    + gred[side, r, 2, 0:2, :] * d[2]
                    for r in (0, 1)
                ]
                for h in (0, 1):
                    ghost[side, h] = bxr[n - 1, side, h] + (
                        uvxr[side, 0, h] * qg[0][h : h + 1, :] + uvxr[side, 1, h] * qg[1][h : h + 1, :]
                    )
            far = [edge_column(qy.at[n - 1], j, f) for j in (0, 1)]
            near = [edge_column(qbuf.at[n - 1, :, 1 - f], j, 1 - f) for j in (0, 1)]
            bf, bl = ghost_terms(
                ghost,
                byr[n - 1] + (uvyr[0] * far[0] + uvyr[1] * far[1]),
                by[n - 1] + (uvy[0] * near[0] + uvy[1] * near[1]),
                bf, bl,
            )
        for h in (0, 1):
            abuf[n, k, 0, h] = bf[h]
            abuf[n, k, 1, h] = bl[h]
        ends = [
            send(M_A + 3 * n + o, abuf.at[n, k], abuf.at[n, k], others[o]) for o in range(3)
        ]
        more = n < TSTEPS - 1
        if more:
            for side, r in ((0, 0), (1, X - 1)):
                ga_out[n, side] = tile([v[h][r : r + 1, :] for v in (bf, bl) for h in (0, 1)])
            ghost_ends = send_rows(M_GA + 8 * n, ga_out.at[n], ga.at[n])
        add_rows(rhs, dx)
        add_column()
        block_solve()
        if more:
            for side in (0, 1):
                pack_rows(base, bx.at[n, side], side, 0)
            pack_columns((base, 0, by.at[n]))
            bases = [
                send(M_B + 3 * n, bx.at[n, 1], bxr.at[n, 0], up),
                send(M_B + 3 * n + 1, bx.at[n, 0], bxr.at[n, 1], down),
                send(M_B + 3 * n + 2, by.at[n], byr.at[n], mate),
            ]
        if n == 0:
            loaded("flag")
            loop(L // 2, creep_tables, 0, 2)
            loaded("imp")
            pack_columns((md, 0, pc.at[2]), (ex, 0, pc.at[3]))
            pack_columns((imp, 0, pc.at[4]), (fl, 0, pc.at[5]))
            for m in spread:
                m.wait_recv()
            interface_system(
                lambda j, i: planes[j, i], lambda r, j, v: red.__setitem__((r, j), v)
            )
            for side in (0, 1):
                interface_system(
                    lambda j, i, side=side: gs[side, j, 2 * i : 2 * i + 2, :],
                    lambda r, j, v, side=side: gred.__setitem__((side, r, j, slice(0, 2)), v),
                )
        else:
            if n == 1:
                for name in ("cre", "har"):
                    loaded(name)
            creep()
            if not more:
                pack_columns((base, 0, pc.at[6]), (cre, 0, pc.at[0]), (har, 0, pc.at[1]))
        for m in ends:
            m.wait_recv()
        r = [abuf[n, j, 1] - abuf[n, j + 1, 0] for j in range(3)]
        qt, qb = [
            red[s, 0] * r[0] + red[s, 1] * r[1] + red[s, 2] * r[2] for s in (0, 1)
        ]
        if more:
            qbuf[n, 0], qbuf[n, 1] = qt, qb
            beside_flux = [send(M_C + 3 * n + 2, qbuf.at[n, :, 1 - f], qy.at[n], mate)]
        if more:
            correct(qt, qb)

    qend[0], qend[1] = qt, qb
    for s, r in ((0, 0), (1, X - 1)):
        for h in (0, 1):
            t = side_row(base, s, h, 0) + (
                uvx[s, 0, h] * qend[0, h, r : r + 1, :] + uvx[s, 1, h] * qend[1, h, r : r + 1, :]
            )
            fx[s, h] = creep_cell(t, *[side_row(a, s, h, 0) for a in state])[2]
    for j, l in ((0, 0), (1, L - 1)):
        zs[j] = creep_cell(solved(l, qt, qb), *[a[:, l] for a in state])[2]
    edges = [
        send(M_F, fx.at[1], fxr.at[0], up),
        send(M_F + 1, fx.at[0], fxr.at[1], down),
        send(M_F + 3, zs.at[1], zm, others[0]),
        send(M_F + 4, zs.at[0], zp, others[2]),
    ]
    col = [
        jnp.broadcast_to(pltpu.roll(qend[j, 1 - f], 1 - f, axis=1)[:, 0:1], (X, W)) for j in (0, 1)
    ]
    tc = pc[6] + (uvy[0] * col[0] + uvy[1] * col[1])
    used = jnp.where(lane < L, pc[1], jnp.float32(1.0))
    fy[...] = creep_cell(tc, pc[0], used, *[pc[2 + j] for j in range(4)])[2]
    beside = send(M_F + 2, fy, fyr, mate)

    lag = 16

    def last_creep(i):
        t = solved(i, qt, qb)
        t_end[:, i] = t
        cre[:, i], har[:, i], stress[:, i + 1] = creep_cell(t, *[a[:, i] for a in state])

    def residual(l):
        hy = column_of(fyr, l)
        sc = (stress[0, l + 1], stress[1, l + 1])
        ysh = y_shifts(
            sc[0], sc[1], (jnp.where(first_col, zero, hy), jnp.where(last_col, zero, hy))
        )
        for h in (0, 1):
            sm, sp = x_shifts(stress, h, l)
            sm, sp = jnp.where(row == 0, zero, sm), jnp.where(row == X - 1, zero, sp)
            rhs[h, l] = (
                ((stress[h, l + 2] + stress[h, l]) + (sm + sp))
                + (ysh[h][0] + ysh[h][1])
            ) - 6.0 * sc[h]

    def first_layers(i, _):
        last_creep(i)
        return 0

    def both(i, _):
        last_creep(i + lag)
        residual(i)
        return 0

    def last_layers(i, _):
        residual(i + L - lag)
        return 0

    loop(lag, first_layers, 0, 4)
    beside.wait_recv()
    loop(L - lag, both, 0, 6)
    loop(lag, last_layers, 0, 8)
    for m in edges:
        m.wait_recv()
    rhs[:, 0] = rhs[:, 0] + jnp.where(k == 0, zero, zm[...])
    rhs[:, L - 1] = rhs[:, L - 1] + jnp.where(k == ns - 1, zero, zp[...])
    ghost[0] = jnp.where(p == 0, zero, fxr[0])
    ghost[1] = jnp.where(p == np_ - 1, zero, fxr[1])
    add_rows(rhs, ghost)
    for m in sent:
        m.wait_send()


def write_out(temp, cre, har, res, t_out, c_out, h_out, s_out, sem):
    copies = []
    for i, (vm, hbm) in enumerate(
        ((temp, t_out), (cre, c_out), (har, h_out), (res, s_out))
    ):
        for h in (0, 1):
            copies.append(pltpu.make_async_copy(
                vm.at[h], hbm.at[:, :, pl.ds(W * h, W)], sem.at[i, h]
            ))
    for cp in copies:
        cp.start()
    for cp in copies:
        cp.wait()


def per_device(*args):
    f32 = jnp.float32
    block = (2, L, X, W)
    tall = (2, L + 2, X, W)

    def vm(*shape):
        return pltpu.VMEM(shape, f32)

    scratch = [
        pltpu.VMEM(block, jnp.int32), pltpu.VMEM(block, jnp.int32), vm(*tall),
        vm(*block), vm(*block),
        vm(*tall),
        *[vm(*block) for _ in range(14)],
        vm(*tall),
        vm(3, 2, X, W), vm(2, 3, 2, X, W),
        vm(4, 3, 2, X, W), vm(TSTEPS, 4, 2, 2, X, W), vm(2, 2, 2, X, W),
        vm(2, 2, 2, L, W), vm(2, X, W), vm(2, 2, 2, L, W), vm(2, X, W),
        vm(2, X, W),
        vm(2, 2, 2, L, W), vm(2, X, W), vm(2, 2, 2, L, W), vm(2, X, W),
        vm(2, 2, 2, L, W), vm(2, X, W), vm(2, 2, 2, L, W), vm(2, X, W),
        vm(2, 2, X, W),
        vm(2, 2, L, W),
        vm(2, 2, L, W), vm(X, W), vm(2, 2, L, W), vm(X, W),
        vm(2, 2, X, W), vm(2, X, W), vm(2, X, W),
        vm(2, 2, L, W), vm(2, 2, L, W),
        vm(7, X, W), vm(2, 2, X, W),
        vm(2, 8, W), vm(2, 4, 8, W), vm(2, 2, 8, W), vm(2, 2, 4, 8, W),
        vm(2, 2, 3, 8, W), vm(X, W), vm(X, W),
        pltpu.SemaphoreType.DMA((7, 2)),
        pltpu.SemaphoreType.DMA((N_MSG,)), pltpu.SemaphoreType.DMA((N_MSG,)),
    ]
    shape = args[0].shape
    results = pl.pallas_call(
        kernel,
        out_shape=[jax.ShapeDtypeStruct(s, f32) for s in (block,) * 4],
        in_specs=[pl.BlockSpec(memory_space=pltpu.HBM)] * 7,
        out_specs=[pl.BlockSpec(memory_space=pltpu.VMEM)] * 4,
        scratch_shapes=scratch,
        compiler_params=pltpu.CompilerParams(
            collective_id=0, has_side_effects=True, vmem_limit_bytes=49 << 20
        ),
        name="thermal_creep_step",
    )(*args)
    return pl.pallas_call(
        write_out,
        out_shape=[jax.ShapeDtypeStruct(shape, f32)] * 4,
        in_specs=[pl.BlockSpec(memory_space=pltpu.VMEM)] * 4,
        out_specs=[pl.BlockSpec(memory_space=pltpu.HBM)] * 4,
        scratch_shapes=[pltpu.SemaphoreType.DMA((4, 2))],
        compiler_params=pltpu.CompilerParams(vmem_limit_bytes=16 << 20),
        name="write_out",
    )(*results)


def solution(mesh):
    spec = P("stack", "plane", "phys")
    return jax.shard_map(
        per_device, mesh=mesh, in_specs=(spec,) * 7, out_specs=(spec,) * 4, check_vma=False
    )
```

```python
import functools

import jax
import jax.numpy as jnp
from jax import lax
from jax.experimental import pallas as pl
from jax.experimental.pallas import tpu as pltpu
from jax.sharding import PartitionSpec as P

MESH = pl.DeviceIdType.MESH
TSTEPS = 3
L, X, W = 64, 16, 128
HALF = L // 2

k_table = (4.0, 0.6, 2.5, 1.2, 0.8)
cap_table = (1.6, 1.8, 1.7, 2.0, 1.9)
mod_table = (1.5, 0.6, 0.9, 1.2, 0.8)
expand_table = (0.1, 0.3, 0.25, 0.15, 0.2)
half_resistance = tuple(0.5 / k for k in k_table)
capacities = tuple(0.0003 * c for c in cap_table)
LAT = 1.2e-05
H_CONV = 0.05
LOG2E = 1.4426950408889634
HALF_LN2 = 0.34657359027997264
RATE = 0.05 * 0.22313016014842982

M_START, M_RZ, M_S, M_UV, M_A, M_B, M_C, M_F = 0, 3, 4, 7, 10, 19, 25, 31
M_GS, M_GA = 36, 44
N_MSG = 60


def rcp(x):
    return pl.reciprocal(x)


def lookup(c, t):
    low = jnp.where(c < 1, jnp.float32(t[0]), jnp.float32(t[1]))
    top = jnp.where(c < 4, jnp.float32(t[3]), jnp.float32(t[4]))
    return jnp.where(c < 2, low, jnp.where(c < 3, jnp.float32(t[2]), top))


def flat(ref):
    return ref.reshape(2, (L + 2) * X, W)


def shifted(ref, h, l, off):
    return flat(ref)[h, pl.ds(l * X + X + off, X), :]


def loop(n, body, carry, unroll):
    return lax.fori_loop(0, n, body, carry, unroll=unroll)


def kernel(
    t_in, src_in, code_in, flag_in, imp_in, cre_in, har_in,
    t_end, cre, har, rhs,
    code, flag, temp, src, imp,
    rk, cap, ip, el, us, vs, gxm, gxp, gym, gyp, c0, base, md, ex, fl, stress,
    mid, red, planes, abuf, qbuf,
    sx, sy, xs, ys, rz, uvx, uvy, uvxr, uvyr, bx, by, bxr, byr, qy,
    ghost, fx, fy, fxr, fyr, zs, zm, zp, gg, dx, pc, qend,
    gs_out, gs, ga_out, ga, gred, ggy, dy,
    in_sem, ss, rs,
):
    k = lax.axis_index("stack")
    p = lax.axis_index("plane")
    f = lax.axis_index("phys")
    ns, np_ = 4, 32
    up = {"plane": lax.rem(p + 1, np_)}
    down = {"plane": lax.rem(p + np_ - 1, np_)}
    mate = {"phys": 1 - f}
    others = [{"stack": lax.rem(k + o, ns)} for o in (1, 2, 3)]
    first_col, last_col = f == 0, f == 1

    def dev(where):
        return (where.get("stack", k), where.get("plane", p), where.get("phys", f))

    barrier = pltpu.get_barrier_semaphore()
    aside = [
        [{"stack": lax.rem(k + o, ns), **side} for o in range(4)] for side in (down, up)
    ]
    peers = [mate] + others + aside[0] + aside[1]
    for w in peers:
        pl.semaphore_signal(barrier, inc=1, device_id=dev(w), device_id_type=MESH)

    loads = {}
    for i, (name, hbm, vm, off) in enumerate((
        ("code", code_in, code, 0), ("temp", t_in, temp, 1), ("src", src_in, src, 0),
        ("flag", flag_in, flag, 0), ("imp", imp_in, imp, 0), ("cre", cre_in, cre, 0),
        ("har", har_in, har, 0),
    )):
        loads[name] = []
        for h in (0, 1):
            cp = pltpu.make_async_copy(
                hbm.at[:, :, pl.ds(W * h, W)], vm.at[h, pl.ds(off, L)], in_sem.at[i, h]
            )
            loads[name].append(cp)

    def load(*names):
        for name in names:
            for cp in loads[name]:
                cp.start()

    load("code", "temp")

    def loaded(name):
        for cp in loads[name]:
            cp.wait()

    def message(i, s, d, where):
        return pltpu.make_async_remote_copy(
            src_ref=s, dst_ref=d, send_sem=ss.at[i], recv_sem=rs.at[i],
            device_id=dev(where), device_id_type=MESH,
        )

    sent = []

    def send(i, s, d, where):
        m = message(i, s, d, where)
        m.start()
        sent.append(m)
        return m

    row = lax.broadcasted_iota(jnp.int32, (X, W), 0)
    lane = lax.broadcasted_iota(jnp.int32, (X, W), 1)
    zero = jnp.float32(0.0)

    blank = jnp.zeros((2, X, W), jnp.float32)
    for edge in (0, L + 1):
        rk[:, edge], temp[:, edge], stress[:, edge] = blank + 1.0, blank, blank

    loaded("code")
    load("src")

    def tables(i, _):
        for h in (0, 1):
            c = code[h, pl.ds(i * 2, 2)]
            rk[h, pl.ds(i * 2 + 1, 2)] = lookup(c, half_resistance)
            cap[h, pl.ds(i * 2, 2)] = lookup(c, capacities)
        return 0

    loop(L // 2, tables, 0, 4)

    def pack_rows(ref, dst, side, off):
        r = 0 if side == 0 else X - 1
        n = ref.shape[1]
        view = ref.reshape(2, n * X, W)
        for h in (0, 1):
            dst[h] = view[h, pl.ds(off * X + r, L, stride=X), :]

    def pack_columns(*items):
        def body(l, acc):
            shift = lax.rem(l + 1 - f, W)
            return tuple(
                jnp.where(lane == l, pltpu.roll(ref[1 - f, l + off], shift, axis=1), old)
                for old, (ref, off, _) in zip(acc, items)
            )

        z = jnp.zeros((X, W), jnp.float32)
        for value, (_, _, dst) in zip(loop(L, body, (z,) * len(items), L), items):
            dst[...] = value

    loaded("temp")
    load("flag", "imp", "cre", "har")
    for side in (0, 1):
        pack_rows(rk, sx.at[side, 0], side, 1)
        pack_rows(temp, sx.at[side, 1], side, 1)
    pl.semaphore_wait(barrier, len(peers))
    start = [
        send(M_START, sx.at[1], xs.at[0], up),
        send(M_START + 1, sx.at[0], xs.at[1], down),
    ]
    to_below = send(M_RZ, rk.at[:, L], rz, others[0])
    pack_columns((rk, 1, sy.at[0]), (temp, 1, sy.at[1]))
    start.append(send(M_START + 2, sy, ys, mate))

    def x_shifts(ref, h, l):
        return shifted(ref, h, l, -1), shifted(ref, h, l, 1)

    def column_of(hy, l):
        v = pltpu.roll(hy[...], lax.rem(W - l, W), axis=1)
        return jnp.broadcast_to(v[:, 0:1], (X, W))

    def y_shifts(v0, v1, edges=None):
        r0, r1 = pltpu.roll(v0, 1, axis=1), pltpu.roll(v1, 1, axis=1)
        q0, q1 = pltpu.roll(v0, W - 1, axis=1), pltpu.roll(v1, W - 1, axis=1)
        m1, p0 = jnp.where(lane == 0, r0, r1), jnp.where(lane == W - 1, q1, q0)
        if edges is None:
            return (r0, p0), (m1, q1)
        return (
            (jnp.where(lane == 0, edges[0], r0), p0),
            (m1, jnp.where(lane == W - 1, edges[1], q1)),
        )

    lat = jnp.float32(LAT)
    sxm = jnp.where(row == 0, zero, lat)
    sxp = jnp.where(row == X - 1, zero, lat)
    sym = (jnp.where(lane == 0, zero, lat), lat)
    syp = (lat, jnp.where(lane == W - 1, zero, lat))

    def lateral(l):
        kc = (rk[0, l + 1], rk[1, l + 1])
        ysh = y_shifts(kc[0], kc[1])
        for h in (0, 1):
            km, kp = x_shifts(rk, h, l)
            a = sxm * rcp(kc[h] + km)
            b = sxp * rcp(kc[h] + kp)
            c = sym[h] * rcp(kc[h] + ysh[h][0])
            d = syp[h] * rcp(kc[h] + ysh[h][1])
            gxm[h, l], gxp[h, l], gym[h, l], gyp[h, l] = a, b, c, d
            c0[h, l] = cap[h, l] - ((a + b) + (c + d))

    one = jnp.ones((2, X, W), jnp.float32)
    top_cap = cap[:, 0] + jnp.where(k == 0, jnp.float32(H_CONV), zero)
    bottom_cap = cap[:, L - 1] + jnp.where(k == ns - 1, jnp.float32(H_CONV), zero)

    def eliminate(i, carry):
        dt, nt, wt, db, nb, wb = carry
        m = L - 1 - i
        g = rcp(rk[:, i + 1] + rk[:, i + 2])
        dn = g * dt + nt
        nn = cap[:, i + 1] * dn + g * nt
        ipv = dt * rcp(dn)
        e = g * ipv
        ip[:, i] = ipv
        el[:, i] = e
        us[:, i] = ipv * wt
        gb = rcp(rk[:, m + 1] + rk[:, m])
        dbn = gb * db + nb
        nbn = cap[:, m - 1] * dbn + gb * nb
        ipb = db * rcp(dbn)
        eb = gb * ipb
        ip[:, m] = ipb
        el[:, m] = eb
        vs[:, m] = ipb * wb
        lateral(i)
        lateral(m)
        return dn, nn, e * wt, dbn, nbn, eb * wb

    dt, nt, wt, db, nb, wb = loop(
        HALF - 1, eliminate, (one, top_cap, one, one, bottom_cap, one), 4
    )
    st, sb = nt * rcp(dt), nb * rcp(db)
    gm = rcp(rk[:, HALF] + rk[:, HALF + 1])
    idet = rcp(st * sb + gm * (st + sb))
    m11, m12, m22 = (sb + gm) * idet, gm * idet, (st + gm) * idet
    mid[0], mid[1], mid[2] = m11, m12, m22
    ut, ub, vt, vb = m11 * wt, m12 * wt, m12 * wb, m22 * wb
    us[:, HALF - 1], us[:, HALF], vs[:, HALF - 1], vs[:, HALF] = ut, ub, vt, vb

    def spikes(i, carry):
        ut, ub, vt, vb = carry
        l, m = HALF - 2 - i, HALF + 1 + i
        e, eb = el[:, l], el[:, m]
        ut = us[:, l] + e * ut
        vt = e * vt
        ub = eb * ub
        vb = vs[:, m] + eb * vb
        us[:, l], vs[:, l], us[:, m], vs[:, m] = ut, vt, ub, vb
        return ut, ub, vt, vb

    lateral(HALF - 1)
    lateral(HALF)
    ut, ub, vt, vb = loop(HALF - 1, spikes, (ut, ub, vt, vb), 8)
    to_below.wait_recv()
    planes[k, 0] = ut + rz[...] + rk[:, 1]
    planes[k, 1] = vb
    planes[k, 2] = ub
    spread = [
        send(M_S + o, planes.at[k], planes.at[k], others[o]) for o in range(3)
    ]

    eight = lax.broadcasted_iota(jnp.int32, (8, W), 0)

    def tile(rows_):
        out = jnp.zeros((8, W), jnp.float32)
        for i, r in enumerate(rows_):
            out = jnp.where(eight == i, r, out)
        return out

    def send_rows(first, out, into):
        return [
            send(first + 4 * side + o, out.at[side], into.at[1 - side, k], aside[side][o])
            for side in (0, 1) for o in range(4)
        ]

    for side, r in ((0, 0), (1, X - 1)):
        gs_out[side] = tile([planes[k, i, h, r : r + 1, :] for i in range(3) for h in (0, 1)])
    spread += send_rows(M_GS, gs_out, gs)

    for side in (0, 1):
        pack_rows(us, uvx.at[side, 0], side, 0)
        pack_rows(vs, uvx.at[side, 1], side, 0)
    pack_columns((us, 0, uvy.at[0]), (vs, 0, uvy.at[1]))
    uv = [
        send(M_UV, uvx.at[1], uvxr.at[0], up),
        send(M_UV + 1, uvx.at[0], uvxr.at[1], down),
        send(M_UV + 2, uvy, uvyr, mate),
    ]

    def right_side():
        def body(l, carry):
            bf, bl = carry
            tc = (temp[0, l + 1], temp[1, l + 1])
            ysh = y_shifts(tc[0], tc[1])
            nf, nl = [], []
            for h in (0, 1):
                tm, tp = x_shifts(temp, h, l)
                d = (c0[h, l] * tc[h] + src[h, l]) + (
                    (gxm[h, l] * tm + gxp[h, l] * tp)
                    + (gym[h, l] * ysh[h][0] + gyp[h, l] * ysh[h][1])
                )
                rhs[h, l] = d
                nf.append(bf[h] + us[h, l] * d)
                nl.append(bl[h] + vs[h, l] * d)
            return tuple(nf), tuple(nl)

        z = jnp.zeros((X, W), jnp.float32)
        return loop(L, body, ((z, z), (z, z)), 32)

    def side_row(ref, s, h, off):
        view = ref.reshape(2, ref.shape[1] * X, W)
        return view[h, pl.ds(off * X + (0 if s == 0 else X - 1), L, stride=X), :]

    edge_lane = (W - 1) * (1 - f)
    edge_masks = ((lane == 0) & last_col, (lane == W - 1) & first_col)

    def add_column():
        def body(l, _):
            hy = column_of(dy, l)
            rhs[1 - f, l] = rhs[1 - f, l] + jnp.where(lane == edge_lane, hy, zero)
            return 0

        loop(L, body, 0, 8)

    def edge_column(q, j, shift):
        return jnp.broadcast_to(pltpu.roll(q[j], shift, axis=1)[:, 0:1], (X, W))

    def ghost_terms(ghost_rows, ghost_column, own_column, bf, bl):
        d = jnp.where(lane < L, ggy[...] * (ghost_column - own_column), zero)
        dy[...] = d
        sums = [jnp.sum(uvy[j] * d, axis=1, keepdims=True) for j in (0, 1)]
        bf, bl = [
            [old[h] + jnp.where(edge_masks[h], sums[j], zero) for h in (0, 1)]
            for j, old in ((0, bf), (1, bl))
        ]
        nf, nl = [], []
        for h in (0, 1):
            f_sum, l_sum = [], []
            for s in (0, 1):
                d = gg[s, h] * (ghost_rows[s, h] - side_row(temp, s, h, 1))
                dx[s, h] = d
                f_sum.append(jnp.sum(uvx[s, 0, h] * d, axis=0, keepdims=True))
                l_sum.append(jnp.sum(uvx[s, 1, h] * d, axis=0, keepdims=True))
            for out, old, sums in ((nf, bf, f_sum), (nl, bl, l_sum)):
                add = jnp.where(row == 0, sums[0], jnp.where(row == X - 1, sums[1], zero))
                out.append(old[h] + add)
        return nf, nl

    def add_rows(ref, rows_ref):
        view = ref.reshape(2, L * X, W)
        for h in (0, 1):
            for s, r in ((0, 0), (1, X - 1)):
                at = pl.ds(r, L, stride=X)
                view[h, at, :] = view[h, at, :] + rows_ref[s, h]

    def block_solve():
        def forward(i, carry):
            t, b = carry
            m = L - 1 - i
            base[:, i] = ip[:, i] * t
            base[:, m] = ip[:, m] * b
            return rhs[:, i + 1] + el[:, i] * t, rhs[:, m - 1] + el[:, m] * b

        t, b = loop(HALF - 1, forward, (rhs[:, 0], rhs[:, L - 1]), 4)
        t, b = mid[0] * t + mid[1] * b, mid[1] * t + mid[2] * b
        base[:, HALF - 1], base[:, HALF] = t, b

        def backward(i, carry):
            t, b = carry
            l, m = HALF - 2 - i, HALF + 1 + i
            t = base[:, l] + el[:, l] * t
            b = base[:, m] + el[:, m] * b
            base[:, l], base[:, m] = t, b
            return t, b

        loop(HALF - 1, backward, (t, b), 4)

    def solved(i, qt, qb):
        return base[:, i] + (us[:, i] * qt + vs[:, i] * qb)

    def correct(qt, qb):
        def body(i, _):
            temp[:, i + 1] = solved(i, qt, qb)
            return 0

        loop(L, body, 0, 4)

    def creep_tables(i, _):
        for h in (0, 1):
            at = pl.ds(i * 2, 2)
            c = code[h, at]
            md[h, at] = lookup(c, mod_table)
            ex[h, at] = lookup(c, expand_table)
            fl[h, at] = jnp.where(flag[h, at] == 1, jnp.float32(RATE), zero)
        return 0

    def creep_cell(t, c, hd, m, e, im, active):
        load = im - e * t
        s = m * (load - c)
        z = jnp.abs(s) * (rcp(hd) * jnp.float32(0.5 * LOG2E))
        d = jnp.exp2(z - 1.0) - jnp.exp2(-1.0 - z)
        arr = jnp.exp2(jnp.float32(0.5 * LOG2E) * jnp.tanh(0.25 * t + jnp.float32(HALF_LN2)))
        rate = (active * arr) * d
        q = jnp.exp2(jnp.float32(-0.1 * LOG2E) * jnp.log(0.5 + d))
        gap = 1.0 - (0.5 * hd) * q
        size = jnp.abs(gap)
        root = size * lax.rsqrt(jnp.maximum(size, jnp.float32(1e-30)))
        cn = c + jnp.where(s < 0.0, -rate, rate)
        return cn, hd + (gap * root) * rate, m * (load - cn)

    state = (cre, har, md, ex, imp, fl)

    def creep():
        def body(i, _):
            cre[:, i], har[:, i], _s = creep_cell(temp[:, i + 1], *[a[:, i] for a in state])
            return 0

        loop(L, body, 0, 4)

    def interface_system(part, put):
        a1 = part(0, 1) + part(1, 0)
        a2 = part(1, 1) + part(2, 0)
        a3 = part(2, 1) + part(3, 0)
        b1, b2 = part(1, 2), part(2, 2)
        d12 = a1 * a2 - b1 * b1
        idet = rcp(d12 * a3 - a1 * (b2 * b2))
        v11, v12, v13 = (a2 * a3 - b2 * b2) * idet, b1 * a3 * idet, b1 * b2 * idet
        v22, v23, v33 = a1 * a3 * idet, a1 * b2 * idet, d12 * idet
        table = ((v11, v12, v13), (v12, v22, v23), (v13, v23, v33))
        for j in range(3):
            for r, sign in ((0, 1.0), (1, -1.0)):
                at = k + r
                v = jnp.where(
                    at == 1, table[0][j],
                    jnp.where(at == 2, table[1][j], jnp.where(at == 3, table[2][j], zero)),
                )
                put(r, j, v * sign)

    loaded("src")
    for n in range(TSTEPS):
        bf, bl = right_side()
        if n == 0:
            for m in start:
                m.wait_recv()
            for s in (0, 1):
                wide = jnp.where(p == (0 if s == 0 else np_ - 1), zero, lat)
                for h in (0, 1):
                    gg[s, h] = wide * rcp(sx[s, 0, h] + xs[s, 0, h])
            ggy[...] = jnp.where(lane < L, lat * rcp(sy[0] + ys[0]), zero)
            bf, bl = ghost_terms(xs.at[:, 1], ys[1], sy[1], bf, bl)
        else:
            if n == 1:
                for m in uv:
                    m.wait_recv()
            for m in bases + beside_flux + ghost_ends:
                m.wait_recv()
            for side in (0, 1):
                d = [ga[n - 1, side, j, 2:4, :] - ga[n - 1, side, j + 1, 0:2, :] for j in range(3)]
                qg = [
                    gred[side, r, 0, 0:2, :] * d[0] + gred[side, r, 1, 0:2, :] * d[1]
                    + gred[side, r, 2, 0:2, :] * d[2]
                    for r in (0, 1)
                ]
                for h in (0, 1):
                    ghost[side, h] = bxr[n - 1, side, h] + (
                        uvxr[side, 0, h] * qg[0][h : h + 1, :] + uvxr[side, 1, h] * qg[1][h : h + 1, :]
                    )
            far = [edge_column(qy.at[n - 1], j, f) for j in (0, 1)]
            near = [edge_column(qbuf.at[n - 1, :, 1 - f], j, 1 - f) for j in (0, 1)]
            bf, bl = ghost_terms(
                ghost,
                byr[n - 1] + (uvyr[0] * far[0] + uvyr[1] * far[1]),
                by[n - 1] + (uvy[0] * near[0] + uvy[1] * near[1]),
                bf, bl,
            )
        for h in (0, 1):
            abuf[n, k, 0, h] = bf[h]
            abuf[n, k, 1, h] = bl[h]
        ends = [
            send(M_A + 3 * n + o, abuf.at[n, k], abuf.at[n, k], others[o]) for o in (1, 0, 2)
        ]
        more = n < TSTEPS - 1
        if more:
            for side, r in ((0, 0), (1, X - 1)):
                ga_out[n, side] = tile([v[h][r : r + 1, :] for v in (bf, bl) for h in (0, 1)])
            ghost_ends = send_rows(M_GA + 8 * n, ga_out.at[n], ga.at[n])
        add_rows(rhs, dx)
        add_column()
        block_solve()
        if more:
            for side in (0, 1):
                pack_rows(base, bx.at[n, side], side, 0)
            pack_columns((base, 0, by.at[n]))
            bases = [
                send(M_B + 3 * n, bx.at[n, 1], bxr.at[n, 0], up),
                send(M_B + 3 * n + 1, bx.at[n, 0], bxr.at[n, 1], down),
                send(M_B + 3 * n + 2, by.at[n], byr.at[n], mate),
            ]
        if n == 0:
            loaded("flag")
            loop(L // 2, creep_tables, 0, 2)
            loaded("imp")
            pack_columns((md, 0, pc.at[2]), (ex, 0, pc.at[3]))
            pack_columns((imp, 0, pc.at[4]), (fl, 0, pc.at[5]))
            for m in spread:
                m.wait_recv()
            interface_system(
                lambda j, i: planes[j, i], lambda r, j, v: red.__setitem__((r, j), v)
            )
            for side in (0, 1):
                interface_system(
                    lambda j, i, side=side: gs[side, j, 2 * i : 2 * i + 2, :],
                    lambda r, j, v, side=side: gred.__setitem__((side, r, j, slice(0, 2)), v),
                )
        else:
            if n == 1:
                for name in ("cre", "har"):
                    loaded(name)
            creep()
            if not more:
                pack_columns((base, 0, pc.at[6]), (cre, 0, pc.at[0]), (har, 0, pc.at[1]))
        for m in ends:
            m.wait_recv()
        r = [abuf[n, j, 1] - abuf[n, j + 1, 0] for j in range(3)]
        qt, qb = [
            red[s, 0] * r[0] + red[s, 1] * r[1] + red[s, 2] * r[2] for s in (0, 1)
        ]
        if more:
            qbuf[n, 0], qbuf[n, 1] = qt, qb
            beside_flux = [send(M_C + 3 * n + 2, qbuf.at[n, :, 1 - f], qy.at[n], mate)]
        if more:
            correct(qt, qb)

    qend[0], qend[1] = qt, qb
    for s, r in ((0, 0), (1, X - 1)):
        for h in (0, 1):
            t = side_row(base, s, h, 0) + (
                uvx[s, 0, h] * qend[0, h, r : r + 1, :] + uvx[s, 1, h] * qend[1, h, r : r + 1, :]
            )
            fx[s, h] = creep_cell(t, *[side_row(a, s, h, 0) for a in state])[2]
    for j, l in ((0, 0), (1, L - 1)):
        zs[j] = creep_cell(solved(l, qt, qb), *[a[:, l] for a in state])[2]
    edges = [
        send(M_F, fx.at[1], fxr.at[0], up),
        send(M_F + 1, fx.at[0], fxr.at[1], down),
        send(M_F + 3, zs.at[1], zm, others[0]),
        send(M_F + 4, zs.at[0], zp, others[2]),
    ]
    col = [
        jnp.broadcast_to(pltpu.roll(qend[j, 1 - f], 1 - f, axis=1)[:, 0:1], (X, W)) for j in (0, 1)
    ]
    tc = pc[6] + (uvy[0] * col[0] + uvy[1] * col[1])
    used = jnp.where(lane < L, pc[1], jnp.float32(1.0))
    fy[...] = creep_cell(tc, pc[0], used, *[pc[2 + j] for j in range(4)])[2]
    beside = send(M_F + 2, fy, fyr, mate)

    lag = 16

    def last_creep(i):
        t = solved(i, qt, qb)
        t_end[:, i] = t
        cre[:, i], har[:, i], stress[:, i + 1] = creep_cell(t, *[a[:, i] for a in state])

    def residual(l):
        hy = column_of(fyr, l)
        sc = (stress[0, l + 1], stress[1, l + 1])
        ysh = y_shifts(
            sc[0], sc[1], (jnp.where(first_col, zero, hy), jnp.where(last_col, zero, hy))
        )
        for h in (0, 1):
            sm, sp = x_shifts(stress, h, l)
            sm, sp = jnp.where(row == 0, zero, sm), jnp.where(row == X - 1, zero, sp)
            rhs[h, l] = (
                ((stress[h, l + 2] + stress[h, l]) + (sm + sp))
                + (ysh[h][0] + ysh[h][1])
            ) - 6.0 * sc[h]

    def first_layers(i, _):
        last_creep(i)
        return 0

    def both(i, _):
        last_creep(i + lag)
        residual(i)
        return 0

    def last_layers(i, _):
        residual(i + L - lag)
        return 0

    loop(lag, first_layers, 0, 4)
    beside.wait_recv()
    loop(L - lag, both, 0, 6)
    loop(lag, last_layers, 0, 8)
    for m in edges:
        m.wait_recv()
    rhs[:, 0] = rhs[:, 0] + jnp.where(k == 0, zero, zm[...])
    rhs[:, L - 1] = rhs[:, L - 1] + jnp.where(k == ns - 1, zero, zp[...])
    ghost[0] = jnp.where(p == 0, zero, fxr[0])
    ghost[1] = jnp.where(p == np_ - 1, zero, fxr[1])
    add_rows(rhs, ghost)
    for m in sent:
        m.wait_send()


def write_out(temp, cre, har, res, t_out, c_out, h_out, s_out, sem):
    copies = []
    for i, (vm, hbm) in enumerate(
        ((temp, t_out), (cre, c_out), (har, h_out), (res, s_out))
    ):
        for h in (0, 1):
            copies.append(pltpu.make_async_copy(
                vm.at[h], hbm.at[:, :, pl.ds(W * h, W)], sem.at[i, h]
            ))
    for cp in copies:
        cp.start()
    for cp in copies:
        cp.wait()


def per_device(*args):
    f32 = jnp.float32
    block = (2, L, X, W)
    tall = (2, L + 2, X, W)

    def vm(*shape):
        return pltpu.VMEM(shape, f32)

    scratch = [
        pltpu.VMEM(block, jnp.int32), pltpu.VMEM(block, jnp.int32), vm(*tall),
        vm(*block), vm(*block),
        vm(*tall),
        *[vm(*block) for _ in range(14)],
        vm(*tall),
        vm(3, 2, X, W), vm(2, 3, 2, X, W),
        vm(4, 3, 2, X, W), vm(TSTEPS, 4, 2, 2, X, W), vm(2, 2, 2, X, W),
        vm(2, 2, 2, L, W), vm(2, X, W), vm(2, 2, 2, L, W), vm(2, X, W),
        vm(2, X, W),
        vm(2, 2, 2, L, W), vm(2, X, W), vm(2, 2, 2, L, W), vm(2, X, W),
        vm(2, 2, 2, L, W), vm(2, X, W), vm(2, 2, 2, L, W), vm(2, X, W),
        vm(2, 2, X, W),
        vm(2, 2, L, W),
        vm(2, 2, L, W), vm(X, W), vm(2, 2, L, W), vm(X, W),
        vm(2, 2, X, W), vm(2, X, W), vm(2, X, W),
        vm(2, 2, L, W), vm(2, 2, L, W),
        vm(7, X, W), vm(2, 2, X, W),
        vm(2, 8, W), vm(2, 4, 8, W), vm(2, 2, 8, W), vm(2, 2, 4, 8, W),
        vm(2, 2, 3, 8, W), vm(X, W), vm(X, W),
        pltpu.SemaphoreType.DMA((7, 2)),
        pltpu.SemaphoreType.DMA((N_MSG,)), pltpu.SemaphoreType.DMA((N_MSG,)),
    ]
    shape = args[0].shape
    results = pl.pallas_call(
        kernel,
        out_shape=[jax.ShapeDtypeStruct(s, f32) for s in (block,) * 4],
        in_specs=[pl.BlockSpec(memory_space=pltpu.HBM)] * 7,
        out_specs=[pl.BlockSpec(memory_space=pltpu.VMEM)] * 4,
        scratch_shapes=scratch,
        compiler_params=pltpu.CompilerParams(
            collective_id=0, has_side_effects=True, vmem_limit_bytes=49 << 20
        ),
        name="thermal_creep_step",
    )(*args)
    return pl.pallas_call(
        write_out,
        out_shape=[jax.ShapeDtypeStruct(shape, f32)] * 4,
        in_specs=[pl.BlockSpec(memory_space=pltpu.VMEM)] * 4,
        out_specs=[pl.BlockSpec(memory_space=pltpu.HBM)] * 4,
        scratch_shapes=[pltpu.SemaphoreType.DMA((4, 2))],
        compiler_params=pltpu.CompilerParams(vmem_limit_bytes=16 << 20),
        name="write_out",
    )(*results)


def solution(mesh):
    spec = P("stack", "plane", "phys")
    return jax.shard_map(
        per_device, mesh=mesh, in_specs=(spec,) * 7, out_specs=(spec,) * 4, check_vma=False
    )
```

```python
import functools

import jax
import jax.numpy as jnp
from jax import lax
from jax.experimental import pallas as pl
from jax.experimental.pallas import tpu as pltpu
from jax.sharding import PartitionSpec as P

MESH = pl.DeviceIdType.MESH
TSTEPS = 3
L, X, W = 64, 16, 128
HALF = L // 2

k_table = (4.0, 0.6, 2.5, 1.2, 0.8)
cap_table = (1.6, 1.8, 1.7, 2.0, 1.9)
mod_table = (1.5, 0.6, 0.9, 1.2, 0.8)
expand_table = (0.1, 0.3, 0.25, 0.15, 0.2)
half_resistance = tuple(0.5 / k for k in k_table)
capacities = tuple(0.0003 * c for c in cap_table)
LAT = 1.2e-05
H_CONV = 0.05
LOG2E = 1.4426950408889634
HALF_LN2 = 0.34657359027997264
RATE = 0.05 * 0.22313016014842982

M_START, M_RZ, M_S, M_UV, M_A, M_B, M_C, M_F = 0, 3, 4, 7, 10, 19, 25, 31
M_GS, M_GA = 36, 44
N_MSG = 60


def rcp(x):
    return pl.reciprocal(x)


def lookup(c, t):
    low = jnp.where(c < 1, jnp.float32(t[0]), jnp.float32(t[1]))
    top = jnp.where(c < 4, jnp.float32(t[3]), jnp.float32(t[4]))
    return jnp.where(c < 2, low, jnp.where(c < 3, jnp.float32(t[2]), top))


def flat(ref):
    return ref.reshape(2, (L + 2) * X, W)


def shifted(ref, h, l, off):
    return flat(ref)[h, pl.ds(l * X + X + off, X), :]


def loop(n, body, carry, unroll):
    return lax.fori_loop(0, n, body, carry, unroll=unroll)


def kernel(
    t_in, src_in, code_in, flag_in, imp_in, cre_in, har_in,
    t_end, cre, har, rhs,
    code, flag, temp, src, imp,
    rk, cap, ip, el, us, vs, gxm, gxp, gym, gyp, c0, base, md, ex, fl, stress,
    mid, red, planes, abuf, qbuf,
    sx, sy, xs, ys, rz, uvx, uvy, uvxr, uvyr, bx, by, bxr, byr, qy,
    ghost, fx, fy, fxr, fyr, zs, zm, zp, gg, dx, pc, qend,
    gs_out, gs, ga_out, ga, gred, ggy, dy,
    in_sem, ss, rs,
):
    k = lax.axis_index("stack")
    p = lax.axis_index("plane")
    f = lax.axis_index("phys")
    ns, np_ = 4, 32
    up = {"plane": lax.rem(p + 1, np_)}
    down = {"plane": lax.rem(p + np_ - 1, np_)}
    mate = {"phys": 1 - f}
    others = [{"stack": lax.rem(k + o, ns)} for o in (1, 2, 3)]
    first_col, last_col = f == 0, f == 1

    def dev(where):
        return (where.get("stack", k), where.get("plane", p), where.get("phys", f))

    barrier = pltpu.get_barrier_semaphore()
    aside = [
        [{"stack": lax.rem(k + o, ns), **side} for o in range(4)] for side in (down, up)
    ]
    peers = [mate] + others + aside[0] + aside[1]
    for w in peers:
        pl.semaphore_signal(barrier, inc=1, device_id=dev(w), device_id_type=MESH)

    loads = {}
    for i, (name, hbm, vm, off) in enumerate((
        ("code", code_in, code, 0), ("temp", t_in, temp, 1), ("src", src_in, src, 0),
        ("flag", flag_in, flag, 0), ("imp", imp_in, imp, 0), ("cre", cre_in, cre, 0),
        ("har", har_in, har, 0),
    )):
        loads[name] = []
        for h in (0, 1):
            cp = pltpu.make_async_copy(
                hbm.at[:, :, pl.ds(W * h, W)], vm.at[h, pl.ds(off, L)], in_sem.at[i, h]
            )
            loads[name].append(cp)

    def load(*names):
        for name in names:
            for cp in loads[name]:
                cp.start()

    load("code", "temp")

    def loaded(name):
        for cp in loads[name]:
            cp.wait()

    def message(i, s, d, where):
        return pltpu.make_async_remote_copy(
            src_ref=s, dst_ref=d, send_sem=ss.at[i], recv_sem=rs.at[i],
            device_id=dev(where), device_id_type=MESH,
        )

    sent = []

    def send(i, s, d, where):
        m = message(i, s, d, where)
        m.start()
        sent.append(m)
        return m

    row = lax.broadcasted_iota(jnp.int32, (X, W), 0)
    lane = lax.broadcasted_iota(jnp.int32, (X, W), 1)
    zero = jnp.float32(0.0)

    blank = jnp.zeros((2, X, W), jnp.float32)
    for edge in (0, L + 1):
        rk[:, edge], temp[:, edge], stress[:, edge] = blank + 1.0, blank, blank

    loaded("code")
    load("src")

    def tables(i, _):
        for h in (0, 1):
            c = code[h, pl.ds(i * 2, 2)]
            rk[h, pl.ds(i * 2 + 1, 2)] = lookup(c, half_resistance)
            cap[h, pl.ds(i * 2, 2)] = lookup(c, capacities)
        return 0

    loop(L // 2, tables, 0, 4)

    def pack_rows(ref, dst, side, off):
        r = 0 if side == 0 else X - 1
        n = ref.shape[1]
        view = ref.reshape(2, n * X, W)
        for h in (0, 1):
            dst[h] = view[h, pl.ds(off * X + r, L, stride=X), :]

    def pack_columns(*items):
        def body(l, acc):
            shift = lax.rem(l + 1 - f, W)
            return tuple(
                jnp.where(lane == l, pltpu.roll(ref[1 - f, l + off], shift, axis=1), old)
                for old, (ref, off, _) in zip(acc, items)
            )

        z = jnp.zeros((X, W), jnp.float32)
        for value, (_, _, dst) in zip(loop(L, body, (z,) * len(items), L), items):
            dst[...] = value

    loaded("temp")
    load("flag", "imp", "cre", "har")
    for side in (0, 1):
        pack_rows(rk, sx.at[side, 0], side, 1)
        pack_rows(temp, sx.at[side, 1], side, 1)
    pl.semaphore_wait(barrier, len(peers))
    start = [
        send(M_START, sx.at[1], xs.at[0], up),
        send(M_START + 1, sx.at[0], xs.at[1], down),
    ]
    to_below = send(M_RZ, rk.at[:, L], rz, others[0])
    pack_columns((rk, 1, sy.at[0]), (temp, 1, sy.at[1]))
    start.append(send(M_START + 2, sy, ys, mate))

    def x_shifts(ref, h, l):
        return shifted(ref, h, l, -1), shifted(ref, h, l, 1)

    def column_of(hy, l):
        v = pltpu.roll(hy[...], lax.rem(W - l, W), axis=1)
        return jnp.broadcast_to(v[:, 0:1], (X, W))

    def y_shifts(v0, v1, edges=None):
        r0, r1 = pltpu.roll(v0, 1, axis=1), pltpu.roll(v1, 1, axis=1)
        q0, q1 = pltpu.roll(v0, W - 1, axis=1), pltpu.roll(v1, W - 1, axis=1)
        m1, p0 = jnp.where(lane == 0, r0, r1), jnp.where(lane == W - 1, q1, q0)
        if edges is None:
            return (r0, p0), (m1, q1)
        return (
            (jnp.where(lane == 0, edges[0], r0), p0),
            (m1, jnp.where(lane == W - 1, edges[1], q1)),
        )

    lat = jnp.float32(LAT)
    sxm = jnp.where(row == 0, zero, lat)
    sxp = jnp.where(row == X - 1, zero, lat)
    sym = (jnp.where(lane == 0, zero, lat), lat)
    syp = (lat, jnp.where(lane == W - 1, zero, lat))

    def lateral(l):
        kc = (rk[0, l + 1], rk[1, l + 1])
        ysh = y_shifts(kc[0], kc[1])
        for h in (0, 1):
            km, kp = x_shifts(rk, h, l)
            a = sxm * rcp(kc[h] + km)
            b = sxp * rcp(kc[h] + kp)
            c = sym[h] * rcp(kc[h] + ysh[h][0])
            d = syp[h] * rcp(kc[h] + ysh[h][1])
            gxm[h, l], gxp[h, l], gym[h, l], gyp[h, l] = a, b, c, d
            c0[h, l] = cap[h, l] - ((a + b) + (c + d))

    one = jnp.ones((2, X, W), jnp.float32)
    top_cap = cap[:, 0] + jnp.where(k == 0, jnp.float32(H_CONV), zero)
    bottom_cap = cap[:, L - 1] + jnp.where(k == ns - 1, jnp.float32(H_CONV), zero)

    def eliminate(i, carry):
        dt, nt, wt, db, nb, wb = carry
        m = L - 1 - i
        g = rcp(rk[:, i + 1] + rk[:, i + 2])
        dn = g * dt + nt
        nn = cap[:, i + 1] * dn + g * nt
        ipv = dt * rcp(dn)
        e = g * ipv
        ip[:, i] = ipv
        el[:, i] = e
        us[:, i] = ipv * wt
        gb = rcp(rk[:, m + 1] + rk[:, m])
        dbn = gb * db + nb
        nbn = cap[:, m - 1] * dbn + gb * nb
        ipb = db * rcp(dbn)
        eb = gb * ipb
        ip[:, m] = ipb
        el[:, m] = eb
        vs[:, m] = ipb * wb
        lateral(i)
        lateral(m)
        return dn, nn, e * wt, dbn, nbn, eb * wb

    dt, nt, wt, db, nb, wb = loop(
        HALF - 1, eliminate, (one, top_cap, one, one, bottom_cap, one), 4
    )
    st, sb = nt * rcp(dt), nb * rcp(db)
    gm = rcp(rk[:, HALF] + rk[:, HALF + 1])
    idet = rcp(st * sb + gm * (st + sb))
    m11, m12, m22 = (sb + gm) * idet, gm * idet, (st + gm) * idet
    mid[0], mid[1], mid[2] = m11, m12, m22
    ut, ub, vt, vb = m11 * wt, m12 * wt, m12 * wb, m22 * wb
    us[:, HALF - 1], us[:, HALF], vs[:, HALF - 1], vs[:, HALF] = ut, ub, vt, vb

    def spikes(i, carry):
        ut, ub, vt, vb = carry
        l, m = HALF - 2 - i, HALF + 1 + i
        e, eb = el[:, l], el[:, m]
        ut = us[:, l] + e * ut
        vt = e * vt
        ub = eb * ub
        vb = vs[:, m] + eb * vb
        us[:, l], vs[:, l], us[:, m], vs[:, m] = ut, vt, ub, vb
        return ut, ub, vt, vb

    lateral(HALF - 1)
    lateral(HALF)
    ut, ub, vt, vb = loop(HALF - 1, spikes, (ut, ub, vt, vb), 8)
    to_below.wait_recv()
    planes[k, 0] = ut + rz[...] + rk[:, 1]
    planes[k, 1] = vb
    planes[k, 2] = ub
    spread = [
        send(M_S + o, planes.at[k], planes.at[k], others[o]) for o in range(3)
    ]

    eight = lax.broadcasted_iota(jnp.int32, (8, W), 0)

    def tile(rows_):
        out = jnp.zeros((8, W), jnp.float32)
        for i, r in enumerate(rows_):
            out = jnp.where(eight == i, r, out)
        return out

    def send_rows(first, out, into):
        return [
            send(first + 4 * side + o, out.at[side], into.at[1 - side, k], aside[side][o])
            for side in (0, 1) for o in range(4)
        ]

    for side, r in ((0, 0), (1, X - 1)):
        gs_out[side] = tile([planes[k, i, h, r : r + 1, :] for i in range(3) for h in (0, 1)])
    spread += send_rows(M_GS, gs_out, gs)

    for side in (0, 1):
        pack_rows(us, uvx.at[side, 0], side, 0)
        pack_rows(vs, uvx.at[side, 1], side, 0)
    pack_columns((us, 0, uvy.at[0]), (vs, 0, uvy.at[1]))
    uv = [
        send(M_UV, uvx.at[1], uvxr.at[0], up),
        send(M_UV + 1, uvx.at[0], uvxr.at[1], down),
        send(M_UV + 2, uvy, uvyr, mate),
    ]

    def right_side():
        def body(l, carry):
            bf, bl = carry
            tc = (temp[0, l + 1], temp[1, l + 1])
            ysh = y_shifts(tc[0], tc[1])
            nf, nl = [], []
            for h in (0, 1):
                tm, tp = x_shifts(temp, h, l)
                d = (c0[h, l] * tc[h] + src[h, l]) + (
                    (gxm[h, l] * tm + gxp[h, l] * tp)
                    + (gym[h, l] * ysh[h][0] + gyp[h, l] * ysh[h][1])
                )
                rhs[h, l] = d
                nf.append(bf[h] + us[h, l] * d)
                nl.append(bl[h] + vs[h, l] * d)
            return tuple(nf), tuple(nl)

        z = jnp.zeros((X, W), jnp.float32)
        return loop(L, body, ((z, z), (z, z)), 16)

    def side_row(ref, s, h, off):
        view = ref.reshape(2, ref.shape[1] * X, W)
        return view[h, pl.ds(off * X + (0 if s == 0 else X - 1), L, stride=X), :]

    edge_lane = (W - 1) * (1 - f)
    edge_masks = ((lane == 0) & last_col, (lane == W - 1) & first_col)

    def add_column():
        def body(l, _):
            hy = column_of(dy, l)
            rhs[1 - f, l] = rhs[1 - f, l] + jnp.where(lane == edge_lane, hy, zero)
            return 0

        loop(L, body, 0, 8)

    def edge_column(q, j, shift):
        return jnp.broadcast_to(pltpu.roll(q[j], shift, axis=1)[:, 0:1], (X, W))

    def ghost_terms(ghost_rows, ghost_column, own_column, bf, bl):
        d = jnp.where(lane < L, ggy[...] * (ghost_column - own_column), zero)
        dy[...] = d
        sums = [jnp.sum(uvy[j] * d, axis=1, keepdims=True) for j in (0, 1)]
        bf, bl = [
            [old[h] + jnp.where(edge_masks[h], sums[j], zero) for h in (0, 1)]
            for j, old in ((0, bf), (1, bl))
        ]
        nf, nl = [], []
        for h in (0, 1):
            f_sum, l_sum = [], []
            for s in (0, 1):
                d = gg[s, h] * (ghost_rows[s, h] - side_row(temp, s, h, 1))
                dx[s, h] = d
                f_sum.append(jnp.sum(uvx[s, 0, h] * d, axis=0, keepdims=True))
                l_sum.append(jnp.sum(uvx[s, 1, h] * d, axis=0, keepdims=True))
            for out, old, sums in ((nf, bf, f_sum), (nl, bl, l_sum)):
                add = jnp.where(row == 0, sums[0], jnp.where(row == X - 1, sums[1], zero))
                out.append(old[h] + add)
        return nf, nl

    def add_rows(ref, rows_ref):
        view = ref.reshape(2, L * X, W)
        for h in (0, 1):
            for s, r in ((0, 0), (1, X - 1)):
                at = pl.ds(r, L, stride=X)
                view[h, at, :] = view[h, at, :] + rows_ref[s, h]

    def block_solve():
        def forward(i, carry):
            t, b = carry
            m = L - 1 - i
            base[:, i] = ip[:, i] * t
            base[:, m] = ip[:, m] * b
            return rhs[:, i + 1] + el[:, i] * t, rhs[:, m - 1] + el[:, m] * b

        t, b = loop(HALF - 1, forward, (rhs[:, 0], rhs[:, L - 1]), 4)
        t, b = mid[0] * t + mid[1] * b, mid[1] * t + mid[2] * b
        base[:, HALF - 1], base[:, HALF] = t, b

        def backward(i, carry):
            t, b = carry
            l, m = HALF - 2 - i, HALF + 1 + i
            t = base[:, l] + el[:, l] * t
            b = base[:, m] + el[:, m] * b
            base[:, l], base[:, m] = t, b
            return t, b

        loop(HALF - 1, backward, (t, b), 4)

    def solved(i, qt, qb):
        return base[:, i] + (us[:, i] * qt + vs[:, i] * qb)

    def correct(qt, qb):
        def body(i, _):
            temp[:, i + 1] = solved(i, qt, qb)
            return 0

        loop(L, body, 0, 4)

    def creep_tables(i, _):
        for h in (0, 1):
            at = pl.ds(i * 2, 2)
            c = code[h, at]
            md[h, at] = lookup(c, mod_table)
            ex[h, at] = lookup(c, expand_table)
            fl[h, at] = jnp.where(flag[h, at] == 1, jnp.float32(RATE), zero)
        return 0

    def creep_cell(t, c, hd, m, e, im, active):
        load = im - e * t
        s = m * (load - c)
        z = jnp.abs(s) * (rcp(hd) * jnp.float32(0.5 * LOG2E))
        d = jnp.exp2(z - 1.0) - jnp.exp2(-1.0 - z)
        arr = jnp.exp2(jnp.float32(0.5 * LOG2E) * jnp.tanh(0.25 * t + jnp.float32(HALF_LN2)))
        rate = (active * arr) * d
        q = jnp.exp2(jnp.float32(-0.1 * LOG2E) * jnp.log(0.5 + d))
        gap = 1.0 - (0.5 * hd) * q
        size = jnp.abs(gap)
        root = size * lax.rsqrt(jnp.maximum(size, jnp.float32(1e-30)))
        cn = c + jnp.where(s < 0.0, -rate, rate)
        return cn, hd + (gap * root) * rate, m * (load - cn)

    state = (cre, har, md, ex, imp, fl)

    def creep():
        def body(i, _):
            cre[:, i], har[:, i], _s = creep_cell(temp[:, i + 1], *[a[:, i] for a in state])
            return 0

        loop(L, body, 0, 4)

    def interface_system(part, put):
        a1 = part(0, 1) + part(1, 0)
        a2 = part(1, 1) + part(2, 0)
        a3 = part(2, 1) + part(3, 0)
        b1, b2 = part(1, 2), part(2, 2)
        d12 = a1 * a2 - b1 * b1
        idet = rcp(d12 * a3 - a1 * (b2 * b2))
        v11, v12, v13 = (a2 * a3 - b2 * b2) * idet, b1 * a3 * idet, b1 * b2 * idet
        v22, v23, v33 = a1 * a3 * idet, a1 * b2 * idet, d12 * idet
        table = ((v11, v12, v13), (v12, v22, v23), (v13, v23, v33))
        for j in range(3):
            for r, sign in ((0, 1.0), (1, -1.0)):
                at = k + r
                v = jnp.where(
                    at == 1, table[0][j],
                    jnp.where(at == 2, table[1][j], jnp.where(at == 3, table[2][j], zero)),
                )
                put(r, j, v * sign)

    loaded("src")
    for n in range(TSTEPS):
        bf, bl = right_side()
        if n == 0:
            for m in start:
                m.wait_recv()
            for s in (0, 1):
                wide = jnp.where(p == (0 if s == 0 else np_ - 1), zero, lat)
                for h in (0, 1):
                    gg[s, h] = wide * rcp(sx[s, 0, h] + xs[s, 0, h])
            ggy[...] = jnp.where(lane < L, lat * rcp(sy[0] + ys[0]), zero)
            bf, bl = ghost_terms(xs.at[:, 1], ys[1], sy[1], bf, bl)
        else:
            if n == 1:
                for m in uv:
                    m.wait_recv()
            for m in bases + beside_flux + ghost_ends:
                m.wait_recv()
            for side in (0, 1):
                d = [ga[n - 1, side, j, 2:4, :] - ga[n - 1, side, j + 1, 0:2, :] for j in range(3)]
                qg = [
                    gred[side, r, 0, 0:2, :] * d[0] + gred[side, r, 1, 0:2, :] * d[1]
                    + gred[side, r, 2, 0:2, :] * d[2]
                    for r in (0, 1)
                ]
                for h in (0, 1):
                    ghost[side, h] = bxr[n - 1, side, h] + (
                        uvxr[side, 0, h] * qg[0][h : h + 1, :] + uvxr[side, 1, h] * qg[1][h : h + 1, :]
                    )
            far = [edge_column(qy.at[n - 1], j, f) for j in (0, 1)]
            near = [edge_column(qbuf.at[n - 1, :, 1 - f], j, 1 - f) for j in (0, 1)]
            bf, bl = ghost_terms(
                ghost,
                byr[n - 1] + (uvyr[0] * far[0] + uvyr[1] * far[1]),
                by[n - 1] + (uvy[0] * near[0] + uvy[1] * near[1]),
                bf, bl,
            )
        for h in (0, 1):
            abuf[n, k, 0, h] = bf[h]
            abuf[n, k, 1, h] = bl[h]
        ends = [
            send(M_A + 3 * n + o, abuf.at[n, k], abuf.at[n, k], others[o]) for o in range(3)
        ]
        more = n < TSTEPS - 1
        if more:
            for side, r in ((0, 0), (1, X - 1)):
                ga_out[n, side] = tile([v[h][r : r + 1, :] for v in (bf, bl) for h in (0, 1)])
            ghost_ends = send_rows(M_GA + 8 * n, ga_out.at[n], ga.at[n])
        add_rows(rhs, dx)
        add_column()
        block_solve()
        if more:
            for side in (0, 1):
                pack_rows(base, bx.at[n, side], side, 0)
            pack_columns((base, 0, by.at[n]))
            bases = [
                send(M_B + 3 * n, bx.at[n, 1], bxr.at[n, 0], up),
                send(M_B + 3 * n + 1, bx.at[n, 0], bxr.at[n, 1], down),
                send(M_B + 3 * n + 2, by.at[n], byr.at[n], mate),
            ]
        if n == 0:
            loaded("flag")
            loop(L // 2, creep_tables, 0, 2)
            loaded("imp")
            pack_columns((md, 0, pc.at[2]), (ex, 0, pc.at[3]))
            pack_columns((imp, 0, pc.at[4]), (fl, 0, pc.at[5]))
            for m in spread:
                m.wait_recv()
            interface_system(
                lambda j, i: planes[j, i], lambda r, j, v: red.__setitem__((r, j), v)
            )
            for side in (0, 1):
                interface_system(
                    lambda j, i, side=side: gs[side, j, 2 * i : 2 * i + 2, :],
                    lambda r, j, v, side=side: gred.__setitem__((side, r, j, slice(0, 2)), v),
                )
        else:
            if n == 1:
                for name in ("cre", "har"):
                    loaded(name)
            creep()
            if not more:
                pack_columns((base, 0, pc.at[6]), (cre, 0, pc.at[0]), (har, 0, pc.at[1]))
        for m in ends:
            m.wait_recv()
        r = [abuf[n, j, 1] - abuf[n, j + 1, 0] for j in range(3)]
        qt, qb = [
            red[s, 0] * r[0] + red[s, 1] * r[1] + red[s, 2] * r[2] for s in (0, 1)
        ]
        if more:
            qbuf[n, 0], qbuf[n, 1] = qt, qb
            beside_flux = [send(M_C + 3 * n + 2, qbuf.at[n, :, 1 - f], qy.at[n], mate)]
        if more:
            correct(qt, qb)

    qend[0], qend[1] = qt, qb
    for s, r in ((0, 0), (1, X - 1)):
        for h in (0, 1):
            t = side_row(base, s, h, 0) + (
                uvx[s, 0, h] * qend[0, h, r : r + 1, :] + uvx[s, 1, h] * qend[1, h, r : r + 1, :]
            )
            fx[s, h] = creep_cell(t, *[side_row(a, s, h, 0) for a in state])[2]
    for j, l in ((0, 0), (1, L - 1)):
        zs[j] = creep_cell(solved(l, qt, qb), *[a[:, l] for a in state])[2]
    edges = [
        send(M_F, fx.at[1], fxr.at[0], up),
        send(M_F + 1, fx.at[0], fxr.at[1], down),
        send(M_F + 3, zs.at[1], zm, others[0]),
        send(M_F + 4, zs.at[0], zp, others[2]),
    ]
    col = [
        jnp.broadcast_to(pltpu.roll(qend[j, 1 - f], 1 - f, axis=1)[:, 0:1], (X, W)) for j in (0, 1)
    ]
    tc = pc[6] + (uvy[0] * col[0] + uvy[1] * col[1])
    used = jnp.where(lane < L, pc[1], jnp.float32(1.0))
    fy[...] = creep_cell(tc, pc[0], used, *[pc[2 + j] for j in range(4)])[2]
    beside = send(M_F + 2, fy, fyr, mate)

    lag = 24

    def last_creep(i):
        t = solved(i, qt, qb)
        t_end[:, i] = t
        cre[:, i], har[:, i], stress[:, i + 1] = creep_cell(t, *[a[:, i] for a in state])

    def residual(l):
        hy = column_of(fyr, l)
        sc = (stress[0, l + 1], stress[1, l + 1])
        ysh = y_shifts(
            sc[0], sc[1], (jnp.where(first_col, zero, hy), jnp.where(last_col, zero, hy))
        )
        for h in (0, 1):
            sm, sp = x_shifts(stress, h, l)
            sm, sp = jnp.where(row == 0, zero, sm), jnp.where(row == X - 1, zero, sp)
            rhs[h, l] = (
                ((stress[h, l + 2] + stress[h, l]) + (sm + sp))
                + (ysh[h][0] + ysh[h][1])
            ) - 6.0 * sc[h]

    def first_layers(i, _):
        last_creep(i)
        return 0

    def both(i, _):
        last_creep(i + lag)
        residual(i)
        return 0

    def last_layers(i, _):
        residual(i + L - lag)
        return 0

    loop(lag, first_layers, 0, 4)
    beside.wait_recv()
    loop(L - lag, both, 0, 6)
    loop(lag, last_layers, 0, 8)
    for m in edges:
        m.wait_recv()
    rhs[:, 0] = rhs[:, 0] + jnp.where(k == 0, zero, zm[...])
    rhs[:, L - 1] = rhs[:, L - 1] + jnp.where(k == ns - 1, zero, zp[...])
    ghost[0] = jnp.where(p == 0, zero, fxr[0])
    ghost[1] = jnp.where(p == np_ - 1, zero, fxr[1])
    add_rows(rhs, ghost)
    for m in sent:
        m.wait_send()


def write_out(temp, cre, har, res, t_out, c_out, h_out, s_out, sem):
    copies = []
    for i, (vm, hbm) in enumerate(
        ((temp, t_out), (cre, c_out), (har, h_out), (res, s_out))
    ):
        for h in (0, 1):
            copies.append(pltpu.make_async_copy(
                vm.at[h], hbm.at[:, :, pl.ds(W * h, W)], sem.at[i, h]
            ))
    for cp in copies:
        cp.start()
    for cp in copies:
        cp.wait()


def per_device(*args):
    f32 = jnp.float32
    block = (2, L, X, W)
    tall = (2, L + 2, X, W)

    def vm(*shape):
        return pltpu.VMEM(shape, f32)

    scratch = [
        pltpu.VMEM(block, jnp.int32), pltpu.VMEM(block, jnp.int32), vm(*tall),
        vm(*block), vm(*block),
        vm(*tall),
        *[vm(*block) for _ in range(14)],
        vm(*tall),
        vm(3, 2, X, W), vm(2, 3, 2, X, W),
        vm(4, 3, 2, X, W), vm(TSTEPS, 4, 2, 2, X, W), vm(2, 2, 2, X, W),
        vm(2, 2, 2, L, W), vm(2, X, W), vm(2, 2, 2, L, W), vm(2, X, W),
        vm(2, X, W),
        vm(2, 2, 2, L, W), vm(2, X, W), vm(2, 2, 2, L, W), vm(2, X, W),
        vm(2, 2, 2, L, W), vm(2, X, W), vm(2, 2, 2, L, W), vm(2, X, W),
        vm(2, 2, X, W),
        vm(2, 2, L, W),
        vm(2, 2, L, W), vm(X, W), vm(2, 2, L, W), vm(X, W),
        vm(2, 2, X, W), vm(2, X, W), vm(2, X, W),
        vm(2, 2, L, W), vm(2, 2, L, W),
        vm(7, X, W), vm(2, 2, X, W),
        vm(2, 8, W), vm(2, 4, 8, W), vm(2, 2, 8, W), vm(2, 2, 4, 8, W),
        vm(2, 2, 3, 8, W), vm(X, W), vm(X, W),
        pltpu.SemaphoreType.DMA((7, 2)),
        pltpu.SemaphoreType.DMA((N_MSG,)), pltpu.SemaphoreType.DMA((N_MSG,)),
    ]
    shape = args[0].shape
    results = pl.pallas_call(
        kernel,
        out_shape=[jax.ShapeDtypeStruct(s, f32) for s in (block,) * 4],
        in_specs=[pl.BlockSpec(memory_space=pltpu.HBM)] * 7,
        out_specs=[pl.BlockSpec(memory_space=pltpu.VMEM)] * 4,
        scratch_shapes=scratch,
        compiler_params=pltpu.CompilerParams(
            collective_id=0, has_side_effects=True, vmem_limit_bytes=49 << 20
        ),
        name="thermal_creep_step",
    )(*args)
    return pl.pallas_call(
        write_out,
        out_shape=[jax.ShapeDtypeStruct(shape, f32)] * 4,
        in_specs=[pl.BlockSpec(memory_space=pltpu.VMEM)] * 4,
        out_specs=[pl.BlockSpec(memory_space=pltpu.HBM)] * 4,
        scratch_shapes=[pltpu.SemaphoreType.DMA((4, 2))],
        compiler_params=pltpu.CompilerParams(vmem_limit_bytes=16 << 20),
        name="write_out",
    )(*results)


def solution(mesh):
    spec = P("stack", "plane", "phys")
    return jax.shard_map(
        per_device, mesh=mesh, in_specs=(spec,) * 7, out_specs=(spec,) * 4, check_vma=False
    )
```
